256 devices in a mesh: seq: 64 (over z, y, core), batch: 4 (over x).
Axes of the slice: x: 4, y: 4, z: 8, core: 2. Of those that a mesh axis runs over, the one named last changes fastest.
Arguments:
- queries: bfloat16 [4, 32768, 16, 128], P('batch', 'seq'), may hold values from -5 to 5
- keys: bfloat16 [4, 32768, 16, 128], P('batch', 'seq'), may hold values from -5 to 5
- values: bfloat16 [4, 32768, 16, 128], P('batch', 'seq'), may hold values from -5 to 5
- keep_count: int32 [4, 16, 256], P('batch'), may hold values from 0 to 128
- query_map: bfloat16 [16, 128, 8], replicated, may hold values from -0.5 to 0.5
- key_map: bfloat16 [16, 128, 8], replicated, may hold values from -0.5 to 0.5
- cotangent: bfloat16 [4, 32768, 16, 128], P('batch', 'seq'), may hold values from -5 to 5
Outputs:
- attended: bfloat16 [4, 32768, 16, 128], P('batch', 'seq')
- grad_query_map: float32 [16, 128, 8], replicated
- grad_key_map: float32 [16, 128, 8], replicated
The draws below stay inside these ranges and needn't reach their ends.
All inputs are finite; a program needn't handle non-finite values.
Results may differ from the reference program's by a relative error of at most 0.0035.
Values may be sent and summed in bfloat16 or wider, within the bound.
A program may use at most 128 MiB of HBM per device.

```python
import math
import jax
import jax.numpy as jnp
from jax import lax

HEADS = 16
DH = 128
RANK = 8
TILE = 128
WINDOW = 256
LEN = 32768
SEQS = 4
TILES = 256


def draw_queries(key, part):
    base = jax.random.truncated_normal(jax.random.fold_in(key, 1), -5.0, 5.0, (SEQS, LEN, HEADS, DH), jnp.float32)
    return base.astype(jnp.bfloat16)


def draw_keys(key, part):
    base = jax.random.truncated_normal(jax.random.fold_in(key, 2), -5.0, 5.0, (SEQS, LEN, HEADS, DH), jnp.float32)
    return base.astype(jnp.bfloat16)


def touch_ends(entries, key, least, top_value):
    longest = entries.shape.index(max(entries.shape))
    spots = []
    for shift in (0, 1):
        where = [jax.random.randint(jax.random.fold_in(key, axis), (), 0, length) for axis, length in enumerate(entries.shape)]
        where[longest] = (where[longest] + shift) % entries.shape[longest]
        spots.append(tuple(where))
    return entries.at[spots[0]].set(least).at[spots[1]].set(top_value)


def shard_levels(stream_key, dims, split, low, largest):
    factor_of, own = 1.0, jax.random.fold_in(stream_key, 6)
    for axis_at, parts in split:
        heights = jnp.exp(jax.random.uniform(jax.random.fold_in(own, axis_at), (parts,), jnp.float32, low / len(split), largest / len(split)))
        factor_of = factor_of * jnp.repeat(heights, dims[axis_at] // parts).reshape([-1 if axis == axis_at else 1 for axis in range(len(dims))])
    return factor_of


def centred(key, dims, scale, bound, split=(), kind=jnp.bfloat16):
    values = scale * jax.random.normal(key, dims, jnp.float32)
    if split:
        values = values * shard_levels(key, dims, split, -0.22, 0.18)
    return jnp.clip(values, -bound, bound).astype(kind)


def setup_inputs(seed: int = 0) -> dict:
    key_of = jax.random.split(jax.random.key(seed), 8)
    queries = draw_queries(jax.random.fold_in(key_of[7], 71), 0)
    keys = draw_keys(jax.random.fold_in(key_of[7], 71), 0)
    values = centred(key_of[2], (SEQS, LEN, HEADS, DH), 1.0, 5.0, ((0, 4), (1, 64)))
    keep_count = touch_ends(jax.random.randint(key_of[3], (SEQS, HEADS, TILES), 0, TILE + 1), jax.random.fold_in(key_of[3], 1), 0, TILE).astype(jnp.int32)
    query_map = centred(key_of[4], (HEADS, DH, RANK), DH ** -0.5, 0.5)
    key_map = centred(key_of[5], (HEADS, DH, RANK), DH ** -0.5, 0.5)
    cotangent = centred(key_of[6], (SEQS, LEN, HEADS, DH), 1.0, 5.0, ((0, 4), (1, 64)))
    return {"queries": queries, "keys": keys, "values": values, "keep_count": keep_count, "query_map": query_map, "key_map": key_map, "cotangent": cotangent}


HIGHEST = lax.Precision.HIGHEST
feature_shift = 1.5

def features(inputs, weights):
    pre_act = jnp.einsum('thd,hdr->thr', inputs.astype(jnp.float32), weights, precision=HIGHEST) - feature_shift
    return jax.nn.softplus(pre_act)

def shifted(array, offset):
    filler = jnp.zeros((offset,) + array.shape[1:], array.dtype)
    return jnp.concatenate([filler, array[:array.shape[0] - offset]], 0)

def exclusive(array):
    summed = jnp.cumsum(array, 0)
    return jnp.concatenate([jnp.zeros_like(array[:1]), summed[:-1]], 0)

def sparse_part(q_rows, k_rows, v_rows, kept):
    length, heads, width = q_rows.shape
    span = WINDOW // TILE
    scale = 1.0 / math.sqrt(width)
    filler = jnp.zeros((WINDOW, heads, width), k_rows.dtype)
    k_padded = jnp.concatenate([filler, k_rows], 0)
    v_padded = jnp.concatenate([filler, v_rows], 0)
    kept_padded = jnp.concatenate([jnp.zeros((WINDOW, heads), bool), kept], 0)

    def one_block(block):
        start = (block * WINDOW).astype(jnp.int32)
        q_block = lax.dynamic_slice_in_dim(q_rows, start, WINDOW, 0)
        k_block = lax.dynamic_slice_in_dim(k_padded, start, 2 * WINDOW, 0)
        v_block = lax.dynamic_slice_in_dim(v_padded, start, 2 * WINDOW, 0)
        kept_block = lax.dynamic_slice_in_dim(kept_padded, start, 2 * WINDOW, 0)
        q_pos = start + jnp.arange(WINDOW, dtype=jnp.int32)
        k_pos = start - WINDOW + jnp.arange(2 * WINDOW, dtype=jnp.int32)
        scores = jnp.einsum('thd,phd->htp', q_block.astype(jnp.float32), k_block.astype(jnp.float32)) * scale
        tile_gap = q_pos[:, None] // TILE - k_pos[None, :] // TILE
        causal = (k_pos[None, :] <= q_pos[:, None]) & (k_pos[None, :] >= 0) & (tile_gap < span)
        live_pairs = causal[None] & ((tile_gap == 0)[None] | kept_block.T[:, None, :])
        row_max = lax.optimization_barrier(jnp.max(jnp.where(live_pairs, scores, -jnp.inf), -1))
        weights = jnp.where(live_pairs, jnp.exp(scores - row_max[..., None]), 0.0)
        denom = lax.optimization_barrier(jnp.sum(weights, -1))
        numer = jnp.einsum('htp,phd->thd', weights.astype(jnp.bfloat16).astype(jnp.float32), v_block.astype(jnp.float32))
        return (numer, denom.T, row_max.T)
    numer, denom, row_max = lax.map(one_block, jnp.arange(length // WINDOW, dtype=jnp.int32))
    return (numer.reshape(length, heads, width), denom.reshape(length, heads), row_max.reshape(length, heads))

def reference(queries, keys, values, keep_count, query_map, key_map, cotangent):
    query_weights = query_map.astype(jnp.float32)
    key_weights = key_map.astype(jnp.float32)
    span = WINDOW // TILE

    def one_sequence(inputs):
        q_rows, k_rows, v_rows, counts, cot_rows = inputs
        length, heads, width = q_rows.shape
        tiles = length // TILE
        within = jnp.arange(length, dtype=jnp.int32) % TILE
        kept = within[:, None] < jnp.repeat(counts, TILE, axis=1).T
        numer, denom, row_max = sparse_part(q_rows, k_rows, v_rows, kept)
        decay = jnp.exp(-row_max)
        v_tiles = v_rows.astype(jnp.float32).reshape(tiles, TILE, heads, width)
        evicted = (1 - kept.astype(jnp.float32)).reshape(tiles, TILE, heads, 1)

        def linear(q_weights, k_weights):
            feat_q = features(q_rows, q_weights).reshape(tiles, TILE, heads, RANK)
            feat_k = features(k_rows, k_weights).reshape(tiles, TILE, heads, RANK)
            all_state = jnp.einsum('nthr,nthd->nhrd', feat_k, v_tiles, precision=HIGHEST)
            all_norm = lax.optimization_barrier(jnp.sum(feat_k, 1))
            ev_feat = feat_k * evicted
            ev_state = jnp.einsum('nthr,nthd->nhrd', ev_feat, v_tiles, precision=HIGHEST)
            ev_norm = lax.optimization_barrier(jnp.sum(ev_feat, 1))
            state = shifted(exclusive(all_state), span - 1)
            norm = shifted(exclusive(all_norm), span - 1)
            for offset in range(1, span):
                state = state + shifted(ev_state, offset)
                norm = norm + shifted(ev_norm, offset)
            kernel_num = jnp.einsum('nthr,nhrd->nthd', feat_q, state, precision=HIGHEST).reshape(length, heads, width)
            kernel_den = jnp.einsum('nthr,nhr->nth', feat_q, norm, precision=HIGHEST).reshape(length, heads)
            return (numer + decay[..., None] * kernel_num) / (denom + decay * kernel_den)[..., None]
        out, pull_back = jax.vjp(linear, query_weights, key_weights)
        grad_q, grad_k = pull_back(cot_rows.astype(jnp.float32))
        return (out.astype(jnp.bfloat16), grad_q, grad_k)
    attended, grad_q, grad_k = lax.map(one_sequence, (queries, keys, values, keep_count, cotangent))
    return (attended, lax.optimization_barrier(jnp.sum(grad_q, 0)), lax.optimization_barrier(jnp.sum(grad_k, 0)))
```

```python
import functools
import math

import jax
import jax.numpy as jnp
from jax import lax
from jax.experimental import pallas as pl
from jax.experimental.pallas import tpu as pltpu
from jax.sharding import Mesh
from jax.sharding import PartitionSpec as P

TILE = 128
SHIFT = 1.5
LOG2E = math.log2(math.e)
Z_AXIS, Y_AXIS, C_AXIS, X_AXIS = "seq_0", "seq_1", "seq_2", "batch"
SEQ = (Z_AXIS, Y_AXIS, C_AXIS)
F32, BF16 = jnp.float32, jnp.bfloat16
BLOCK = 16


def dot_nn(a, b):
    return lax.dot_general(a, b, (((1,), (0,)), ((), ())), preferred_element_type=F32)


def dot_nt(a, b):
    return lax.dot_general(a, b, (((1,), (1,)), ((), ())), preferred_element_type=F32)


def dot_tn(a, b):
    return lax.dot_general(a, b, (((0,), (0,)), ((), ())), preferred_element_type=F32)


def halves(x):
    high = x.astype(BF16).astype(F32)
    return high, x - high


def stacked(x):
    return jnp.concatenate(halves(x), 0).astype(BF16)


def folded(x):
    half = x.shape[0] // 2
    return x[:half] + x[half:]


def feature(pre):
    small = jnp.exp(-jnp.abs(pre))
    inverse = 1.0 / (1.0 + small)
    return jnp.maximum(pre, 0.0) + jnp.log1p(small), jnp.where(pre >= 0.0, inverse, small * inverse)


def remote(source, target, send, receive, device):
    return pltpu.make_async_remote_copy(
        src_ref=source,
        dst_ref=target,
        send_sem=send,
        recv_sem=receive,
        device_id=device,
        device_id_type=pl.DeviceIdType.MESH,
    )


def kernel(
    sizes,
    q_hbm, k_hbm, v_hbm, c_hbm, count_ref, wq_ref, wk_ref,
    out_hbm, gq_ref, gk_ref,
    q_raw, k_raw, v_raw, c_raw, halo_raw, o_raw,
    q_rows, k_rows, v_rows, c_rows, o_rows, numer,
    feat_q, slope_q, feat_k, slope_k, kept_lane, count_lane,
    state_local, norm_local, u_local, row_data, g_rows, gpre_q, d_state, d_norm, gk_local,
    p_send, p_land, p_total, p_far, p_out, p_back,
    s_send, s_land, s_total, s_far, s_out, s_back,
    rq_send, rq_land, rq_z, rq_zland, rq_x, rq_xland, rq_sum,
    rk_send, rk_land, rk_z, rk_zland, rk_x, rk_xland, rk_sum,
    acc,
    load_sem, store_sem, halo_sems, p_sems, s_sems, rq_sems, rk_sems,
):
    nz, ny, nc, nx = sizes
    group = ny * nc
    devices = nz * group
    tokens, heads, width = q_raw.shape
    tiles = tokens // TILE
    own = heads // group
    lanes = lax.broadcasted_iota(jnp.int32, (8, TILE), 1)
    z, y, c, x = (lax.axis_index(a) for a in (Z_AXIS, Y_AXIS, C_AXIS, X_AXIS))
    me = y * nc + c
    index = z * group + me

    def peer(s):
        return {Y_AXIS: s // nc, C_AXIS: s % nc}

    def place(i):
        return {Z_AXIS: i // group, Y_AXIS: (i // nc) % ny, C_AXIS: i % nc}

    after = place((index + 1) % devices)
    before = place((index + devices - 1) % devices)

    barrier = pltpu.get_barrier_semaphore()

    def greet(device):
        pl.semaphore_signal(barrier, inc=1, device_id=device, device_id_type=pl.DeviceIdType.MESH)

    greet(after)
    greet(before)
    for k in range(1, group):
        greet(peer((me + k) % group))
    for k in range(1, nz):
        greet({Z_AXIS: (z + k) % nz})
    for k in range(1, nx):
        greet({X_AXIS: (x + k) % nx})

    sources = (k_hbm, v_hbm, c_hbm, q_hbm)
    raws = (k_raw, v_raw, c_raw, q_raw)

    def load(a, t):
        rows = pl.ds(t * TILE, TILE)
        return pltpu.make_async_copy(sources[a].at[rows], raws[a].at[rows], load_sem.at[a * tiles + t])

    for a in range(4):
        for t in range(tiles):
            load(a, t).start()

    def by_head(raw, rows, first, target, count):
        def step(b, _):
            block = raw[pl.ds(rows + b * BLOCK, BLOCK)]
            target[:, pl.ds(first + b * BLOCK, BLOCK), :] = jnp.swapaxes(block, 0, 1)
            return 0

        lax.fori_loop(0, count // BLOCK, step, 0, unroll=4)

    for t in range(tiles):
        load(0, t).wait()
        by_head(k_raw, t * TILE, (t + 1) * TILE, k_rows, TILE)
        load(1, t).wait()
        by_head(v_raw, t * TILE, (t + 1) * TILE, v_rows, TILE)

    counts = count_ref[...]
    which = lax.broadcasted_iota(jnp.int32, counts.shape, 1)
    lane16 = lax.broadcasted_iota(jnp.int32, (heads, TILE), 1)
    for e in range(tiles + 1):
        picked = jnp.sum(jnp.where(which == index * tiles + (e - 1), counts, 0), 1, keepdims=True)
        spread = jnp.broadcast_to(picked, (heads, TILE))
        kept = (lane16 < spread).astype(F32)
        for h in range(heads):
            count_lane[e, h] = jnp.broadcast_to(spread[h : h + 1], (8, TILE))
            kept_lane[h, :, e * TILE : (e + 1) * TILE] = jnp.broadcast_to(kept[h : h + 1], (8, TILE))

    pl.semaphore_wait(barrier, 2 + group - 1 + nz - 1 + nx - 1)
    halo_from = pl.ds(tokens - TILE, TILE)
    halo_copies = [
        remote(k_hbm.at[halo_from], halo_raw.at[0], halo_sems.at[0], halo_sems.at[2], after),
        remote(v_hbm.at[halo_from], halo_raw.at[1], halo_sems.at[1], halo_sems.at[3], after),
    ]
    for copy in halo_copies:
        copy.start()

    def scatter(buffer, land, sems, s):
        return remote(buffer.at[s], land.at[me], sems.at[s], sems.at[group + me], peer(s))

    def arrival(buffer, land, sems, s):
        return remote(buffer.at[s], land.at[s], sems.at[s], sems.at[group + s], peer(s))

    def share(buffer, land, sems, s):
        return remote(buffer, land.at[me], sems.at[s], sems.at[group + me], peer(s))

    def share_arrival(buffer, land, sems, s):
        return remote(buffer, land.at[s], sems.at[s], sems.at[group + s], peer(s))

    def z_copy(buffer, land, sems, t):
        return remote(buffer, land.at[z], sems.at[t], sems.at[nz + z], {Z_AXIS: t})

    def z_arrival(buffer, land, sems, t):
        return remote(buffer, land.at[t], sems.at[t], sems.at[nz + t], {Z_AXIS: t})

    def x_copy(buffer, land, sems, t):
        return remote(buffer, land.at[x], sems.at[t], sems.at[nx + x], {X_AXIS: t})

    def x_arrival(buffer, land, sems, t):
        return remote(buffer, land.at[t], sems.at[t], sems.at[nx + t], {X_AXIS: t})

    def others(step, count=group, here=None):
        here = me if here is None else here

        def one(k, _):
            step((here + 1 + k) % count)
            return 0

        lax.fori_loop(0, count - 1, one, 0)

    def owner_slice(pieces, norms):
        low = jnp.where(lanes < TILE // 2, norms[0], norms[1])
        return jnp.concatenate([*pieces, low], 0)

    def norm_of(tile, i):
        turned = pltpu.roll(tile, TILE // 2, 1)
        return jnp.where(lanes < TILE // 2, *((tile, turned) if i == 0 else (turned, tile)))

    own_rows = pl.ds(TILE, tokens)

    def state_slice(o):
        pieces, norms = [], []
        for i in range(own):
            h = o * own + i
            feat, slope = feature(dot_nt(wk_ref[h], k_rows[h, own_rows, :]) - SHIFT)
            feat_k[h, :, TILE:] = feat
            slope_k[h, :, TILE:] = slope
            pieces.append(folded(dot_nn(stacked(feat), v_rows[h, own_rows, :])))
            norms.append(jnp.sum(feat, 1, keepdims=True))
        return owner_slice(pieces, norms)

    def state_send(o):
        p_send[o] = state_slice(o)
        scatter(p_send, p_land, p_sems[0], o).start()

    others(state_send)
    p_land[me] = state_slice(me)

    def query_features(h, _):
        feat, slope = feature(dot_nt(wq_ref[h], q_rows[h]) - SHIFT)
        feat_q[h] = feat
        slope_q[h] = slope
        return 0

    for t in range(tiles):
        load(2, t).wait()
        by_head(c_raw, t * TILE, t * TILE, c_rows, TILE)
        load(3, t).wait()
        by_head(q_raw, t * TILE, t * TILE, q_rows, TILE)
    lax.fori_loop(0, heads, query_features, 0)

    def local_terms(h, j, state, norm):
        cols = slice(j * TILE, (j + 1) * TILE)
        state_local[h, j] = state
        norm_local[h, :, cols] = jnp.broadcast_to(norm, (8, TILE))
        u = folded(dot_nt(stacked(state), c_rows[h, cols, :]))
        u_local[h, :, cols] = u
        fq = feat_q[h, :, cols]
        row_data[h, 3:4, cols] = jnp.sum(fq * norm, 0, keepdims=True)
        row_data[h, 4:5, cols] = jnp.sum(fq * u, 0, keepdims=True)

    def local_states(h, _):
        full, full_norm, out, out_norm = [], [], [], []
        for i in range(tiles - 1):
            cols = slice((i + 1) * TILE, (i + 2) * TILE)
            feat = feat_k[h, :, cols]
            gone = feat * (1.0 - kept_lane[h, :, cols])
            both = jnp.concatenate([*halves(feat), *halves(gone)], 0).astype(BF16)
            result = dot_nn(both, v_rows[h, cols, :])
            full.append(folded(result[:16]))
            out.append(folded(result[16:]))
            full_norm.append(jnp.sum(feat, 1, keepdims=True))
            out_norm.append(jnp.sum(gone, 1, keepdims=True))
        for j in range(1, tiles):
            local_terms(
                h, j, sum(full[: j - 1], out[j - 1]), sum(full_norm[: j - 1], out_norm[j - 1])
            )
        return 0

    scale2 = LOG2E / math.sqrt(width)
    key_at = lax.broadcasted_iota(jnp.int32, (TILE, TILE), 0)
    causal = key_at <= lax.broadcasted_iota(jnp.int32, (TILE, TILE), 1)

    def sparse(h, j):
        cols = slice(j * TILE, (j + 1) * TILE)
        window = slice(j * TILE, (j + 2) * TILE)
        v_window = v_rows[h, window, :]
        scores = dot_nt(k_rows[h, window, :], q_rows[h, cols, :])
        live = key_at < count_lane[j, h, 0:1, :]
        near = jnp.where(live, scores[:TILE], -1e30)
        here = jnp.where(causal, scores[TILE:], -1e30)
        top = jnp.maximum(jnp.max(near, 0, keepdims=True), jnp.max(here, 0, keepdims=True))
        shift = top * scale2
        masked = jnp.concatenate([near, here], 0)
        weights = jnp.exp2(masked * scale2 - shift)
        rounded = weights.astype(BF16)
        numer[h, cols, :] = dot_tn(rounded, v_window)
        along = dot_nt(v_window, c_rows[h, cols, :])
        row_data[h, 0:1, cols] = jnp.exp2(-shift)
        row_data[h, 1:2, cols] = jnp.sum(weights, 0, keepdims=True)
        row_data[h, 2:3, cols] = jnp.sum(rounded.astype(F32) * along, 0, keepdims=True)

    def sparse_tile(j):
        def one(h, _):
            sparse(h, j)
            return 0

        lax.fori_loop(0, heads, one, 0)

    others(lambda s: arrival(p_send, p_land, p_sems[0], s).wait_recv())
    p_total[...] = sum(p_land[s] for s in range(1, group)) + p_land[0]
    for t in range(1, nz):
        @pl.when(t > z)
        def _():
            z_copy(p_total, p_far, p_sems[1], t).start()

    lax.fori_loop(0, heads, local_states, 0)
    sparse_tile(1)
    sparse_tile(2)

    acc[...] = jnp.zeros_like(acc)
    for t in range(nz - 1):
        @pl.when(t < z)
        def _():
            z_arrival(p_total, p_far, p_sems[1], t).wait_recv()
            acc[...] += p_far[t]

    running = acc[...]
    for s in range(group):
        p_out[s] = running
        running = running + p_land[s]
    others(lambda s: scatter(p_out, p_back, p_sems[2], s).start())
    p_back[me] = p_out[me]

    sparse_tile(3)

    for copy in halo_copies:
        copy.wait_recv()
    by_head(halo_raw.at[0], 0, 0, k_rows, TILE)
    by_head(halo_raw.at[1], 0, 0, v_rows, TILE)

    def halo_head(h, _):
        feat, slope = feature(dot_nt(wk_ref[h], k_rows[h, :TILE, :]) - SHIFT)
        slope_k[h, :, :TILE] = slope
        held = feat * kept_lane[h, :, :TILE]
        state = folded(dot_nn(stacked(held), v_rows[h, :TILE, :]))
        local_terms(h, 0, -state, -jnp.sum(held, 1, keepdims=True))
        sparse(h, 0)
        return 0

    lax.fori_loop(0, heads, halo_head, 0)

    def d_slice(o):
        pieces, norms = [], []
        back = p_back[o]
        for i in range(own):
            h = o * own + i
            far = back[i * 8 : (i + 1) * 8]
            far_norm = jnp.concatenate([norm_of(back[own * 8 :], i)] * tiles, 1)
            fq = feat_q[h]
            u_far = folded(dot_nt(stacked(far), c_rows[h]))
            decay = row_data[h, 0:1, :]
            kd = row_data[h, 3:4, :] + jnp.sum(fq * far_norm, 0, keepdims=True)
            cu = row_data[h, 4:5, :] + jnp.sum(fq * u_far, 0, keepdims=True)
            inverse = 1.0 / (row_data[h, 1:2, :] + decay * kd)
            share_of = decay * inverse
            g = fq * share_of
            g_den = -share_of * ((row_data[h, 2:3, :] + decay * cu) * inverse)
            g_rows[h] = g
            row_data[h, 5:6, :] = inverse
            gpre_q[h] = (
                share_of * (u_local[h] + u_far) + g_den * (norm_local[h] + far_norm)
            ) * slope_q[h]
            weighted = fq * g_den
            total, total_norm = None, None
            for j in range(tiles):
                cols = slice(j * TILE, (j + 1) * TILE)
                piece = folded(dot_nn(stacked(g[:, cols]), c_rows[h, cols, :]))
                norm = jnp.sum(weighted[:, cols], 1, keepdims=True)
                d_state[h, j] = piece
                d_norm[h, j] = jnp.broadcast_to(norm, (8, TILE))
                total = piece if j == 0 else total + piece
                total_norm = norm if j == 0 else total_norm + norm
            pieces.append(total)
            norms.append(total_norm)
        return owner_slice(pieces, norms)

    def d_send(o):
        arrival(p_out, p_back, p_sems[2], o).wait_recv()
        s_send[o] = d_slice(o)
        scatter(s_send, s_land, s_sems[0], o).start()

    others(d_send)
    s_land[me] = d_slice(me)

    def query_slice(o):
        pieces = []
        for i in range(own):
            h = o * own + i
            pieces.append(folded(dot_nn(stacked(gpre_q[h]), q_rows[h])))
        return jnp.concatenate(pieces, 0)

    def query_send(o):
        rq_send[o] = query_slice(o)
        scatter(rq_send, rq_land, rq_sems[0], o).start()

    others(query_send)
    rq_land[me] = query_slice(me)

    def key_local(h, _):
        parts = []
        for e in range(tiles):
            cols = slice(e * TILE, (e + 1) * TILE)
            v_tile = v_rows[h, cols, :]
            kept = kept_lane[h, :, cols]
            if e == 0:
                grad = -kept * (folded(dot_nt(stacked(d_state[h, 0]), v_tile)) + d_norm[h, 0])
            else:
                near, near_norm = d_state[h, e], d_norm[h, e]
                if e + 1 < tiles:
                    full = sum([d_state[h, j] for j in range(e + 2, tiles)], d_state[h, e + 1])
                    full_norm = sum([d_norm[h, j] for j in range(e + 2, tiles)], d_norm[h, e + 1])
                    both = jnp.concatenate([*halves(near), *halves(full)], 0).astype(BF16)
                    result = dot_nt(both, v_tile)
                    grad = (1.0 - kept) * (folded(result[:16]) + near_norm)
                    grad = grad + (folded(result[16:]) + full_norm)
                else:
                    grad = (1.0 - kept) * (folded(dot_nt(stacked(near), v_tile)) + near_norm)
            parts.append(grad * slope_k[h, :, cols])
        gk_local[h] = folded(dot_nn(stacked(jnp.concatenate(parts, 1)), k_rows[h, :tokens, :]))
        return 0

    sub = lax.broadcasted_iota(jnp.int32, (8, TILE), 0)

    def outputs(h, o, i):
        back = p_back[o]
        far = back[i * 8 : (i + 1) * 8]
        for j in range(tiles):
            cols = slice(j * TILE, (j + 1) * TILE)
            high, low = halves(far + state_local[h, j])
            g_high, g_low = halves(g_rows[h, :, cols])
            first, rest = halves(row_data[h, 5:6, cols])
            second, third = halves(rest)
            inverse = jnp.where(sub == 0, first, jnp.where(sub == 1, second, third))
            inverse = jnp.where(sub < 3, inverse, 0.0)
            left = jnp.concatenate([g_high, g_low, g_high, inverse], 0).astype(BF16)
            zeros, ones = jnp.zeros((8, TILE), F32), jnp.ones((8, TILE), F32)
            right = jnp.concatenate(
                [
                    jnp.concatenate([high, high, low, zeros], 0),
                    jnp.concatenate([zeros, zeros, zeros, ones], 0),
                ],
                1,
            ).astype(BF16)
            both = dot_tn(left, right)
            result = numer[h, cols, :] * both[:, TILE:] + both[:, :TILE]
            o_rows[h, cols, :] = result.astype(BF16)

    def outputs_owner(o, _):
        for i in range(own):
            outputs(o * own + i, o, i)
        return 0

    lax.fori_loop(0, heads, key_local, 0)

    others(lambda s: arrival(s_send, s_land, s_sems[0], s).wait_recv())
    s_total[...] = sum(s_land[s] for s in range(1, group)) + s_land[0]
    for t in range(nz - 1):
        @pl.when(t < z)
        def _():
            z_copy(s_total, s_far, s_sems[1], t).start()

    others(lambda s: arrival(rq_send, rq_land, rq_sems[0], s).wait_recv())
    rq_z[...] = sum(rq_land[s] for s in range(1, group)) + rq_land[0]
    others(lambda t: z_copy(rq_z, rq_zland, rq_sems[1], t).start(), nz, z)
    rq_zland[z] = rq_z[...]

    lax.fori_loop(0, group, outputs_owner, 0)

    acc[...] = jnp.zeros_like(acc)
    for t in range(1, nz):
        @pl.when(t > z)
        def _():
            z_arrival(s_total, s_far, s_sems[1], t).wait_recv()
            acc[...] += s_far[t]

    running = acc[...]
    for s in reversed(range(group)):
        s_out[s] = running
        running = running + s_land[s]
    others(lambda s: scatter(s_out, s_back, s_sems[2], s).start())
    s_back[me] = s_out[me]

    others(lambda t: z_arrival(rq_z, rq_zland, rq_sems[1], t).wait_recv(), nz, z)
    rq_x[...] = sum(rq_zland[t] for t in range(1, nz)) + rq_zland[0]
    others(lambda t: x_copy(rq_x, rq_xland, rq_sems[2], t).start(), nx, x)
    rq_xland[x] = rq_x[...]

    def by_position(b, _):
        block = o_rows[:, pl.ds(b * BLOCK, BLOCK), :]
        o_raw[pl.ds(b * BLOCK, BLOCK)] = jnp.swapaxes(block, 0, 1)
        return 0

    lax.fori_loop(0, tokens // BLOCK, by_position, 0, unroll=4)
    store = pltpu.make_async_copy(o_raw, out_hbm, store_sem)
    store.start()

    def key_slice(o):
        pieces = []
        back = s_back[o]
        for i in range(own):
            h = o * own + i
            far_norm = jnp.concatenate([norm_of(back[own * 8 :], i)] * tiles, 1)
            grad = folded(dot_nt(stacked(back[i * 8 : (i + 1) * 8]), v_rows[h, own_rows, :]))
            grad = (grad + far_norm) * slope_k[h, :, TILE:]
            pieces.append(gk_local[h] + folded(dot_nn(stacked(grad), k_rows[h, own_rows, :])))
        return jnp.concatenate(pieces, 0)

    def key_send(o):
        arrival(s_out, s_back, s_sems[2], o).wait_recv()
        rk_send[o] = key_slice(o)
        scatter(rk_send, rk_land, rk_sems[0], o).start()

    others(key_send)
    rk_land[me] = key_slice(me)

    others(lambda t: x_arrival(rq_x, rq_xland, rq_sems[2], t).wait_recv(), nx, x)
    rq_sum[...] = sum(rq_xland[t] for t in range(1, nx)) + rq_xland[0]
    others(lambda s: share(rq_sum, gq_ref, rq_sems[3], s).start())
    gq_ref[me] = rq_sum[...]

    others(lambda s: arrival(rk_send, rk_land, rk_sems[0], s).wait_recv())
    rk_z[...] = sum(rk_land[s] for s in range(1, group)) + rk_land[0]
    others(lambda t: z_copy(rk_z, rk_zland, rk_sems[1], t).start(), nz, z)
    rk_zland[z] = rk_z[...]
    others(lambda t: z_arrival(rk_z, rk_zland, rk_sems[1], t).wait_recv(), nz, z)
    rk_x[...] = sum(rk_zland[t] for t in range(1, nz)) + rk_zland[0]
    others(lambda t: x_copy(rk_x, rk_xland, rk_sems[2], t).start(), nx, x)
    rk_xland[x] = rk_x[...]
    others(lambda t: x_arrival(rk_x, rk_xland, rk_sems[2], t).wait_recv(), nx, x)
    rk_sum[...] = sum(rk_xland[t] for t in range(1, nx)) + rk_xland[0]
    others(lambda s: share(rk_sum, gk_ref, rk_sems[3], s).start())
    gk_ref[me] = rk_sum[...]

    for copy in halo_copies:
        copy.wait_send()
    others(lambda s: scatter(p_send, p_land, p_sems[0], s).wait_send())
    others(lambda s: scatter(p_out, p_back, p_sems[2], s).wait_send())
    others(lambda s: scatter(s_send, s_land, s_sems[0], s).wait_send())
    others(lambda s: scatter(s_out, s_back, s_sems[2], s).wait_send())
    for t in range(nz):
        @pl.when(t > z)
        def _():
            z_copy(p_total, p_far, p_sems[1], t).wait_send()

        @pl.when(t < z)
        def _():
            z_copy(s_total, s_far, s_sems[1], t).wait_send()
    for send, land, zs, zland, xs, xland, total, grad, sems in (
        (rq_send, rq_land, rq_z, rq_zland, rq_x, rq_xland, rq_sum, gq_ref, rq_sems),
        (rk_send, rk_land, rk_z, rk_zland, rk_x, rk_xland, rk_sum, gk_ref, rk_sems),
    ):
        others(lambda s: scatter(send, land, sems[0], s).wait_send())
        others(lambda t: z_copy(zs, zland, sems[1], t).wait_send(), nz, z)
        others(lambda t: x_copy(xs, xland, sems[2], t).wait_send(), nx, x)
        others(lambda s: share(total, grad, sems[3], s).wait_send())
        others(lambda s: share_arrival(total, grad, sems[3], s).wait_recv())
    store.wait()


def body(queries, keys, values, keep_count, query_map, key_map, cotangent):
    _, tokens, heads, width = queries.shape
    rank = query_map.shape[2]
    tiles = tokens // TILE
    sizes = tuple(lax.axis_size(a) for a in (Z_AXIS, Y_AXIS, C_AXIS, X_AXIS))
    nz, ny, nc, nx = sizes
    group = ny * nc
    own = heads // group
    ext = tokens + TILE
    part = (own * rank, width)
    slab = (own * rank + 8, width)
    dma = pltpu.SemaphoreType.DMA

    def vmem(shape, dtype=F32):
        return pltpu.VMEM(shape, dtype)

    def sums():
        return [
            vmem((group, *part)), vmem((group, *part)), vmem(part), vmem((nz, *part)),
            vmem(part), vmem((nx, *part)), vmem(part),
        ]

    def scans():
        return [
            vmem((group, *slab)), vmem((group, *slab)), vmem(slab), vmem((nz, *slab)),
            vmem((group, *slab)), vmem((group, *slab)),
        ]

    raw = (tokens, heads, width)
    lane_rows = (heads, rank, tokens)
    scratch = [
        *[vmem(raw, BF16)] * 4, vmem((2, TILE, heads, width), BF16), vmem(raw, BF16),
        vmem((heads, tokens, width), BF16), vmem((heads, ext, width), BF16),
        vmem((heads, ext, width), BF16), vmem((heads, tokens, width), BF16),
        vmem((heads, tokens, width), BF16), vmem((heads, tokens, width)),
        vmem(lane_rows), vmem(lane_rows), vmem((heads, rank, ext)), vmem((heads, rank, ext)),
        vmem((heads, 8, ext)), vmem((tiles + 1, heads, 8, TILE), jnp.int32),
        vmem((heads, tiles, rank, width)), vmem(lane_rows), vmem(lane_rows),
        vmem((heads, 8, tokens)), vmem(lane_rows), vmem(lane_rows),
        vmem((heads, tiles, rank, width)), vmem((heads, tiles, rank, width)),
        vmem((heads, rank, width)),
        *scans(), *scans(), *sums(), *sums(), vmem(slab),
        dma((4 * tiles,)), dma, dma((4,)),
        [dma((2 * group,)), dma((2 * nz,)), dma((2 * group,))],
        [dma((2 * group,)), dma((2 * nz,)), dma((2 * group,))],
        [dma((2 * group,)), dma((2 * nz,)), dma((2 * nx,)), dma((2 * group,))],
        [dma((2 * group,)), dma((2 * nz,)), dma((2 * nx,)), dma((2 * group,))],
    ]
    anywhere = pl.BlockSpec(memory_space=pl.ANY)
    here = pl.BlockSpec(memory_space=pltpu.VMEM)
    grad = jax.ShapeDtypeStruct((group, *part), F32)
    out, grad_q, grad_k = pl.pallas_call(
        functools.partial(kernel, sizes),
        out_shape=(jax.ShapeDtypeStruct(raw, BF16), grad, grad),
        in_specs=[anywhere] * 4 + [here] * 3,
        out_specs=(anywhere, here, here),
        scratch_shapes=scratch,
        compiler_params=pltpu.CompilerParams(
            collective_id=0, has_side_effects=True, vmem_limit_bytes=60 * 2**20
        ),
        name="less_step",
    )(
        queries[0], keys[0], values[0], cotangent[0], keep_count[0],
        query_map.transpose(0, 2, 1), key_map.transpose(0, 2, 1),
    )

    def map_grad(g):
        return g.reshape(heads, rank, width).transpose(0, 2, 1)

    return (out[None], map_grad(grad_q), map_grad(grad_k))


def solution(mesh):
    chips, last = mesh.shape["seq"], mesh.shape["batch"]
    torus = Mesh(mesh.devices.reshape(chips // 8, 4, 2, last), (*SEQ, X_AXIS))
    rows = P(X_AXIS, SEQ, None, None)
    return jax.shard_map(
        body,
        mesh=torus,
        in_specs=(rows, rows, rows, P(X_AXIS, None, None), P(), P(), rows),
        out_specs=(rows, P(), P()),
        check_vma=False,
    )
```

```python
import functools
import math

import jax
import jax.numpy as jnp
from jax import lax
from jax.experimental import pallas as pl
from jax.experimental.pallas import tpu as pltpu
from jax.sharding import Mesh
from jax.sharding import PartitionSpec as P

TILE = 128
SHIFT = 1.5
LOG2E = math.log2(math.e)
Z_AXIS, Y_AXIS, C_AXIS, X_AXIS = "seq_0", "seq_1", "seq_2", "batch"
SEQ = (Z_AXIS, Y_AXIS, C_AXIS)
F32, BF16 = jnp.float32, jnp.bfloat16
BLOCK = 16


def dot_nn(a, b):
    return lax.dot_general(a, b, (((1,), (0,)), ((), ())), preferred_element_type=F32)


def dot_nt(a, b):
    return lax.dot_general(a, b, (((1,), (1,)), ((), ())), preferred_element_type=F32)


def dot_tn(a, b):
    return lax.dot_general(a, b, (((0,), (0,)), ((), ())), preferred_element_type=F32)


def halves(x):
    high = x.astype(BF16).astype(F32)
    return high, x - high


def stacked(x):
    return jnp.concatenate(halves(x), 0).astype(BF16)


def folded(x):
    half = x.shape[0] // 2
    return x[:half] + x[half:]


def feature(pre):
    small = jnp.exp(-jnp.abs(pre))
    inverse = 1.0 / (1.0 + small)
    return jnp.maximum(pre, 0.0) + jnp.log1p(small), jnp.where(pre >= 0.0, inverse, small * inverse)


def remote(source, target, send, receive, device):
    return pltpu.make_async_remote_copy(
        src_ref=source,
        dst_ref=target,
        send_sem=send,
        recv_sem=receive,
        device_id=device,
        device_id_type=pl.DeviceIdType.MESH,
    )


def kernel(
    sizes,
    q_hbm, k_hbm, v_hbm, c_hbm, count_ref, wq_ref, wk_ref,
    out_hbm, gq_ref, gk_ref,
    q_raw, k_raw, v_raw, c_raw, halo_raw,
    q_rows, k_rows, v_rows, c_rows, o_rows, weight_rows,
    feat_q, slope_q, feat_k, slope_k, kept_lane, count_lane,
    state_local, norm_local, u_local, row_data, inverse_rows, g_rows, gpre_q, d_state, d_norm, gk_local,
    p_send, p_land, p_total, p_far, p_out, p_back,
    s_send, s_land, s_total, s_far, s_out, s_back,
    rq_send, rq_land, rq_z, rq_zland, rq_x, rq_xland, rq_sum,
    rk_send, rk_land, rk_z, rk_zland, rk_x, rk_xland, rk_sum,
    acc,
    load_sem, store_sem, halo_sems, p_sems, s_sems, rq_sems, rk_sems,
):
    nz, ny, nc, nx = sizes
    group = ny * nc
    devices = nz * group
    tokens, heads, width = q_raw.shape
    tiles = tokens // TILE
    own = heads // group
    lanes = lax.broadcasted_iota(jnp.int32, (8, TILE), 1)
    z, y, c, x = (lax.axis_index(a) for a in (Z_AXIS, Y_AXIS, C_AXIS, X_AXIS))
    me = y * nc + c
    index = z * group + me

    def peer(s):
        return {Y_AXIS: s // nc, C_AXIS: s % nc}

    def place(i):
        return {Z_AXIS: i // group, Y_AXIS: (i // nc) % ny, C_AXIS: i % nc}

    after = place((index + 1) % devices)
    before = place((index + devices - 1) % devices)

    barrier = pltpu.get_barrier_semaphore()

    def greet(device):
        pl.semaphore_signal(barrier, inc=1, device_id=device, device_id_type=pl.DeviceIdType.MESH)

    greet(after)
    greet(before)
    for k in range(1, group):
        greet(peer((me + k) % group))
    for k in range(1, nz):
        greet({Z_AXIS: (z + k) % nz})
    for k in range(1, nx):
        greet({X_AXIS: (x + k) % nx})

    sources = (k_hbm, v_hbm, c_hbm, q_hbm)
    raws = (k_raw, v_raw, c_raw, q_raw)

    def load(a, t):
        rows = pl.ds(t * TILE, TILE)
        return pltpu.make_async_copy(sources[a].at[rows], raws[a].at[rows], load_sem.at[a * tiles + t])

    for a in range(4):
        for t in range(tiles):
            load(a, t).start()

    def by_head(raw, rows, first, target, count):
        def step(b, _):
            block = raw[pl.ds(rows + b * BLOCK, BLOCK)]
            target[:, pl.ds(first + b * BLOCK, BLOCK), :] = jnp.swapaxes(block, 0, 1)
            return 0

        lax.fori_loop(0, count // BLOCK, step, 0, unroll=4)

    for t in range(tiles):
        load(0, t).wait()
        by_head(k_raw, t * TILE, (t + 1) * TILE, k_rows, TILE)
    pl.semaphore_wait(barrier, 2 + group - 1 + nz - 1 + nx - 1)
    halo_from = pl.ds(tokens - TILE, TILE)
    halo_copies = [
        remote(k_hbm.at[halo_from], halo_raw.at[0], halo_sems.at[0], halo_sems.at[2], after),
        remote(v_hbm.at[halo_from], halo_raw.at[1], halo_sems.at[1], halo_sems.at[3], after),
    ]
    halo_copies[0].start()
    for t in range(tiles):
        load(1, t).wait()
        by_head(v_raw, t * TILE, (t + 1) * TILE, v_rows, TILE)

    counts = count_ref[...]
    which = lax.broadcasted_iota(jnp.int32, counts.shape, 1)
    lane16 = lax.broadcasted_iota(jnp.int32, (heads, TILE), 1)
    for e in range(tiles + 1):
        picked = jnp.sum(jnp.where(which == index * tiles + (e - 1), counts, 0), 1, keepdims=True)
        spread = jnp.broadcast_to(picked, (heads, TILE))
        kept = (lane16 < spread).astype(F32)
        for h in range(heads):
            count_lane[e, h] = jnp.broadcast_to(spread[h : h + 1], (8, TILE))
            kept_lane[h, :, e * TILE : (e + 1) * TILE] = jnp.broadcast_to(kept[h : h + 1], (8, TILE))

    def scatter(buffer, land, sems, s):
        return remote(buffer.at[s], land.at[me], sems.at[s], sems.at[group + me], peer(s))

    def arrival(buffer, land, sems, s):
        return remote(buffer.at[s], land.at[s], sems.at[s], sems.at[group + s], peer(s))

    def share(buffer, land, sems, s):
        return remote(buffer, land.at[me], sems.at[s], sems.at[group + me], peer(s))

    def share_arrival(buffer, land, sems, s):
        return remote(buffer, land.at[s], sems.at[s], sems.at[group + s], peer(s))

    def z_copy(buffer, land, sems, t):
        return remote(buffer, land.at[z], sems.at[t], sems.at[nz + z], {Z_AXIS: t})

    def z_arrival(buffer, land, sems, t):
        return remote(buffer, land.at[t], sems.at[t], sems.at[nz + t], {Z_AXIS: t})

    def x_copy(buffer, land, sems, t):
        return remote(buffer, land.at[x], sems.at[t], sems.at[nx + x], {X_AXIS: t})

    def x_arrival(buffer, land, sems, t):
        return remote(buffer, land.at[t], sems.at[t], sems.at[nx + t], {X_AXIS: t})

    def others(step, count=group, here=None):
        here = me if here is None else here
        for k in sorted(range(1, count), key=lambda k: -min(k, count - k)):
            step((here + k) % count)

    def by_owner(compute, buffer, land, sems, ready=None):
        def one(k, _):
            pair = [(me + group // 2 - k) % group, (me + group // 2 + 1 + k) % group]
            if ready is not None:
                for o in pair:
                    pl.when(o != me)(functools.partial(ready, o))
            slices = [compute(o) for o in pair]
            for o, piece in zip(pair, slices):
                buffer[o] = piece
            for o in pair:
                @pl.when(o != me)
                def _():
                    scatter(buffer, land, sems, o).start()
            return 0

        lax.fori_loop(0, group // 2, one, 0)
        land[me] = buffer[me]

    def owner_slice(pieces, norms):
        low = jnp.where(lanes < TILE // 2, norms[0], norms[1])
        return jnp.concatenate([*pieces, low], 0)

    def norm_of(tile, i):
        turned = pltpu.roll(tile, TILE // 2, 1)
        return jnp.where(lanes < TILE // 2, *((tile, turned) if i == 0 else (turned, tile)))

    own_rows = pl.ds(TILE, tokens)

    def state_slice(o):
        pieces, norms = [], []
        for i in range(own):
            h = o * own + i
            feat, slope = feature(dot_nt(wk_ref[h], k_rows[h, own_rows, :]) - SHIFT)
            feat_k[h, :, TILE:] = feat
            slope_k[h, :, TILE:] = slope
            pieces.append(folded(dot_nn(stacked(feat), v_rows[h, own_rows, :])))
            norms.append(jnp.sum(feat, 1, keepdims=True))
        return owner_slice(pieces, norms)

    by_owner(state_slice, p_send, p_land, p_sems[0])
    halo_copies[1].start()

    def query_features(h, _):
        feat, slope = feature(dot_nt(wq_ref[h], q_rows[h]) - SHIFT)
        feat_q[h] = feat
        slope_q[h] = slope
        return 0

    for t in range(tiles):
        load(2, t).wait()
        by_head(c_raw, t * TILE, t * TILE, c_rows, TILE)
        load(3, t).wait()
        by_head(q_raw, t * TILE, t * TILE, q_rows, TILE)
    lax.fori_loop(0, heads, query_features, 0, unroll=4)

    def local_terms(h, j, state, norm):
        cols = slice(j * TILE, (j + 1) * TILE)
        state_local[h, j] = state
        norm_local[h, :, cols] = jnp.broadcast_to(norm, (8, TILE))
        u = folded(dot_nt(stacked(state), c_rows[h, cols, :]))
        u_local[h, :, cols] = u
        fq = feat_q[h, :, cols]
        row_data[h, 3:4, cols] = jnp.sum(fq * norm, 0, keepdims=True)
        row_data[h, 4:5, cols] = jnp.sum(fq * u, 0, keepdims=True)

    def local_states(h, _):
        full, full_norm, out, out_norm = [], [], [], []
        for i in range(tiles - 1):
            cols = slice((i + 1) * TILE, (i + 2) * TILE)
            feat = feat_k[h, :, cols]
            gone = feat * (1.0 - kept_lane[h, :, cols])
            both = jnp.concatenate([*halves(feat), *halves(gone)], 0).astype(BF16)
            result = dot_nn(both, v_rows[h, cols, :])
            full.append(folded(result[:16]))
            out.append(folded(result[16:]))
            full_norm.append(jnp.sum(feat, 1, keepdims=True))
            out_norm.append(jnp.sum(gone, 1, keepdims=True))
        for j in range(1, tiles):
            local_terms(
                h, j, sum(full[: j - 1], out[j - 1]), sum(full_norm[: j - 1], out_norm[j - 1])
            )
        return 0

    scale2 = LOG2E / math.sqrt(width)
    key_at = lax.broadcasted_iota(jnp.int32, (TILE, TILE), 0)
    causal = key_at <= lax.broadcasted_iota(jnp.int32, (TILE, TILE), 1)

    def sparse(h, j):
        cols = slice(j * TILE, (j + 1) * TILE)
        window = slice(j * TILE, (j + 2) * TILE)
        v_window = v_rows[h, window, :]
        scores = dot_nt(k_rows[h, window, :], q_rows[h, cols, :])
        live = key_at < count_lane[j, h, 0:1, :]
        near = jnp.where(live, scores[:TILE], -1e30)
        here = jnp.where(causal, scores[TILE:], -1e30)
        top = jnp.maximum(jnp.max(near, 0, keepdims=True), jnp.max(here, 0, keepdims=True))
        shift = top * scale2
        masked = jnp.concatenate([near, here], 0)
        weights = jnp.exp2(masked * scale2 - shift)
        rounded = weights.astype(BF16)
        weight_rows[h, j] = rounded
        along = dot_nt(v_window, c_rows[h, cols, :])
        row_data[h, 0:1, cols] = jnp.exp2(-shift)
        row_data[h, 1:2, cols] = jnp.sum(weights, 0, keepdims=True)
        row_data[h, 2:3, cols] = jnp.sum(weights * along, 0, keepdims=True)

    def sparse_tile(j):
        def one(h, _):
            sparse(h, j)
            return 0

        lax.fori_loop(0, heads, one, 0, unroll=4)

    others(lambda s: arrival(p_send, p_land, p_sems[0], s).wait_recv())
    p_total[...] = sum(p_land[s] for s in range(1, group)) + p_land[0]
    for t in range(1, nz):
        @pl.when(t > z)
        def _():
            z_copy(p_total, p_far, p_sems[1], t).start()

    lax.fori_loop(0, heads, local_states, 0, unroll=4)
    sparse_tile(1)
    sparse_tile(2)

    acc[...] = jnp.zeros_like(acc)
    for t in range(nz - 1):
        @pl.when(t < z)
        def _():
            z_arrival(p_total, p_far, p_sems[1], t).wait_recv()
            acc[...] += p_far[t]

    running = acc[...]
    for s in range(group):
        p_out[s] = running
        running = running + p_land[s]
    others(lambda s: scatter(p_out, p_back, p_sems[2], s).start())
    p_back[me] = p_out[me]

    sparse_tile(3)

    for copy in halo_copies:
        copy.wait_recv()
    by_head(halo_raw.at[0], 0, 0, k_rows, TILE)
    by_head(halo_raw.at[1], 0, 0, v_rows, TILE)

    def halo_head(h, _):
        feat, slope = feature(dot_nt(wk_ref[h], k_rows[h, :TILE, :]) - SHIFT)
        slope_k[h, :, :TILE] = slope
        held = feat * kept_lane[h, :, :TILE]
        state = folded(dot_nn(stacked(held), v_rows[h, :TILE, :]))
        local_terms(h, 0, -state, -jnp.sum(held, 1, keepdims=True))
        sparse(h, 0)
        return 0

    lax.fori_loop(0, heads, halo_head, 0, unroll=4)

    def d_slice(o):
        pieces, norms = [], []
        back = p_back[o]
        for i in range(own):
            h = o * own + i
            far = back[i * 8 : (i + 1) * 8]
            far_norm = jnp.concatenate([norm_of(back[own * 8 :], i)] * tiles, 1)
            fq = feat_q[h]
            u_far = folded(dot_nt(stacked(far), c_rows[h]))
            decay = row_data[h, 0:1, :]
            kd = row_data[h, 3:4, :] + jnp.sum(fq * far_norm, 0, keepdims=True)
            cu = row_data[h, 4:5, :] + jnp.sum(fq * u_far, 0, keepdims=True)
            inverse = 1.0 / (row_data[h, 1:2, :] + decay * kd)
            share_of = decay * inverse
            g = fq * share_of
            g_den = -share_of * ((row_data[h, 2:3, :] + decay * cu) * inverse)
            g_rows[h] = g
            inverse_rows[h] = inverse
            gpre_q[h] = (
                share_of * (u_local[h] + u_far) + g_den * (norm_local[h] + far_norm)
            ) * slope_q[h]
            weighted = fq * g_den
            total, total_norm = None, None
            for j in range(tiles):
                cols = slice(j * TILE, (j + 1) * TILE)
                piece = folded(dot_nn(stacked(g[:, cols]), c_rows[h, cols, :]))
                norm = jnp.sum(weighted[:, cols], 1, keepdims=True)
                d_state[h, j] = piece
                d_norm[h, j] = jnp.broadcast_to(norm, (8, TILE))
                total = piece if j == 0 else total + piece
                total_norm = norm if j == 0 else total_norm + norm
            pieces.append(total)
            norms.append(total_norm)
        return owner_slice(pieces, norms)

    by_owner(
        d_slice, s_send, s_land, s_sems[0],
        lambda o: arrival(p_out, p_back, p_sems[2], o).wait_recv(),
    )

    def query_slice(o):
        pieces = []
        for i in range(own):
            h = o * own + i
            pieces.append(folded(dot_nn(stacked(gpre_q[h]), q_rows[h])))
        return jnp.concatenate(pieces, 0)

    by_owner(query_slice, rq_send, rq_land, rq_sems[0])

    def key_local(h, _):
        parts = []
        for e in range(tiles):
            cols = slice(e * TILE, (e + 1) * TILE)
            v_tile = v_rows[h, cols, :]
            kept = kept_lane[h, :, cols]
            if e == 0:
                grad = -kept * (folded(dot_nt(stacked(d_state[h, 0]), v_tile)) + d_norm[h, 0])
            else:
                near, near_norm = d_state[h, e], d_norm[h, e]
                if e + 1 < tiles:
                    full = sum([d_state[h, j] for j in range(e + 2, tiles)], d_state[h, e + 1])
                    full_norm = sum([d_norm[h, j] for j in range(e + 2, tiles)], d_norm[h, e + 1])
                    both = jnp.concatenate([*halves(near), *halves(full)], 0).astype(BF16)
                    result = dot_nt(both, v_tile)
                    grad = (1.0 - kept) * (folded(result[:16]) + near_norm)
                    grad = grad + (folded(result[16:]) + full_norm)
                else:
                    grad = (1.0 - kept) * (folded(dot_nt(stacked(near), v_tile)) + near_norm)
            parts.append(grad * slope_k[h, :, cols])
        gk_local[h] = folded(dot_nn(stacked(jnp.concatenate(parts, 1)), k_rows[h, :tokens, :]))
        return 0

    sub = lax.broadcasted_iota(jnp.int32, (8, TILE), 0)

    def outputs(h, o, i):
        back = p_back[o]
        far = back[i * 8 : (i + 1) * 8]
        for j in range(tiles):
            cols = slice(j * TILE, (j + 1) * TILE)
            high, low = halves(far + state_local[h, j])
            g_high, g_low = halves(g_rows[h, :, cols])
            first, rest = halves(inverse_rows[h, :, cols])
            second, third = halves(rest)
            inverse = jnp.where(sub == 0, first, jnp.where(sub == 1, second, third))
            inverse = jnp.where(sub < 3, inverse, 0.0)
            left = jnp.concatenate([g_high, g_low, g_high, inverse], 0).astype(BF16)
            zeros, ones = jnp.zeros((8, TILE), F32), jnp.ones((8, TILE), F32)
            right = jnp.concatenate(
                [
                    jnp.concatenate([high, high, low, zeros], 0),
                    jnp.concatenate([zeros, zeros, zeros, ones], 0),
                ],
                1,
            ).astype(BF16)
            both = dot_tn(left, right)
            window = slice(j * TILE, (j + 2) * TILE)
            numer = dot_tn(weight_rows[h, j], v_rows[h, window, :])
            result = numer * both[:, TILE:] + both[:, :TILE]
            o_rows[h, cols, :] = result.astype(BF16)

    def outputs_owner(o, _):
        for i in range(own):
            outputs(o * own + i, o, i)
        return 0

    lax.fori_loop(0, heads, key_local, 0, unroll=4)

    others(lambda s: arrival(s_send, s_land, s_sems[0], s).wait_recv())
    s_total[...] = sum(s_land[s] for s in range(1, group)) + s_land[0]
    for t in range(nz - 1):
        @pl.when(t < z)
        def _():
            z_copy(s_total, s_far, s_sems[1], t).start()

    others(lambda s: arrival(rq_send, rq_land, rq_sems[0], s).wait_recv())
    rq_z[...] = sum(rq_land[s] for s in range(1, group)) + rq_land[0]
    others(lambda t: z_copy(rq_z, rq_zland, rq_sems[1], t).start(), nz, z)
    rq_zland[z] = rq_z[...]

    lax.fori_loop(0, 4, outputs_owner, 0)

    acc[...] = jnp.zeros_like(acc)
    for t in range(1, nz):
        @pl.when(t > z)
        def _():
            z_arrival(s_total, s_far, s_sems[1], t).wait_recv()
            acc[...] += s_far[t]

    running = acc[...]
    for s in reversed(range(group)):
        s_out[s] = running
        running = running + s_land[s]
    others(lambda s: scatter(s_out, s_back, s_sems[2], s).start())
    s_back[me] = s_out[me]

    others(lambda t: z_arrival(rq_z, rq_zland, rq_sems[1], t).wait_recv(), nz, z)
    rq_x[...] = sum(rq_zland[t] for t in range(1, nz)) + rq_zland[0]
    others(lambda t: x_copy(rq_x, rq_xland, rq_sems[2], t).start(), nx, x)
    rq_xland[x] = rq_x[...]

    lax.fori_loop(4, 6, outputs_owner, 0)

    def key_slice(o):
        pieces = []
        back = s_back[o]
        for i in range(own):
            h = o * own + i
            far_norm = jnp.concatenate([norm_of(back[own * 8 :], i)] * tiles, 1)
            grad = folded(dot_nt(stacked(back[i * 8 : (i + 1) * 8]), v_rows[h, own_rows, :]))
            grad = (grad + far_norm) * slope_k[h, :, TILE:]
            pieces.append(gk_local[h] + folded(dot_nn(stacked(grad), k_rows[h, own_rows, :])))
        return jnp.concatenate(pieces, 0)

    by_owner(
        key_slice, rk_send, rk_land, rk_sems[0],
        lambda o: arrival(s_out, s_back, s_sems[2], o).wait_recv(),
    )

    others(lambda t: x_arrival(rq_x, rq_xland, rq_sems[2], t).wait_recv(), nx, x)
    rq_sum[...] = sum(rq_xland[t] for t in range(1, nx)) + rq_xland[0]
    others(lambda s: share(rq_sum, gq_ref, rq_sems[3], s).start())
    gq_ref[me] = rq_sum[...]

    lax.fori_loop(6, group, outputs_owner, 0)
    store = pltpu.make_async_copy(o_rows, out_hbm, store_sem)
    store.start()

    others(lambda s: arrival(rk_send, rk_land, rk_sems[0], s).wait_recv())
    rk_z[...] = sum(rk_land[s] for s in range(1, group)) + rk_land[0]
    others(lambda t: z_copy(rk_z, rk_zland, rk_sems[1], t).start(), nz, z)
    rk_zland[z] = rk_z[...]
    others(lambda t: z_arrival(rk_z, rk_zland, rk_sems[1], t).wait_recv(), nz, z)
    rk_x[...] = sum(rk_zland[t] for t in range(1, nz)) + rk_zland[0]
    others(lambda t: x_copy(rk_x, rk_xland, rk_sems[2], t).start(), nx, x)
    rk_xland[x] = rk_x[...]
    others(lambda t: x_arrival(rk_x, rk_xland, rk_sems[2], t).wait_recv(), nx, x)
    rk_sum[...] = sum(rk_xland[t] for t in range(1, nx)) + rk_xland[0]
    others(lambda s: share(rk_sum, gk_ref, rk_sems[3], s).start())
    gk_ref[me] = rk_sum[...]

    for copy in halo_copies:
        copy.wait_send()
    others(lambda s: scatter(p_send, p_land, p_sems[0], s).wait_send())
    others(lambda s: scatter(p_out, p_back, p_sems[2], s).wait_send())
    others(lambda s: scatter(s_send, s_land, s_sems[0], s).wait_send())
    others(lambda s: scatter(s_out, s_back, s_sems[2], s).wait_send())
    for t in range(nz):
        @pl.when(t > z)
        def _():
            z_copy(p_total, p_far, p_sems[1], t).wait_send()

        @pl.when(t < z)
        def _():
            z_copy(s_total, s_far, s_sems[1], t).wait_send()
    for send, land, zs, zland, xs, xland, total, grad, sems in (
        (rq_send, rq_land, rq_z, rq_zland, rq_x, rq_xland, rq_sum, gq_ref, rq_sems),
        (rk_send, rk_land, rk_z, rk_zland, rk_x, rk_xland, rk_sum, gk_ref, rk_sems),
    ):
        others(lambda s: scatter(send, land, sems[0], s).wait_send())
        others(lambda t: z_copy(zs, zland, sems[1], t).wait_send(), nz, z)
        others(lambda t: x_copy(xs, xland, sems[2], t).wait_send(), nx, x)
        others(lambda s: share(total, grad, sems[3], s).wait_send())
        others(lambda s: share_arrival(total, grad, sems[3], s).wait_recv())
    store.wait()


def finish(rows_ref, gq_ref, gk_ref, out_ref, gq_out, gk_out):
    for b in range(out_ref.shape[0] // BLOCK):
        rows = slice(b * BLOCK, (b + 1) * BLOCK)
        out_ref[rows] = jnp.swapaxes(rows_ref[:, rows, :], 0, 1)

    @pl.when(pl.program_id(0) == 0)
    def _():
        gq_out[...] = gq_ref[...]
        gk_out[...] = gk_ref[...]


def body(queries, keys, values, keep_count, query_map, key_map, cotangent):
    _, tokens, heads, width = queries.shape
    rank = query_map.shape[2]
    tiles = tokens // TILE
    sizes = tuple(lax.axis_size(a) for a in (Z_AXIS, Y_AXIS, C_AXIS, X_AXIS))
    nz, ny, nc, nx = sizes
    group = ny * nc
    own = heads // group
    ext = tokens + TILE
    part = (own * rank, width)
    slab = (own * rank + 8, width)
    dma = pltpu.SemaphoreType.DMA

    def vmem(shape, dtype=F32):
        return pltpu.VMEM(shape, dtype)

    def sums():
        return [
            vmem((group, *part)), vmem((group, *part)), vmem(part), vmem((nz, *part)),
            vmem(part), vmem((nx, *part)), vmem(part),
        ]

    def scans():
        return [
            vmem((group, *slab)), vmem((group, *slab)), vmem(slab), vmem((nz, *slab)),
            vmem((group, *slab)), vmem((group, *slab)),
        ]

    raw = (tokens, heads, width)
    lane_rows = (heads, rank, tokens)
    scratch = [
        *[vmem(raw, BF16)] * 4, vmem((2, TILE, heads, width), BF16),
        vmem((heads, tokens, width), BF16), vmem((heads, ext, width), BF16),
        vmem((heads, ext, width), BF16), vmem((heads, tokens, width), BF16),
        vmem((heads, tokens, width), BF16), vmem((heads, tiles, 2 * TILE, TILE), BF16),
        vmem(lane_rows), vmem(lane_rows), vmem((heads, rank, ext)), vmem((heads, rank, ext)),
        vmem((heads, 8, ext)), vmem((tiles + 1, heads, 8, TILE), jnp.int32),
        vmem((heads, tiles, rank, width)), vmem(lane_rows), vmem(lane_rows),
        vmem((heads, 8, tokens)), vmem((heads, 1, tokens)), vmem(lane_rows), vmem(lane_rows),
        vmem((heads, tiles, rank, width)), vmem((heads, tiles, rank, width)),
        vmem((heads, rank, width)),
        *scans(), *scans(), *sums(), *sums(), vmem(slab),
        dma((4 * tiles,)), dma, dma((4,)),
        [dma((2 * group,)), dma((2 * nz,)), dma((2 * group,))],
        [dma((2 * group,)), dma((2 * nz,)), dma((2 * group,))],
        [dma((2 * group,)), dma((2 * nz,)), dma((2 * nx,)), dma((2 * group,))],
        [dma((2 * group,)), dma((2 * nz,)), dma((2 * nx,)), dma((2 * group,))],
    ]
    anywhere = pl.BlockSpec(memory_space=pl.ANY)
    here = pl.BlockSpec(memory_space=pltpu.VMEM)
    grad = jax.ShapeDtypeStruct((group, *part), F32)
    rows, grad_q, grad_k = pl.pallas_call(
        functools.partial(kernel, sizes),
        out_shape=(jax.ShapeDtypeStruct((heads, tokens, width), BF16), grad, grad),
        in_specs=[anywhere] * 4 + [here] * 3,
        out_specs=(anywhere, here, here),
        scratch_shapes=scratch,
        compiler_params=pltpu.CompilerParams(
            collective_id=0, has_side_effects=True, vmem_limit_bytes=60 * 2**20
        ),
        name="less_step",
    )(
        queries[0], keys[0], values[0], cotangent[0], keep_count[0],
        query_map.transpose(0, 2, 1), key_map.transpose(0, 2, 1),
    )

    whole = pl.BlockSpec((group, *part), lambda t: (0, 0, 0))
    out, grad_q, grad_k = pl.pallas_call(
        finish,
        grid=(tiles,),
        out_shape=(jax.ShapeDtypeStruct(raw, BF16), grad, grad),
        in_specs=[pl.BlockSpec((heads, TILE, width), lambda t: (0, t, 0)), whole, whole],
        out_specs=(pl.BlockSpec((TILE, heads, width), lambda t: (t, 0, 0)), whole, whole),
        name="finish",
    )(rows, grad_q, grad_k)

    def map_grad(g):
        return g.reshape(heads, rank, width).transpose(0, 2, 1)

    return (out[None], map_grad(grad_q), map_grad(grad_k))


def solution(mesh):
    chips, last = mesh.shape["seq"], mesh.shape["batch"]
    torus = Mesh(mesh.devices.reshape(chips // 8, 4, 2, last), (*SEQ, X_AXIS))
    rows = P(X_AXIS, SEQ, None, None)
    return jax.shard_map(
        body,
        mesh=torus,
        in_specs=(rows, rows, rows, P(X_AXIS, None, None), P(), P(), rows),
        out_specs=(rows, P(), P()),
        check_vma=False,
    )
```

```python
import functools
import math

import jax
import jax.numpy as jnp
from jax import lax
from jax.experimental import pallas as pl
from jax.experimental.pallas import tpu as pltpu
from jax.sharding import Mesh
from jax.sharding import PartitionSpec as P

TILE = 128
SHIFT = 1.5
LOG2E = math.log2(math.e)
Z_AXIS, Y_AXIS, C_AXIS, X_AXIS = "seq_0", "seq_1", "seq_2", "batch"
SEQ = (Z_AXIS, Y_AXIS, C_AXIS)
F32, BF16 = jnp.float32, jnp.bfloat16
BLOCK = 16
HALO_PIECES = ((0, 0, 64), (0, 64, 64), (1, 0, 128))


def dot_nn(a, b):
    return lax.dot_general(a, b, (((1,), (0,)), ((), ())), preferred_element_type=F32)


def dot_nt(a, b):
    return lax.dot_general(a, b, (((1,), (1,)), ((), ())), preferred_element_type=F32)


def dot_tn(a, b):
    return lax.dot_general(a, b, (((0,), (0,)), ((), ())), preferred_element_type=F32)


def halves(x):
    high = x.astype(BF16).astype(F32)
    return high, x - high


def stacked(x):
    return jnp.concatenate(halves(x), 0).astype(BF16)


def folded(x):
    half = x.shape[0] // 2
    return x[:half] + x[half:]


def feature(pre):
    small = jnp.exp(-jnp.abs(pre))
    inverse = 1.0 / (1.0 + small)
    return jnp.maximum(pre, 0.0) + jnp.log1p(small), jnp.where(pre >= 0.0, inverse, small * inverse)


def remote(source, target, send, receive, device):
    return pltpu.make_async_remote_copy(
        src_ref=source,
        dst_ref=target,
        send_sem=send,
        recv_sem=receive,
        device_id=device,
        device_id_type=pl.DeviceIdType.MESH,
    )


def kernel(
    sizes,
    q_hbm, k_hbm, v_hbm, c_hbm, count_hbm, wq_hbm, wk_hbm,
    out_hbm, gq_hbm, gk_hbm,
    count_ref, wq_ref, wk_ref, o_raw,
    q_raw, k_raw, v_raw, c_raw, halo_raw,
    q_rows, k_rows, v_rows, c_rows, o_rows, weight_rows,
    feat_q, slope_q, feat_k, slope_k, kept_lane, count_lane,
    state_local, norm_local, u_local, row_data, inverse_rows, g_rows, gpre_q, d_state, d_norm, gk_local,
    p_send, p_land, p_total, p_far, p_out, p_back,
    s_send, s_land, s_total, s_far, s_out, s_back,
    rq_send, rq_land, rq_z, rq_zland, rq_x, rq_xland, rq_sum,
    rk_send, rk_land, rk_z, rk_zland, rk_x, rk_xland, rk_sum,
    acc,
    load_sem, store_sem, halo_sems, p_sems, s_sems, rq_sems, rk_sems,
):
    nz, ny, nc, nx = sizes
    group = ny * nc
    devices = nz * group
    tokens, heads, width = q_raw.shape
    tiles = tokens // TILE
    own = heads // group
    lanes = lax.broadcasted_iota(jnp.int32, (8, TILE), 1)
    z, y, c, x = (lax.axis_index(a) for a in (Z_AXIS, Y_AXIS, C_AXIS, X_AXIS))
    me = y * nc + c
    index = z * group + me

    def peer(s):
        return {Y_AXIS: s // nc, C_AXIS: s % nc}

    def place(i):
        return {Z_AXIS: i // group, Y_AXIS: (i // nc) % ny, C_AXIS: i % nc}

    after = place((index + 1) % devices)
    before = place((index + devices - 1) % devices)

    barrier = pltpu.get_barrier_semaphore()

    def greet(device):
        pl.semaphore_signal(barrier, inc=1, device_id=device, device_id_type=pl.DeviceIdType.MESH)

    greet(after)
    greet(before)
    for k in range(1, group):
        greet(peer((me + k) % group))
    for k in range(1, nz):
        greet({Z_AXIS: (z + k) % nz})
    for k in range(1, nx):
        greet({X_AXIS: (x + k) % nx})

    sources = (k_hbm, v_hbm, c_hbm, q_hbm)
    raws = (k_raw, v_raw, c_raw, q_raw)

    def load(a, t):
        rows = pl.ds(t * TILE, TILE)
        return pltpu.make_async_copy(sources[a].at[rows], raws[a].at[rows], load_sem.at[a * tiles + t])

    small = [
        pltpu.make_async_copy(source, target, load_sem.at[4 * tiles + n])
        for n, (source, target) in enumerate(
            ((wk_hbm, wk_ref), (count_hbm, count_ref), (wq_hbm, wq_ref))
        )
    ]
    for a in range(4):
        for t in range(tiles):
            load(a, t).start()
        if a == 0:
            for copy in small:
                copy.start()

    def by_head(raw, rows, first, target, count):
        def step(b, _):
            block = raw[pl.ds(rows + b * BLOCK, BLOCK)]
            target[:, pl.ds(first + b * BLOCK, BLOCK), :] = jnp.swapaxes(block, 0, 1)
            return 0

        lax.fori_loop(0, count // BLOCK, step, 0, unroll=4)

    for t in range(tiles):
        load(0, t).wait()
        by_head(k_raw, t * TILE, (t + 1) * TILE, k_rows, TILE)
    pl.semaphore_wait(barrier, 2 + group - 1 + nz - 1 + nx - 1)
    halo_copies = []
    for n, (a, first, count) in enumerate(HALO_PIECES):
        source = (k_hbm, v_hbm)[a].at[pl.ds(tokens - TILE + first, count)]
        target = halo_raw.at[a, pl.ds(first, count)]
        halo_copies.append(remote(source, target, halo_sems.at[0, n], halo_sems.at[1, n], after))
    halo_copies[0].start()
    for t in range(tiles):
        load(1, t).wait()
        by_head(v_raw, t * TILE, (t + 1) * TILE, v_rows, TILE)

    for copy in small:
        copy.wait()
    counts = count_ref[...]
    which = lax.broadcasted_iota(jnp.int32, counts.shape, 1)
    lane16 = lax.broadcasted_iota(jnp.int32, (heads, TILE), 1)
    for e in range(tiles + 1):
        picked = jnp.sum(jnp.where(which == index * tiles + (e - 1), counts, 0), 1, keepdims=True)
        spread = jnp.broadcast_to(picked, (heads, TILE))
        kept = (lane16 < spread).astype(F32)
        for h in range(heads):
            count_lane[e, h] = jnp.broadcast_to(spread[h : h + 1], (8, TILE))
            kept_lane[h, :, e * TILE : (e + 1) * TILE] = jnp.broadcast_to(kept[h : h + 1], (8, TILE))

    def scatter(buffer, land, sems, s):
        return remote(buffer.at[s], land.at[me], sems.at[s], sems.at[group + me], peer(s))

    def arrival(buffer, land, sems, s):
        return remote(buffer.at[s], land.at[s], sems.at[s], sems.at[group + s], peer(s))

    def share(buffer, land, sems, s):
        return remote(buffer, land.at[me], sems.at[s], sems.at[group + me], peer(s))

    def share_arrival(buffer, land, sems, s):
        return remote(buffer, land.at[s], sems.at[s], sems.at[group + s], peer(s))

    def z_copy(buffer, land, sems, t):
        return remote(buffer, land.at[z], sems.at[t], sems.at[nz + z], {Z_AXIS: t})

    def z_arrival(buffer, land, sems, t):
        return remote(buffer, land.at[t], sems.at[t], sems.at[nz + t], {Z_AXIS: t})

    def x_copy(buffer, land, sems, t):
        return remote(buffer, land.at[x], sems.at[t], sems.at[nx + x], {X_AXIS: t})

    def x_arrival(buffer, land, sems, t):
        return remote(buffer, land.at[t], sems.at[t], sems.at[nx + t], {X_AXIS: t})

    def others(step, count=group, here=None):
        here = me if here is None else here
        for k in sorted(range(1, count), key=lambda k: -min(k, count - k)):
            step((here + k) % count)

    def by_owner(compute, buffer, land, sems, ready=None):
        def one(k, _):
            pair = [(me + group // 2 - k) % group, (me + group // 2 + 1 + k) % group]
            if ready is not None:
                for o in pair:
                    pl.when(o != me)(functools.partial(ready, o))
            slices = [compute(o) for o in pair]
            for o, piece in zip(pair, slices):
                buffer[o] = piece
            for o in pair:
                @pl.when(o != me)
                def _():
                    scatter(buffer, land, sems, o).start()
            return 0

        lax.fori_loop(0, group // 2, one, 0)
        land[me] = buffer[me]

    def owner_slice(pieces, norms):
        low = jnp.where(lanes < TILE // 2, norms[0], norms[1])
        return jnp.concatenate([*pieces, low], 0)

    def norm_of(tile, i):
        turned = pltpu.roll(tile, TILE // 2, 1)
        return jnp.where(lanes < TILE // 2, *((tile, turned) if i == 0 else (turned, tile)))

    own_rows = pl.ds(TILE, tokens)

    def state_slice(o):
        pieces, norms = [], []
        for i in range(own):
            h = o * own + i
            feat, slope = feature(dot_nt(wk_ref[h], k_rows[h, own_rows, :]) - SHIFT)
            feat_k[h, :, TILE:] = feat
            slope_k[h, :, TILE:] = slope
            pieces.append(folded(dot_nn(stacked(feat), v_rows[h, own_rows, :])))
            norms.append(jnp.sum(feat, 1, keepdims=True))
        return owner_slice(pieces, norms)

    by_owner(state_slice, p_send, p_land, p_sems[0])
    for copy in halo_copies[1:]:
        copy.start()

    def query_features(h, _):
        feat, slope = feature(dot_nt(wq_ref[h], q_rows[h]) - SHIFT)
        feat_q[h] = feat
        slope_q[h] = slope
        return 0

    for t in range(tiles):
        load(2, t).wait()
        by_head(c_raw, t * TILE, t * TILE, c_rows, TILE)
        load(3, t).wait()
        by_head(q_raw, t * TILE, t * TILE, q_rows, TILE)
    lax.fori_loop(0, heads, query_features, 0, unroll=4)

    def local_terms(h, j, state, norm):
        cols = slice(j * TILE, (j + 1) * TILE)
        state_local[h, j] = state
        norm_local[h, :, cols] = jnp.broadcast_to(norm, (8, TILE))
        u = folded(dot_nt(stacked(state), c_rows[h, cols, :]))
        u_local[h, :, cols] = u
        fq = feat_q[h, :, cols]
        row_data[h, 3:4, cols] = jnp.sum(fq * norm, 0, keepdims=True)
        row_data[h, 4:5, cols] = jnp.sum(fq * u, 0, keepdims=True)

    def local_states(h, _):
        span = slice(TILE, tiles * TILE)
        feat = feat_k[h, :, span]
        gone = feat * (1.0 - kept_lane[h, :, span])
        lines, norms = [], []
        for j in range(1, tiles):
            cut = (j - 1) * TILE
            pieces = [feat[:, :cut]] * (cut > 0) + [gone[:, cut : cut + TILE]]
            pieces += [jnp.zeros((8, (tiles - 1 - j) * TILE), F32)] * (j < tiles - 1)
            line = jnp.concatenate(pieces, 1)
            lines += halves(line)
            blocks = [line[:, i * TILE : (i + 1) * TILE] for i in range(j)]
            norms.append(jnp.sum(sum(blocks[1:], blocks[0]), 1, keepdims=True))
        result = dot_nn(jnp.concatenate(lines, 0).astype(BF16), v_rows[h, span, :])
        for j in range(1, tiles):
            local_terms(h, j, folded(result[(j - 1) * 16 : j * 16]), norms[j - 1])
        return 0

    scale2 = LOG2E / math.sqrt(width)
    key_at = lax.broadcasted_iota(jnp.int32, (TILE, TILE), 0)
    causal = key_at <= lax.broadcasted_iota(jnp.int32, (TILE, TILE), 1)

    def sparse(h, j):
        cols = slice(j * TILE, (j + 1) * TILE)
        window = slice(j * TILE, (j + 2) * TILE)
        v_window = v_rows[h, window, :]
        scores = dot_nt(k_rows[h, window, :], q_rows[h, cols, :])
        live = key_at < count_lane[j, h, 0:1, :]
        near = jnp.where(live, scores[:TILE], -1e30)
        here = jnp.where(causal, scores[TILE:], -1e30)
        top = jnp.maximum(jnp.max(near, 0, keepdims=True), jnp.max(here, 0, keepdims=True))
        shift = top * scale2
        masked = jnp.concatenate([near, here], 0)
        weights = jnp.exp2(masked * scale2 - shift)
        rounded = weights.astype(BF16)
        weight_rows[h, j] = rounded
        along = dot_nt(v_window, c_rows[h, cols, :])
        row_data[h, 0:1, cols] = jnp.exp2(-shift)
        row_data[h, 1:2, cols] = jnp.sum(weights, 0, keepdims=True)
        row_data[h, 2:3, cols] = jnp.sum(rounded.astype(F32) * along, 0, keepdims=True)

    def sparse_tile(j):
        def one(h, _):
            sparse(h, j)
            return 0

        lax.fori_loop(0, heads, one, 0, unroll=4)

    others(lambda s: arrival(p_send, p_land, p_sems[0], s).wait_recv())
    p_total[...] = sum(p_land[s] for s in range(1, group)) + p_land[0]
    for t in range(1, nz):
        @pl.when(t > z)
        def _():
            z_copy(p_total, p_far, p_sems[1], t).start()

    lax.fori_loop(0, heads, local_states, 0, unroll=4)
    sparse_tile(1)
    sparse_tile(2)

    acc[...] = jnp.zeros_like(acc)
    for t in range(nz - 1):
        @pl.when(t < z)
        def _():
            z_arrival(p_total, p_far, p_sems[1], t).wait_recv()
            acc[...] += p_far[t]

    running = acc[...]
    for s in range(group):
        p_out[s] = running
        running = running + p_land[s]
    others(lambda s: scatter(p_out, p_back, p_sems[2], s).start())
    p_back[me] = p_out[me]

    sparse_tile(3)

    for copy in halo_copies:
        copy.wait_recv()
    by_head(halo_raw.at[0], 0, 0, k_rows, TILE)
    by_head(halo_raw.at[1], 0, 0, v_rows, TILE)

    def halo_head(h, _):
        feat, slope = feature(dot_nt(wk_ref[h], k_rows[h, :TILE, :]) - SHIFT)
        slope_k[h, :, :TILE] = slope
        held = feat * kept_lane[h, :, :TILE]
        state = folded(dot_nn(stacked(held), v_rows[h, :TILE, :]))
        local_terms(h, 0, -state, -jnp.sum(held, 1, keepdims=True))
        sparse(h, 0)
        return 0

    lax.fori_loop(0, heads, halo_head, 0, unroll=4)

    def d_slice(o):
        pieces, norms = [], []
        back = p_back[o]
        for i in range(own):
            h = o * own + i
            far = back[i * 8 : (i + 1) * 8]
            far_norm = jnp.concatenate([norm_of(back[own * 8 :], i)] * tiles, 1)
            fq = feat_q[h]
            u_far = folded(dot_nt(stacked(far), c_rows[h]))
            decay = row_data[h, 0:1, :]
            kd = row_data[h, 3:4, :] + jnp.sum(fq * far_norm, 0, keepdims=True)
            cu = row_data[h, 4:5, :] + jnp.sum(fq * u_far, 0, keepdims=True)
            inverse = 1.0 / (row_data[h, 1:2, :] + decay * kd)
            share_of = decay * inverse
            g = fq * share_of
            g_den = -share_of * ((row_data[h, 2:3, :] + decay * cu) * inverse)
            g_rows[h] = g
            inverse_rows[h] = inverse
            gpre_q[h] = (
                share_of * (u_local[h] + u_far) + g_den * (norm_local[h] + far_norm)
            ) * slope_q[h]
            weighted = fq * g_den
            total, total_norm = None, None
            for j in range(tiles):
                cols = slice(j * TILE, (j + 1) * TILE)
                piece = folded(dot_nn(stacked(g[:, cols]), c_rows[h, cols, :]))
                norm = jnp.sum(weighted[:, cols], 1, keepdims=True)
                d_state[h, j] = piece
                d_norm[h, j] = jnp.broadcast_to(norm, (8, TILE))
                total = piece if j == 0 else total + piece
                total_norm = norm if j == 0 else total_norm + norm
            pieces.append(total)
            norms.append(total_norm)
        return owner_slice(pieces, norms)

    by_owner(
        d_slice, s_send, s_land, s_sems[0],
        lambda o: arrival(p_out, p_back, p_sems[2], o).wait_recv(),
    )

    def query_slice(o):
        pieces = []
        for i in range(own):
            h = o * own + i
            pieces.append(folded(dot_nn(stacked(gpre_q[h]), q_rows[h])))
        return jnp.concatenate(pieces, 0)

    by_owner(query_slice, rq_send, rq_land, rq_sems[0])

    def key_local(h, _):
        parts = []
        for e in range(tiles):
            cols = slice(e * TILE, (e + 1) * TILE)
            v_tile = v_rows[h, cols, :]
            kept = kept_lane[h, :, cols]
            if e == 0:
                grad = -kept * (folded(dot_nt(stacked(d_state[h, 0]), v_tile)) + d_norm[h, 0])
            else:
                near, near_norm = d_state[h, e], d_norm[h, e]
                if e + 1 < tiles:
                    full = sum([d_state[h, j] for j in range(e + 2, tiles)], d_state[h, e + 1])
                    full_norm = sum([d_norm[h, j] for j in range(e + 2, tiles)], d_norm[h, e + 1])
                    both = jnp.concatenate([*halves(near), *halves(full)], 0).astype(BF16)
                    result = dot_nt(both, v_tile)
                    grad = (1.0 - kept) * (folded(result[:16]) + near_norm)
                    grad = grad + (folded(result[16:]) + full_norm)
                else:
                    grad = (1.0 - kept) * (folded(dot_nt(stacked(near), v_tile)) + near_norm)
            parts.append(grad * slope_k[h, :, cols])
        gk_local[h] = folded(dot_nn(stacked(jnp.concatenate(parts, 1)), k_rows[h, :tokens, :]))
        return 0

    sub = lax.broadcasted_iota(jnp.int32, (8, TILE), 0)

    def outputs(h, o, i):
        back = p_back[o]
        far = back[i * 8 : (i + 1) * 8]
        for j in range(tiles):
            cols = slice(j * TILE, (j + 1) * TILE)
            high, low = halves(far + state_local[h, j])
            g_high, g_low = halves(g_rows[h, :, cols])
            first, rest = halves(inverse_rows[h, :, cols])
            second, third = halves(rest)
            inverse = jnp.where(sub == 0, first, jnp.where(sub == 1, second, third))
            inverse = jnp.where(sub < 3, inverse, 0.0)
            left = jnp.concatenate([g_high, g_low, g_high, inverse], 0).astype(BF16)
            zeros, ones = jnp.zeros((8, TILE), F32), jnp.ones((8, TILE), F32)
            right = jnp.concatenate(
                [
                    jnp.concatenate([high, high, low, zeros], 0),
                    jnp.concatenate([zeros, zeros, zeros, ones], 0),
                ],
                1,
            ).astype(BF16)
            both = dot_tn(left, right)
            window = slice(j * TILE, (j + 2) * TILE)
            numer = dot_tn(weight_rows[h, j], v_rows[h, window, :])
            result = numer * both[:, TILE:] + both[:, :TILE]
            o_rows[h, cols, :] = result.astype(BF16)

    def outputs_owner(o, _):
        for i in range(own):
            outputs(o * own + i, o, i)
        return 0

    lax.fori_loop(0, heads, key_local, 0, unroll=4)

    others(lambda s: arrival(s_send, s_land, s_sems[0], s).wait_recv())
    s_total[...] = sum(s_land[s] for s in range(1, group)) + s_land[0]
    for t in range(nz - 1):
        @pl.when(t < z)
        def _():
            z_copy(s_total, s_far, s_sems[1], t).start()

    others(lambda s: arrival(rq_send, rq_land, rq_sems[0], s).wait_recv())
    rq_z[...] = sum(rq_land[s] for s in range(1, group)) + rq_land[0]
    others(lambda t: z_copy(rq_z, rq_zland, rq_sems[1], t).start(), nz, z)
    rq_zland[z] = rq_z[...]

    lax.fori_loop(0, 4, outputs_owner, 0)

    acc[...] = jnp.zeros_like(acc)
    for t in range(1, nz):
        @pl.when(t > z)
        def _():
            z_arrival(s_total, s_far, s_sems[1], t).wait_recv()
            acc[...] += s_far[t]

    running = acc[...]
    for s in reversed(range(group)):
        s_out[s] = running
        running = running + s_land[s]
    others(lambda s: scatter(s_out, s_back, s_sems[2], s).start())
    s_back[me] = s_out[me]

    others(lambda t: z_arrival(rq_z, rq_zland, rq_sems[1], t).wait_recv(), nz, z)
    rq_x[...] = sum(rq_zland[t] for t in range(1, nz)) + rq_zland[0]
    others(lambda t: x_copy(rq_x, rq_xland, rq_sems[2], t).start(), nx, x)
    rq_xland[x] = rq_x[...]

    lax.fori_loop(4, 6, outputs_owner, 0)

    def key_slice(o):
        pieces = []
        back = s_back[o]
        for i in range(own):
            h = o * own + i
            far_norm = jnp.concatenate([norm_of(back[own * 8 :], i)] * tiles, 1)
            grad = folded(dot_nt(stacked(back[i * 8 : (i + 1) * 8]), v_rows[h, own_rows, :]))
            grad = (grad + far_norm) * slope_k[h, :, TILE:]
            pieces.append(gk_local[h] + folded(dot_nn(stacked(grad), k_rows[h, own_rows, :])))
        return jnp.concatenate(pieces, 0)

    by_owner(
        key_slice, rk_send, rk_land, rk_sems[0],
        lambda o: arrival(s_out, s_back, s_sems[2], o).wait_recv(),
    )

    others(lambda t: x_arrival(rq_x, rq_xland, rq_sems[2], t).wait_recv(), nx, x)
    rq_sum[...] = sum(rq_xland[t] for t in range(1, nx)) + rq_xland[0]
    others(lambda s: share(rq_sum, gq_hbm, rq_sems[3], s).start())
    own_gq = pltpu.make_async_copy(rq_sum, gq_hbm.at[me], store_sem.at[tiles])
    own_gq.start()

    lax.fori_loop(6, group, outputs_owner, 0)

    def by_position(b, _):
        block = o_rows[:, pl.ds(b * BLOCK, BLOCK), :]
        o_raw[pl.ds(b * BLOCK, BLOCK)] = jnp.swapaxes(block, 0, 1)
        return 0

    stores = []

    def store(t):
        blocks = TILE // BLOCK
        lax.fori_loop(t * blocks, (t + 1) * blocks, by_position, 0, unroll=4)
        rows = pl.ds(t * TILE, TILE)
        stores.append(pltpu.make_async_copy(o_raw.at[rows], out_hbm.at[rows], store_sem.at[t]))
        stores[-1].start()

    store(0)

    others(lambda s: arrival(rk_send, rk_land, rk_sems[0], s).wait_recv())
    rk_z[...] = sum(rk_land[s] for s in range(1, group)) + rk_land[0]
    others(lambda t: z_copy(rk_z, rk_zland, rk_sems[1], t).start(), nz, z)
    rk_zland[z] = rk_z[...]
    for t in range(1, tiles):
        store(t)
    others(lambda t: z_arrival(rk_z, rk_zland, rk_sems[1], t).wait_recv(), nz, z)
    rk_x[...] = sum(rk_zland[t] for t in range(1, nz)) + rk_zland[0]
    others(lambda t: x_copy(rk_x, rk_xland, rk_sems[2], t).start(), nx, x)
    rk_xland[x] = rk_x[...]
    others(lambda t: x_arrival(rk_x, rk_xland, rk_sems[2], t).wait_recv(), nx, x)
    rk_sum[...] = sum(rk_xland[t] for t in range(1, nx)) + rk_xland[0]
    others(lambda s: share(rk_sum, gk_hbm, rk_sems[3], s).start())
    own_gk = pltpu.make_async_copy(rk_sum, gk_hbm.at[me], store_sem.at[tiles + 1])
    own_gk.start()

    for copy in halo_copies:
        copy.wait_send()
    others(lambda s: scatter(p_send, p_land, p_sems[0], s).wait_send())
    others(lambda s: scatter(p_out, p_back, p_sems[2], s).wait_send())
    others(lambda s: scatter(s_send, s_land, s_sems[0], s).wait_send())
    others(lambda s: scatter(s_out, s_back, s_sems[2], s).wait_send())
    for t in range(nz):
        @pl.when(t > z)
        def _():
            z_copy(p_total, p_far, p_sems[1], t).wait_send()

        @pl.when(t < z)
        def _():
            z_copy(s_total, s_far, s_sems[1], t).wait_send()
    for send, land, zs, zland, xs, xland, total, grad, sems in (
        (rq_send, rq_land, rq_z, rq_zland, rq_x, rq_xland, rq_sum, gq_hbm, rq_sems),
        (rk_send, rk_land, rk_z, rk_zland, rk_x, rk_xland, rk_sum, gk_hbm, rk_sems),
    ):
        others(lambda s: scatter(send, land, sems[0], s).wait_send())
        others(lambda t: z_copy(zs, zland, sems[1], t).wait_send(), nz, z)
        others(lambda t: x_copy(xs, xland, sems[2], t).wait_send(), nx, x)
        others(lambda s: share(total, grad, sems[3], s).wait_send())
        others(lambda s: share_arrival(total, grad, sems[3], s).wait_recv())
    for copy in (*stores, own_gq, own_gk):
        copy.wait()


def finish(rows_hbm, gq_hbm, gk_hbm, out_hbm, gq_out, gk_out, rows, gq, gk, sems):
    parts = rows.shape[0] // TILE
    moves = [(gq_hbm, gq, gq_out), (gk_hbm, gk, gk_out)]
    for t in range(parts):
        span = pl.ds(t * TILE, TILE)
        moves.append((rows_hbm.at[span], rows.at[span], out_hbm.at[span]))
    ins = [pltpu.make_async_copy(a, b, sems.at[0, n]) for n, (a, b, _) in enumerate(moves)]
    outs = [pltpu.make_async_copy(b, c, sems.at[1, n]) for n, (_, b, c) in enumerate(moves)]
    for copy in ins:
        copy.start()
    for arrived, copy in zip(ins, outs):
        arrived.wait()
        copy.start()
    for copy in outs:
        copy.wait()


def body(queries, keys, values, keep_count, query_map, key_map, cotangent):
    _, tokens, heads, width = queries.shape
    rank = query_map.shape[2]
    tiles = tokens // TILE
    sizes = tuple(lax.axis_size(a) for a in (Z_AXIS, Y_AXIS, C_AXIS, X_AXIS))
    nz, ny, nc, nx = sizes
    group = ny * nc
    own = heads // group
    ext = tokens + TILE
    part = (own * rank, width)
    slab = (own * rank + 8, width)
    dma = pltpu.SemaphoreType.DMA

    def vmem(shape, dtype=F32):
        return pltpu.VMEM(shape, dtype)

    def sums():
        return [
            vmem((group, *part)), vmem((group, *part)), vmem(part), vmem((nz, *part)),
            vmem(part), vmem((nx, *part)), vmem(part),
        ]

    def scans():
        return [
            vmem((group, *slab)), vmem((group, *slab)), vmem(slab), vmem((nz, *slab)),
            vmem((group, *slab)), vmem((group, *slab)),
        ]

    raw = (tokens, heads, width)
    lane_rows = (heads, rank, tokens)
    small = [vmem((heads, nz * group * tiles), jnp.int32), *[vmem((heads, rank, width), BF16)] * 2]
    scratch = [
        *small, vmem(raw, BF16),
        *[vmem(raw, BF16)] * 4, vmem((2, TILE, heads, width), BF16),
        vmem((heads, tokens, width), BF16), vmem((heads, ext, width), BF16),
        vmem((heads, ext, width), BF16), vmem((heads, tokens, width), BF16),
        vmem((heads, tokens, width), BF16), vmem((heads, tiles, 2 * TILE, TILE), BF16),
        vmem(lane_rows), vmem(lane_rows), vmem((heads, rank, ext)), vmem((heads, rank, ext)),
        vmem((heads, 8, ext)), vmem((tiles + 1, heads, 8, TILE), jnp.int32),
        vmem((heads, tiles, rank, width)), vmem(lane_rows), vmem(lane_rows),
        vmem((heads, 8, tokens)), vmem((heads, 1, tokens)), vmem(lane_rows), vmem(lane_rows),
        vmem((heads, tiles, rank, width)), vmem((heads, tiles, rank, width)),
        vmem((heads, rank, width)),
        *scans(), *scans(), *sums(), *sums(), vmem(slab),
        dma((4 * tiles + 3,)), dma((tiles + 2,)), dma((2, len(HALO_PIECES))),
        [dma((2 * group,)), dma((2 * nz,)), dma((2 * group,))],
        [dma((2 * group,)), dma((2 * nz,)), dma((2 * group,))],
        [dma((2 * group,)), dma((2 * nz,)), dma((2 * nx,)), dma((2 * group,))],
        [dma((2 * group,)), dma((2 * nz,)), dma((2 * nx,)), dma((2 * group,))],
    ]
    anywhere = pl.BlockSpec(memory_space=pl.ANY)
    grad = jax.ShapeDtypeStruct((group, *part), F32)
    rows, grad_q, grad_k = pl.pallas_call(
        functools.partial(kernel, sizes),
        out_shape=(jax.ShapeDtypeStruct(raw, BF16), grad, grad),
        in_specs=[anywhere] * 7,
        out_specs=(anywhere,) * 3,
        scratch_shapes=scratch,
        compiler_params=pltpu.CompilerParams(
            collective_id=0, has_side_effects=True, vmem_limit_bytes=60 * 2**20
        ),
        name="less_step",
    )(
        queries[0], keys[0], values[0], cotangent[0], keep_count[0],
        query_map.transpose(0, 2, 1), key_map.transpose(0, 2, 1),
    )

    out, grad_q, grad_k = pl.pallas_call(
        finish,
        out_shape=(jax.ShapeDtypeStruct(raw, BF16), grad, grad),
        in_specs=[anywhere] * 3,
        out_specs=(anywhere,) * 3,
        scratch_shapes=[
            vmem(raw, BF16), vmem((group, *part)), vmem((group, *part)), dma((2, tiles + 2)),
        ],
        name="finish",
    )(rows, grad_q, grad_k)

    def map_grad(g):
        return g.reshape(heads, rank, width).transpose(0, 2, 1)

    return (out[None], map_grad(grad_q), map_grad(grad_k))


def solution(mesh):
    chips, last = mesh.shape["seq"], mesh.shape["batch"]
    torus = Mesh(mesh.devices.reshape(chips // 8, 4, 2, last), (*SEQ, X_AXIS))
    rows = P(X_AXIS, SEQ, None, None)
    return jax.shard_map(
        body,
        mesh=torus,
        in_specs=(rows, rows, rows, P(X_AXIS, None, None), P(), P(), rows),
        out_specs=(rows, P(), P()),
        check_vma=False,
    )
```

```python
import functools
import math

import jax
import jax.numpy as jnp
from jax import lax
from jax.experimental import pallas as pl
from jax.experimental.pallas import tpu as pltpu
from jax.sharding import Mesh
from jax.sharding import PartitionSpec as P

TILE = 128
SHIFT = 1.5
LOG2E = math.log2(math.e)
Z_AXIS, Y_AXIS, C_AXIS, X_AXIS = "seq_0", "seq_1", "seq_2", "batch"
SEQ = (Z_AXIS, Y_AXIS, C_AXIS)
F32, BF16 = jnp.float32, jnp.bfloat16
BLOCK = 16
HALO_PIECES = ((0, 0, 64), (0, 64, 64), (1, 0, 128))


def dot_nn(a, b):
    return lax.dot_general(a, b, (((1,), (0,)), ((), ())), preferred_element_type=F32)


def dot_nt(a, b):
    return lax.dot_general(a, b, (((1,), (1,)), ((), ())), preferred_element_type=F32)


def dot_tn(a, b):
    return lax.dot_general(a, b, (((0,), (0,)), ((), ())), preferred_element_type=F32)


def halves(x):
    high = x.astype(BF16).astype(F32)
    return high, x - high


def stacked(x):
    return jnp.concatenate(halves(x), 0).astype(BF16)


def folded(x):
    half = x.shape[0] // 2
    return x[:half] + x[half:]


def feature(pre):
    small = jnp.exp(-jnp.abs(pre))
    inverse = 1.0 / (1.0 + small)
    return jnp.maximum(pre, 0.0) + jnp.log1p(small), jnp.where(pre >= 0.0, inverse, small * inverse)


def remote(source, target, send, receive, device):
    return pltpu.make_async_remote_copy(
        src_ref=source,
        dst_ref=target,
        send_sem=send,
        recv_sem=receive,
        device_id=device,
        device_id_type=pl.DeviceIdType.MESH,
    )


def kernel(
    sizes,
    q_hbm, k_hbm, v_hbm, c_hbm, count_hbm, wq_hbm, wk_hbm,
    out_hbm, gq_hbm, gk_hbm,
    count_ref, wq_ref, wk_ref, o_raw,
    q_raw, k_raw, v_raw, c_raw, halo_raw,
    q_rows, k_rows, v_rows, c_rows, o_rows, weight_rows,
    feat_q, slope_q, feat_k, slope_k, kept_lane, count_lane,
    state_local, norm_local, u_local, row_data, inverse_rows, g_rows, gpre_q, d_state, d_norm, gk_local, far_rows,
    p_send, p_land, p_total, p_far, p_out, p_back,
    s_send, s_land, s_total, s_far, s_out, s_back,
    rq_send, rq_land, rq_z, rq_zland, rq_x, rq_xland, rq_sum,
    rk_send, rk_land, rk_z, rk_zland, rk_x, rk_xland, rk_sum,
    acc,
    load_sem, store_sem, halo_sems, p_sems, s_sems, rq_sems, rk_sems,
):
    nz, ny, nc, nx = sizes
    group = ny * nc
    devices = nz * group
    tokens, heads, width = q_raw.shape
    tiles = tokens // TILE
    own = heads // group
    lanes = lax.broadcasted_iota(jnp.int32, (8, TILE), 1)
    z, y, c, x = (lax.axis_index(a) for a in (Z_AXIS, Y_AXIS, C_AXIS, X_AXIS))
    me = y * nc + c
    index = z * group + me

    def peer(s):
        return {Y_AXIS: s // nc, C_AXIS: s % nc}

    def place(i):
        return {Z_AXIS: i // group, Y_AXIS: (i // nc) % ny, C_AXIS: i % nc}

    after = place((index + 1) % devices)
    before = place((index + devices - 1) % devices)

    barrier = pltpu.get_barrier_semaphore()

    def greet(device):
        pl.semaphore_signal(barrier, inc=1, device_id=device, device_id_type=pl.DeviceIdType.MESH)

    greet(after)
    greet(before)
    for k in range(1, group):
        greet(peer((me + k) % group))
    for k in range(1, nz):
        greet({Z_AXIS: (z + k) % nz})
    for k in range(1, nx):
        greet({X_AXIS: (x + k) % nx})

    sources = (k_hbm, v_hbm, c_hbm, q_hbm)
    raws = (k_raw, v_raw, c_raw, q_raw)

    def load(a, t):
        rows = pl.ds(t * TILE, TILE)
        return pltpu.make_async_copy(sources[a].at[rows], raws[a].at[rows], load_sem.at[a * tiles + t])

    small = [
        pltpu.make_async_copy(source, target, load_sem.at[4 * tiles + n])
        for n, (source, target) in enumerate(
            ((wk_hbm, wk_ref), (count_hbm, count_ref), (wq_hbm, wq_ref))
        )
    ]
    for a in range(4):
        for t in range(tiles):
            load(a, t).start()
        if a == 0:
            for copy in small:
                copy.start()

    def by_head(raw, rows, first, target, count):
        def step(b, _):
            block = raw[pl.ds(rows + b * BLOCK, BLOCK)]
            target[:, pl.ds(first + b * BLOCK, BLOCK), :] = jnp.swapaxes(block, 0, 1)
            return 0

        lax.fori_loop(0, count // BLOCK, step, 0, unroll=4)

    for t in range(tiles):
        load(0, t).wait()
        by_head(k_raw, t * TILE, (t + 1) * TILE, k_rows, TILE)
    pl.semaphore_wait(barrier, 2 + group - 1 + nz - 1 + nx - 1)
    halo_copies = []
    for n, (a, first, count) in enumerate(HALO_PIECES):
        source = (k_hbm, v_hbm)[a].at[pl.ds(tokens - TILE + first, count)]
        target = halo_raw.at[a, pl.ds(first, count)]
        halo_copies.append(remote(source, target, halo_sems.at[0, n], halo_sems.at[1, n], after))
    halo_copies[0].start()
    small[0].wait()

    def key_features(h, _):
        feat, slope = feature(dot_nt(wk_ref[h], k_rows[h, pl.ds(TILE, tokens), :]) - SHIFT)
        feat_k[h, :, TILE:] = feat
        slope_k[h, :, TILE:] = slope
        return 0

    lax.fori_loop(0, heads, key_features, 0, unroll=4)
    for t in range(tiles):
        load(1, t).wait()
        by_head(v_raw, t * TILE, (t + 1) * TILE, v_rows, TILE)

    for copy in small[1:]:
        copy.wait()
    counts = count_ref[...]
    which = lax.broadcasted_iota(jnp.int32, counts.shape, 1)
    lane16 = lax.broadcasted_iota(jnp.int32, (heads, TILE), 1)
    for e in range(tiles + 1):
        picked = jnp.sum(jnp.where(which == index * tiles + (e - 1), counts, 0), 1, keepdims=True)
        spread = jnp.broadcast_to(picked, (heads, TILE))
        kept = (lane16 < spread).astype(F32)
        for h in range(heads):
            count_lane[e, h] = jnp.broadcast_to(spread[h : h + 1], (8, TILE))
            kept_lane[h, :, e * TILE : (e + 1) * TILE] = jnp.broadcast_to(kept[h : h + 1], (8, TILE))

    def scatter(buffer, land, sems, s):
        return remote(buffer.at[s], land.at[me], sems.at[s], sems.at[group + me], peer(s))

    def arrival(buffer, land, sems, s):
        return remote(buffer.at[s], land.at[s], sems.at[s], sems.at[group + s], peer(s))

    def share(buffer, land, sems, s):
        return remote(buffer, land.at[me], sems.at[s], sems.at[group + me], peer(s))

    def share_arrival(buffer, land, sems, s):
        return remote(buffer, land.at[s], sems.at[s], sems.at[group + s], peer(s))

    def z_copy(buffer, land, sems, t):
        return remote(buffer, land.at[z], sems.at[t], sems.at[nz + z], {Z_AXIS: t})

    def z_arrival(buffer, land, sems, t):
        return remote(buffer, land.at[t], sems.at[t], sems.at[nz + t], {Z_AXIS: t})

    def x_copy(buffer, land, sems, t):
        return remote(buffer, land.at[x], sems.at[t], sems.at[nx + x], {X_AXIS: t})

    def x_arrival(buffer, land, sems, t):
        return remote(buffer, land.at[t], sems.at[t], sems.at[nx + t], {X_AXIS: t})

    def others(step, count=group, here=None):
        here = me if here is None else here
        for k in sorted(range(1, count), key=lambda k: -min(k, count - k)):
            step((here + k) % count)

    def nearer(k, steps):
        found = []
        for n in range(steps):
            n = k * steps + n
            found += [(me + group // 2 - n) % group, (me + group // 2 + 1 + n) % group]
        return found

    def by_owner(compute, buffer, land, sems, steps=1):
        def one(k, _):
            pair = nearer(k, steps)
            slices = [compute(o) for o in pair]
            for o, piece in zip(pair, slices):
                buffer[o] = piece
            for o in pair:
                @pl.when(o != me)
                def _():
                    scatter(buffer, land, sems, o).start()
            return 0

        lax.fori_loop(0, group // 2 // steps, one, 0)
        land[me] = buffer[me]

    def owner_slice(pieces, norms):
        low = jnp.where(lanes < TILE // 2, norms[0], norms[1])
        return jnp.concatenate([*pieces, low], 0)

    def norm_of(tile, i):
        turned = pltpu.roll(tile, TILE // 2, 1)
        return jnp.where(lanes < TILE // 2, *((tile, turned) if i == 0 else (turned, tile)))

    own_rows = pl.ds(TILE, tokens)

    def each_head(step):
        def one(h, _):
            step(h)
            return 0

        lax.fori_loop(0, heads, one, 0, unroll=4)

    def each_owner(step, ready):
        def one(k, _):
            pair = nearer(k, 1)
            for o in pair:
                pl.when(o != me)(functools.partial(ready, o))
            for o in pair:
                for i in range(own):
                    step(o, i)
            return 0

        lax.fori_loop(0, group // 2, one, 0)

    def state_slice(o):
        pieces, norms = [], []
        for i in range(own):
            h = o * own + i
            feat = feat_k[h, :, TILE:]
            pieces.append(folded(dot_nn(stacked(feat), v_rows[h, own_rows, :])))
            norms.append(jnp.sum(feat, 1, keepdims=True))
        return owner_slice(pieces, norms)

    by_owner(state_slice, p_send, p_land, p_sems[0])
    for copy in halo_copies[1:]:
        copy.start()

    def query_features(h, _):
        feat, slope = feature(dot_nt(wq_ref[h], q_rows[h]) - SHIFT)
        feat_q[h] = feat
        slope_q[h] = slope
        return 0

    for t in range(tiles):
        load(2, t).wait()
        by_head(c_raw, t * TILE, t * TILE, c_rows, TILE)
        load(3, t).wait()
        by_head(q_raw, t * TILE, t * TILE, q_rows, TILE)
    lax.fori_loop(0, heads, query_features, 0, unroll=4)

    def keep_state(h, j, state, norm):
        state_local[h, j] = state
        norm_local[h, :, j * TILE : (j + 1) * TILE] = jnp.broadcast_to(norm, (8, TILE))

    def local_products(h, j):
        cols = slice(j * TILE, (j + 1) * TILE)
        u = folded(dot_nt(stacked(state_local[h, j]), c_rows[h, cols, :]))
        u_local[h, :, cols] = u
        fq = feat_q[h, :, cols]
        row_data[h, 3:4, cols] = jnp.sum(fq * norm_local[h, :, cols], 0, keepdims=True)
        row_data[h, 4:5, cols] = jnp.sum(fq * u, 0, keepdims=True)

    def local_states(h, _):
        span = slice(TILE, tiles * TILE)
        feat = feat_k[h, :, span]
        gone = feat * (1.0 - kept_lane[h, :, span])
        lines, norms = [], []
        for j in range(1, tiles):
            cut = (j - 1) * TILE
            pieces = [feat[:, :cut]] * (cut > 0) + [gone[:, cut : cut + TILE]]
            pieces += [jnp.zeros((8, (tiles - 1 - j) * TILE), F32)] * (j < tiles - 1)
            line = jnp.concatenate(pieces, 1)
            lines += halves(line)
            blocks = [line[:, i * TILE : (i + 1) * TILE] for i in range(j)]
            norms.append(jnp.sum(sum(blocks[1:], blocks[0]), 1, keepdims=True))
        result = dot_nn(jnp.concatenate(lines, 0).astype(BF16), v_rows[h, span, :])
        for j in range(1, tiles):
            keep_state(h, j, folded(result[(j - 1) * 16 : j * 16]), norms[j - 1])
        return 0

    scale2 = LOG2E / math.sqrt(width)
    key_at = lax.broadcasted_iota(jnp.int32, (TILE, TILE), 0)
    causal = key_at <= lax.broadcasted_iota(jnp.int32, (TILE, TILE), 1)

    def sparse(h, j):
        cols = slice(j * TILE, (j + 1) * TILE)
        window = slice(j * TILE, (j + 2) * TILE)
        v_window = v_rows[h, window, :]
        scores = dot_nt(k_rows[h, window, :], q_rows[h, cols, :])
        live = key_at < count_lane[j, h, 0:1, :]
        near = jnp.where(live, scores[:TILE], -1e30)
        here = jnp.where(causal, scores[TILE:], -1e30)
        top = jnp.maximum(jnp.max(near, 0, keepdims=True), jnp.max(here, 0, keepdims=True))
        shift = top * scale2
        masked = jnp.concatenate([near, here], 0)
        weights = jnp.exp2(masked * scale2 - shift)
        rounded = weights.astype(BF16)
        weight_rows[h, j] = rounded
        along = dot_nt(v_window, c_rows[h, cols, :])
        row_data[h, 0:1, cols] = jnp.exp2(-shift)
        row_data[h, 1:2, cols] = jnp.sum(weights, 0, keepdims=True)
        row_data[h, 2:3, cols] = jnp.sum(rounded.astype(F32) * along, 0, keepdims=True)

    def sparse_tile(j):
        def one(h, _):
            sparse(h, j)
            return 0

        lax.fori_loop(0, heads, one, 0, unroll=4)

    others(lambda s: arrival(p_send, p_land, p_sems[0], s).wait_recv())
    p_total[...] = sum(p_land[s] for s in range(1, group)) + p_land[0]
    for t in range(1, nz):
        @pl.when(t > z)
        def _():
            z_copy(p_total, p_far, p_sems[1], t).start()

    lax.fori_loop(0, heads, local_states, 0, unroll=4)
    each_head(lambda h: [local_products(h, j) for j in range(1, tiles)])
    sparse_tile(1)
    sparse_tile(2)

    acc[...] = jnp.zeros_like(acc)
    for t in range(nz - 1):
        @pl.when(t < z)
        def _():
            z_arrival(p_total, p_far, p_sems[1], t).wait_recv()
            acc[...] += p_far[t]

    running = acc[...]
    for s in range(group):
        p_out[s] = running
        running = running + p_land[s]
    others(lambda s: scatter(p_out, p_back, p_sems[2], s).start())
    p_back[me] = p_out[me]

    sparse_tile(3)

    for copy in halo_copies:
        copy.wait_recv()
    by_head(halo_raw.at[0], 0, 0, k_rows, TILE)
    by_head(halo_raw.at[1], 0, 0, v_rows, TILE)

    def halo_features(h):
        feat, slope = feature(dot_nt(wk_ref[h], k_rows[h, :TILE, :]) - SHIFT)
        slope_k[h, :, :TILE] = slope
        feat_k[h, :, :TILE] = feat * kept_lane[h, :, :TILE]

    def halo_state(h):
        held = feat_k[h, :, :TILE]
        state = folded(dot_nn(stacked(held), v_rows[h, :TILE, :]))
        keep_state(h, 0, -state, -jnp.sum(held, 1, keepdims=True))

    each_head(halo_features)
    each_head(halo_state)
    each_head(lambda h: local_products(h, 0))
    sparse_tile(0)

    def d_slice(o):
        pieces, norms = [], []
        back = p_back[o]
        for i in range(own):
            h = o * own + i
            far_norm = jnp.concatenate([norm_of(back[own * 8 :], i)] * tiles, 1)
            fq = feat_q[h]
            u_far = far_rows[h]
            decay = row_data[h, 0:1, :]
            kd = row_data[h, 3:4, :] + jnp.sum(fq * far_norm, 0, keepdims=True)
            cu = row_data[h, 4:5, :] + jnp.sum(fq * u_far, 0, keepdims=True)
            inverse = 1.0 / (row_data[h, 1:2, :] + decay * kd)
            share_of = decay * inverse
            g = fq * share_of
            g_den = -share_of * ((row_data[h, 2:3, :] + decay * cu) * inverse)
            g_rows[h] = g
            inverse_rows[h] = inverse
            gpre_q[h] = (
                share_of * (u_local[h] + u_far) + g_den * (norm_local[h] + far_norm)
            ) * slope_q[h]
            weighted = fq * g_den
            total, total_norm = None, None
            for j in range(tiles):
                cols = slice(j * TILE, (j + 1) * TILE)
                piece = folded(dot_nn(stacked(g[:, cols]), c_rows[h, cols, :]))
                norm = jnp.sum(weighted[:, cols], 1, keepdims=True)
                d_state[h, j] = piece
                d_norm[h, j] = jnp.broadcast_to(norm, (8, TILE))
                total = piece if j == 0 else total + piece
                total_norm = norm if j == 0 else total_norm + norm
            pieces.append(total)
            norms.append(total_norm)
        return owner_slice(pieces, norms)

    def far_products(o, i):
        far = p_back[o, i * 8 : (i + 1) * 8]
        far_rows[o * own + i] = folded(dot_nt(stacked(far), c_rows[o * own + i]))

    each_owner(far_products, lambda o: arrival(p_out, p_back, p_sems[2], o).wait_recv())
    by_owner(d_slice, s_send, s_land, s_sems[0], 2)

    def query_slice(o):
        pieces = []
        for i in range(own):
            h = o * own + i
            pieces.append(folded(dot_nn(stacked(gpre_q[h]), q_rows[h])))
        return jnp.concatenate(pieces, 0)

    by_owner(query_slice, rq_send, rq_land, rq_sems[0])

    def key_local(h):
        parts = []
        for e in range(tiles):
            cols = slice(e * TILE, (e + 1) * TILE)
            v_tile = v_rows[h, cols, :]
            kept = kept_lane[h, :, cols]
            if e == 0:
                grad = -kept * (folded(dot_nt(stacked(d_state[h, 0]), v_tile)) + d_norm[h, 0])
            else:
                near, near_norm = d_state[h, e], d_norm[h, e]
                if e + 1 < tiles:
                    full = sum([d_state[h, j] for j in range(e + 2, tiles)], d_state[h, e + 1])
                    full_norm = sum([d_norm[h, j] for j in range(e + 2, tiles)], d_norm[h, e + 1])
                    both = jnp.concatenate([*halves(near), *halves(full)], 0).astype(BF16)
                    result = dot_nt(both, v_tile)
                    grad = (1.0 - kept) * (folded(result[:16]) + near_norm)
                    grad = grad + (folded(result[16:]) + full_norm)
                else:
                    grad = (1.0 - kept) * (folded(dot_nt(stacked(near), v_tile)) + near_norm)
            parts.append(grad * slope_k[h, :, cols])
        far_rows[h] = jnp.concatenate(parts, 1)

    def key_gradient(h):
        gk_local[h] = folded(dot_nn(stacked(far_rows[h]), k_rows[h, :tokens, :]))

    sub = lax.broadcasted_iota(jnp.int32, (8, TILE), 0)

    def outputs(h, o, i):
        back = p_back[o]
        far = back[i * 8 : (i + 1) * 8]
        for j in range(tiles):
            cols = slice(j * TILE, (j + 1) * TILE)
            high, low = halves(far + state_local[h, j])
            g_high, g_low = halves(g_rows[h, :, cols])
            first, rest = halves(inverse_rows[h, :, cols])
            second, third = halves(rest)
            inverse = jnp.where(sub == 0, first, jnp.where(sub == 1, second, third))
            inverse = jnp.where(sub < 3, inverse, 0.0)
            left = jnp.concatenate([g_high, g_low, g_high, inverse], 0).astype(BF16)
            zeros, ones = jnp.zeros((8, TILE), F32), jnp.ones((8, TILE), F32)
            right = jnp.concatenate(
                [
                    jnp.concatenate([high, high, low, zeros], 0),
                    jnp.concatenate([zeros, zeros, zeros, ones], 0),
                ],
                1,
            ).astype(BF16)
            both = dot_tn(left, right)
            window = slice(j * TILE, (j + 2) * TILE)
            numer = dot_tn(weight_rows[h, j], v_rows[h, window, :])
            result = numer * both[:, TILE:] + both[:, :TILE]
            o_rows[h, cols, :] = result.astype(BF16)

    def outputs_owner(o, _):
        for i in range(own):
            outputs(o * own + i, o, i)
        return 0

    each_head(key_local)
    each_head(key_gradient)

    others(lambda s: arrival(s_send, s_land, s_sems[0], s).wait_recv())
    s_total[...] = sum(s_land[s] for s in range(1, group)) + s_land[0]
    for t in range(nz - 1):
        @pl.when(t < z)
        def _():
            z_copy(s_total, s_far, s_sems[1], t).start()

    others(lambda s: arrival(rq_send, rq_land, rq_sems[0], s).wait_recv())
    rq_z[...] = sum(rq_land[s] for s in range(1, group)) + rq_land[0]
    others(lambda t: z_copy(rq_z, rq_zland, rq_sems[1], t).start(), nz, z)
    rq_zland[z] = rq_z[...]

    lax.fori_loop(0, 4, outputs_owner, 0)

    acc[...] = jnp.zeros_like(acc)
    for t in range(1, nz):
        @pl.when(t > z)
        def _():
            z_arrival(s_total, s_far, s_sems[1], t).wait_recv()
            acc[...] += s_far[t]

    running = acc[...]
    for s in reversed(range(group)):
        s_out[s] = running
        running = running + s_land[s]
    others(lambda s: scatter(s_out, s_back, s_sems[2], s).start())
    s_back[me] = s_out[me]

    others(lambda t: z_arrival(rq_z, rq_zland, rq_sems[1], t).wait_recv(), nz, z)
    rq_x[...] = sum(rq_zland[t] for t in range(1, nz)) + rq_zland[0]
    others(lambda t: x_copy(rq_x, rq_xland, rq_sems[2], t).start(), nx, x)
    rq_xland[x] = rq_x[...]

    lax.fori_loop(4, 6, outputs_owner, 0)

    def key_products(o, i):
        h = o * own + i
        back = s_back[o]
        far_norm = jnp.concatenate([norm_of(back[own * 8 :], i)] * tiles, 1)
        grad = folded(dot_nt(stacked(back[i * 8 : (i + 1) * 8]), v_rows[h, own_rows, :]))
        far_rows[h] = (grad + far_norm) * slope_k[h, :, TILE:]

    def key_slice(o):
        pieces = []
        for i in range(own):
            h = o * own + i
            pieces.append(gk_local[h] + folded(dot_nn(stacked(far_rows[h]), k_rows[h, own_rows, :])))
        return jnp.concatenate(pieces, 0)

    each_owner(key_products, lambda o: arrival(s_out, s_back, s_sems[2], o).wait_recv())
    by_owner(key_slice, rk_send, rk_land, rk_sems[0])

    others(lambda t: x_arrival(rq_x, rq_xland, rq_sems[2], t).wait_recv(), nx, x)
    rq_sum[...] = sum(rq_xland[t] for t in range(1, nx)) + rq_xland[0]
    others(lambda s: share(rq_sum, gq_hbm, rq_sems[3], s).start())
    own_gq = pltpu.make_async_copy(rq_sum, gq_hbm.at[me], store_sem.at[tiles])
    own_gq.start()

    lax.fori_loop(6, group, outputs_owner, 0)

    def by_position(b, _):
        block = o_rows[:, pl.ds(b * BLOCK, BLOCK), :]
        o_raw[pl.ds(b * BLOCK, BLOCK)] = jnp.swapaxes(block, 0, 1)
        return 0

    stores = []

    def store(t):
        blocks = TILE // BLOCK
        lax.fori_loop(t * blocks, (t + 1) * blocks, by_position, 0, unroll=4)
        rows = pl.ds(t * TILE, TILE)
        stores.append(pltpu.make_async_copy(o_raw.at[rows], out_hbm.at[rows], store_sem.at[t]))
        stores[-1].start()

    store(0)

    others(lambda s: arrival(rk_send, rk_land, rk_sems[0], s).wait_recv())
    rk_z[...] = sum(rk_land[s] for s in range(1, group)) + rk_land[0]
    others(lambda t: z_copy(rk_z, rk_zland, rk_sems[1], t).start(), nz, z)
    rk_zland[z] = rk_z[...]
    for t in range(1, tiles):
        store(t)
    others(lambda t: z_arrival(rk_z, rk_zland, rk_sems[1], t).wait_recv(), nz, z)
    rk_x[...] = sum(rk_zland[t] for t in range(1, nz)) + rk_zland[0]
    others(lambda t: x_copy(rk_x, rk_xland, rk_sems[2], t).start(), nx, x)
    rk_xland[x] = rk_x[...]
    others(lambda t: x_arrival(rk_x, rk_xland, rk_sems[2], t).wait_recv(), nx, x)
    rk_sum[...] = sum(rk_xland[t] for t in range(1, nx)) + rk_xland[0]
    others(lambda s: share(rk_sum, gk_hbm, rk_sems[3], s).start())
    own_gk = pltpu.make_async_copy(rk_sum, gk_hbm.at[me], store_sem.at[tiles + 1])
    own_gk.start()

    for copy in halo_copies:
        copy.wait_send()
    others(lambda s: scatter(p_send, p_land, p_sems[0], s).wait_send())
    others(lambda s: scatter(p_out, p_back, p_sems[2], s).wait_send())
    others(lambda s: scatter(s_send, s_land, s_sems[0], s).wait_send())
    others(lambda s: scatter(s_out, s_back, s_sems[2], s).wait_send())
    for t in range(nz):
        @pl.when(t > z)
        def _():
            z_copy(p_total, p_far, p_sems[1], t).wait_send()

        @pl.when(t < z)
        def _():
            z_copy(s_total, s_far, s_sems[1], t).wait_send()
    for send, land, zs, zland, xs, xland, total, grad, sems in (
        (rq_send, rq_land, rq_z, rq_zland, rq_x, rq_xland, rq_sum, gq_hbm, rq_sems),
        (rk_send, rk_land, rk_z, rk_zland, rk_x, rk_xland, rk_sum, gk_hbm, rk_sems),
    ):
        others(lambda s: scatter(send, land, sems[0], s).wait_send())
        others(lambda t: z_copy(zs, zland, sems[1], t).wait_send(), nz, z)
        others(lambda t: x_copy(xs, xland, sems[2], t).wait_send(), nx, x)
        others(lambda s: share(total, grad, sems[3], s).wait_send())
        others(lambda s: share_arrival(total, grad, sems[3], s).wait_recv())
    for copy in (*stores, own_gq, own_gk):
        copy.wait()


def finish(rows_hbm, gq_hbm, gk_hbm, out_hbm, gq_out, gk_out, rows, gq, gk, sems):
    parts = rows.shape[0] // TILE
    moves = [(gq_hbm, gq, gq_out), (gk_hbm, gk, gk_out)]
    for t in range(parts):
        span = pl.ds(t * TILE, TILE)
        moves.append((rows_hbm.at[span], rows.at[span], out_hbm.at[span]))
    ins = [pltpu.make_async_copy(a, b, sems.at[0, n]) for n, (a, b, _) in enumerate(moves)]
    outs = [pltpu.make_async_copy(b, c, sems.at[1, n]) for n, (_, b, c) in enumerate(moves)]
    for copy in ins:
        copy.start()
    for arrived, copy in zip(ins, outs):
        arrived.wait()
        copy.start()
    for copy in outs:
        copy.wait()


def body(queries, keys, values, keep_count, query_map, key_map, cotangent):
    _, tokens, heads, width = queries.shape
    rank = query_map.shape[2]
    tiles = tokens // TILE
    sizes = tuple(lax.axis_size(a) for a in (Z_AXIS, Y_AXIS, C_AXIS, X_AXIS))
    nz, ny, nc, nx = sizes
    group = ny * nc
    own = heads // group
    ext = tokens + TILE
    part = (own * rank, width)
    slab = (own * rank + 8, width)
    dma = pltpu.SemaphoreType.DMA

    def vmem(shape, dtype=F32):
        return pltpu.VMEM(shape, dtype)

    def sums():
        return [
            vmem((group, *part)), vmem((group, *part)), vmem(part), vmem((nz, *part)),
            vmem(part), vmem((nx, *part)), vmem(part),
        ]

    def scans():
        return [
            vmem((group, *slab)), vmem((group, *slab)), vmem(slab), vmem((nz, *slab)),
            vmem((group, *slab)), vmem((group, *slab)),
        ]

    raw = (tokens, heads, width)
    lane_rows = (heads, rank, tokens)
    small = [vmem((heads, nz * group * tiles), jnp.int32), *[vmem((heads, rank, width), BF16)] * 2]
    scratch = [
        *small, vmem(raw, BF16),
        *[vmem(raw, BF16)] * 4, vmem((2, TILE, heads, width), BF16),
        vmem((heads, tokens, width), BF16), vmem((heads, ext, width), BF16),
        vmem((heads, ext, width), BF16), vmem((heads, tokens, width), BF16),
        vmem((heads, tokens, width), BF16), vmem((heads, tiles, 2 * TILE, TILE), BF16),
        vmem(lane_rows), vmem(lane_rows), vmem((heads, rank, ext)), vmem((heads, rank, ext)),
        vmem((heads, 8, ext)), vmem((tiles + 1, heads, 8, TILE), jnp.int32),
        vmem((heads, tiles, rank, width)), vmem(lane_rows), vmem(lane_rows),
        vmem((heads, 8, tokens)), vmem((heads, 1, tokens)), vmem(lane_rows), vmem(lane_rows),
        vmem((heads, tiles, rank, width)), vmem((heads, tiles, rank, width)),
        vmem((heads, rank, width)), vmem(lane_rows),
        *scans(), *scans(), *sums(), *sums(), vmem(slab),
        dma((4 * tiles + 3,)), dma((tiles + 2,)), dma((2, len(HALO_PIECES))),
        [dma((2 * group,)), dma((2 * nz,)), dma((2 * group,))],
        [dma((2 * group,)), dma((2 * nz,)), dma((2 * group,))],
        [dma((2 * group,)), dma((2 * nz,)), dma((2 * nx,)), dma((2 * group,))],
        [dma((2 * group,)), dma((2 * nz,)), dma((2 * nx,)), dma((2 * group,))],
    ]
    anywhere = pl.BlockSpec(memory_space=pl.ANY)
    grad = jax.ShapeDtypeStruct((group, *part), F32)
    rows, grad_q, grad_k = pl.pallas_call(
        functools.partial(kernel, sizes),
        out_shape=(jax.ShapeDtypeStruct(raw, BF16), grad, grad),
        in_specs=[anywhere] * 7,
        out_specs=(anywhere,) * 3,
        scratch_shapes=scratch,
        compiler_params=pltpu.CompilerParams(
            collective_id=0, has_side_effects=True, vmem_limit_bytes=60 * 2**20
        ),
        name="less_step",
    )(
        queries[0], keys[0], values[0], cotangent[0], keep_count[0],
        query_map.transpose(0, 2, 1), key_map.transpose(0, 2, 1),
    )

    out, grad_q, grad_k = pl.pallas_call(
        finish,
        out_shape=(jax.ShapeDtypeStruct(raw, BF16), grad, grad),
        in_specs=[anywhere] * 3,
        out_specs=(anywhere,) * 3,
        scratch_shapes=[
            vmem(raw, BF16), vmem((group, *part)), vmem((group, *part)), dma((2, tiles + 2)),
        ],
        name="finish",
    )(rows, grad_q, grad_k)

    def map_grad(g):
        return g.reshape(heads, rank, width).transpose(0, 2, 1)

    return (out[None], map_grad(grad_q), map_grad(grad_k))


def solution(mesh):
    chips, last = mesh.shape["seq"], mesh.shape["batch"]
    torus = Mesh(mesh.devices.reshape(chips // 8, 4, 2, last), (*SEQ, X_AXIS))
    rows = P(X_AXIS, SEQ, None, None)
    return jax.shard_map(
        body,
        mesh=torus,
        in_specs=(rows, rows, rows, P(X_AXIS, None, None), P(), P(), rows),
        out_specs=(rows, P(), P()),
        check_vma=False,
    )
```

```python
import functools
import math

import jax
import jax.numpy as jnp
from jax import lax
from jax.experimental import pallas as pl
from jax.experimental.pallas import tpu as pltpu
from jax.sharding import Mesh
from jax.sharding import PartitionSpec as P

TILE = 128
SHIFT = 1.5
LOG2E = math.log2(math.e)
Z_AXIS, Y_AXIS, C_AXIS, X_AXIS = "seq_0", "seq_1", "seq_2", "batch"
SEQ = (Z_AXIS, Y_AXIS, C_AXIS)
F32, BF16 = jnp.float32, jnp.bfloat16
BLOCK = 16
HALO_PIECES = ((0, 0, 64), (0, 64, 64), (1, 0, 128))


def dot_nn(a, b):
    return lax.dot_general(a, b, (((1,), (0,)), ((), ())), preferred_element_type=F32)


def dot_nt(a, b):
    return lax.dot_general(a, b, (((1,), (1,)), ((), ())), preferred_element_type=F32)


def dot_tn(a, b):
    return lax.dot_general(a, b, (((0,), (0,)), ((), ())), preferred_element_type=F32)


def halves(x):
    high = x.astype(BF16).astype(F32)
    return high, x - high


def stacked(x):
    return jnp.concatenate(halves(x), 0).astype(BF16)


def folded(x):
    half = x.shape[0] // 2
    return x[:half] + x[half:]


def feature(pre):
    small = jnp.exp(-jnp.abs(pre))
    inverse = 1.0 / (1.0 + small)
    return jnp.maximum(pre, 0.0) + jnp.log1p(small), jnp.where(pre >= 0.0, inverse, small * inverse)


def remote(source, target, send, receive, device):
    return pltpu.make_async_remote_copy(
        src_ref=source,
        dst_ref=target,
        send_sem=send,
        recv_sem=receive,
        device_id=device,
        device_id_type=pl.DeviceIdType.MESH,
    )


def kernel(
    sizes,
    q_hbm, k_hbm, v_hbm, c_hbm, count_hbm, wq_hbm, wk_hbm,
    out_hbm, gq_hbm, gk_hbm,
    count_ref, wq_ref, wk_ref, o_raw,
    q_raw, k_raw, v_raw, c_raw, halo_raw,
    q_rows, k_rows, v_rows, c_rows, o_rows, weight_rows,
    feat_q, slope_q, feat_k, slope_k, kept_lane, count_lane,
    state_local, norm_local, u_local, row_data, inverse_rows, g_rows, gpre_q, d_state, d_norm, gk_local, far_rows,
    p_send, p_land, p_total, p_far, p_out, p_back,
    s_send, s_land, s_total, s_far, s_out, s_back,
    rq_send, rq_land, rq_z, rq_zland, rq_x, rq_xland, rq_sum,
    rk_send, rk_land, rk_z, rk_zland, rk_x, rk_xland, rk_sum,
    acc,
    load_sem, store_sem, halo_sems, p_sems, s_sems, rq_sems, rk_sems,
):
    nz, ny, nc, nx = sizes
    group = ny * nc
    devices = nz * group
    tokens, heads, width = q_raw.shape
    tiles = tokens // TILE
    own = heads // group
    lanes = lax.broadcasted_iota(jnp.int32, (8, TILE), 1)
    z, y, c, x = (lax.axis_index(a) for a in (Z_AXIS, Y_AXIS, C_AXIS, X_AXIS))
    me = y * nc + c
    index = z * group + me

    def peer(s):
        return {Y_AXIS: s // nc, C_AXIS: s % nc}

    def place(i):
        return {Z_AXIS: i // group, Y_AXIS: (i // nc) % ny, C_AXIS: i % nc}

    after = place((index + 1) % devices)
    before = place((index + devices - 1) % devices)

    barrier = pltpu.get_barrier_semaphore()

    def greet(device):
        pl.semaphore_signal(barrier, inc=1, device_id=device, device_id_type=pl.DeviceIdType.MESH)

    greet(after)
    greet(before)
    for k in range(1, group):
        greet(peer((me + k) % group))
    for k in range(1, nz):
        greet({Z_AXIS: (z + k) % nz})
    for k in range(1, nx):
        greet({X_AXIS: (x + k) % nx})

    sources = (k_hbm, v_hbm, c_hbm, q_hbm)
    raws = (k_raw, v_raw, c_raw, q_raw)

    def load(a, t):
        rows = pl.ds(t * TILE, TILE)
        return pltpu.make_async_copy(sources[a].at[rows], raws[a].at[rows], load_sem.at[a * tiles + t])

    small = [
        pltpu.make_async_copy(source, target, load_sem.at[4 * tiles + n])
        for n, (source, target) in enumerate(
            ((wk_hbm, wk_ref), (count_hbm, count_ref), (wq_hbm, wq_ref))
        )
    ]
    for a in range(4):
        for t in range(tiles):
            load(a, t).start()
        if a == 0:
            for copy in small:
                copy.start()

    def by_head(raw, rows, first, target, count):
        def step(b, _):
            block = raw[pl.ds(rows + b * BLOCK, BLOCK)]
            target[:, pl.ds(first + b * BLOCK, BLOCK), :] = jnp.swapaxes(block, 0, 1)
            return 0

        lax.fori_loop(0, count // BLOCK, step, 0, unroll=4)

    for t in range(tiles):
        load(0, t).wait()
        by_head(k_raw, t * TILE, (t + 1) * TILE, k_rows, TILE)
    pl.semaphore_wait(barrier, 2 + group - 1 + nz - 1 + nx - 1)
    halo_copies = []
    for n, (a, first, count) in enumerate(HALO_PIECES):
        source = (k_hbm, v_hbm)[a].at[pl.ds(tokens - TILE + first, count)]
        target = halo_raw.at[a, pl.ds(first, count)]
        halo_copies.append(remote(source, target, halo_sems.at[0, n], halo_sems.at[1, n], after))
    halo_copies[0].start()
    small[0].wait()

    def key_features(h, _):
        feat, slope = feature(dot_nt(wk_ref[h], k_rows[h, pl.ds(TILE, tokens), :]) - SHIFT)
        feat_k[h, :, TILE:] = feat
        slope_k[h, :, TILE:] = slope
        return 0

    lax.fori_loop(0, heads, key_features, 0, unroll=8)
    for t in range(tiles):
        load(1, t).wait()
        by_head(v_raw, t * TILE, (t + 1) * TILE, v_rows, TILE)

    for copy in small[1:]:
        copy.wait()
    counts = count_ref[...]
    which = lax.broadcasted_iota(jnp.int32, counts.shape, 1)
    lane16 = lax.broadcasted_iota(jnp.int32, (heads, TILE), 1)
    for e in range(tiles + 1):
        picked = jnp.sum(jnp.where(which == index * tiles + (e - 1), counts, 0), 1, keepdims=True)
        spread = jnp.broadcast_to(picked, (heads, TILE))
        kept = (lane16 < spread).astype(F32)
        for h in range(heads):
            count_lane[e, h] = jnp.broadcast_to(spread[h : h + 1], (8, TILE))
            kept_lane[h, :, e * TILE : (e + 1) * TILE] = jnp.broadcast_to(kept[h : h + 1], (8, TILE))

    def scatter(buffer, land, sems, s):
        return remote(buffer.at[s], land.at[me], sems.at[s], sems.at[group + me], peer(s))

    def arrival(buffer, land, sems, s):
        return remote(buffer.at[s], land.at[s], sems.at[s], sems.at[group + s], peer(s))

    def share(buffer, land, sems, s):
        return remote(buffer, land.at[me], sems.at[s], sems.at[group + me], peer(s))

    def share_arrival(buffer, land, sems, s):
        return remote(buffer, land.at[s], sems.at[s], sems.at[group + s], peer(s))

    def z_copy(buffer, land, sems, t):
        return remote(buffer, land.at[z], sems.at[t], sems.at[nz + z], {Z_AXIS: t})

    def z_arrival(buffer, land, sems, t):
        return remote(buffer, land.at[t], sems.at[t], sems.at[nz + t], {Z_AXIS: t})

    def x_copy(buffer, land, sems, t):
        return remote(buffer, land.at[x], sems.at[t], sems.at[nx + x], {X_AXIS: t})

    def x_arrival(buffer, land, sems, t):
        return remote(buffer, land.at[t], sems.at[t], sems.at[nx + t], {X_AXIS: t})

    def others(step, count=group, here=None):
        here = me if here is None else here
        for k in sorted(range(1, count), key=lambda k: -min(k, count - k)):
            step((here + k) % count)

    def nearer(k, steps):
        found = []
        for n in range(steps):
            n = k * steps + n
            found += [(me + group // 2 - n) % group, (me + group // 2 + 1 + n) % group]
        return found

    def by_owner(compute, buffer, land, sems, steps=1):
        def one(k, _):
            pair = nearer(k, steps)
            slices = [compute(o) for o in pair]
            for o, piece in zip(pair, slices):
                buffer[o] = piece
            for o in pair:
                @pl.when(o != me)
                def _():
                    scatter(buffer, land, sems, o).start()
            return 0

        lax.fori_loop(0, group // 2 // steps, one, 0)
        land[me] = buffer[me]

    def owner_slice(pieces, norms):
        low = jnp.where(lanes < TILE // 2, norms[0], norms[1])
        return jnp.concatenate([*pieces, low], 0)

    def norm_of(tile, i):
        turned = pltpu.roll(tile, TILE // 2, 1)
        return jnp.where(lanes < TILE // 2, *((tile, turned) if i == 0 else (turned, tile)))

    own_rows = pl.ds(TILE, tokens)

    def each_head(step, unroll=4):
        def one(h, _):
            step(h)
            return 0

        lax.fori_loop(0, heads, one, 0, unroll=unroll)

    def each_owner(step, ready):
        def one(k, _):
            pair = nearer(k, 2)
            for o in pair:
                pl.when(o != me)(functools.partial(ready, o))
            for o in pair:
                for i in range(own):
                    step(o, i)
            return 0

        lax.fori_loop(0, group // 4, one, 0)

    def state_slice(o):
        pieces, norms = [], []
        for i in range(own):
            h = o * own + i
            feat = feat_k[h, :, TILE:]
            pieces.append(folded(dot_nn(stacked(feat), v_rows[h, own_rows, :])))
            norms.append(jnp.sum(feat, 1, keepdims=True))
        return owner_slice(pieces, norms)

    by_owner(state_slice, p_send, p_land, p_sems[0], 2)
    for copy in halo_copies[1:]:
        copy.start()

    def query_features(h, _):
        feat, slope = feature(dot_nt(wq_ref[h], q_rows[h]) - SHIFT)
        feat_q[h] = feat
        slope_q[h] = slope
        return 0

    for t in range(tiles):
        load(2, t).wait()
        by_head(c_raw, t * TILE, t * TILE, c_rows, TILE)
        load(3, t).wait()
        by_head(q_raw, t * TILE, t * TILE, q_rows, TILE)
    lax.fori_loop(0, heads, query_features, 0, unroll=8)

    def keep_state(h, j, state, norm):
        state_local[h, j] = state
        norm_local[h, :, j * TILE : (j + 1) * TILE] = jnp.broadcast_to(norm, (8, TILE))

    def local_products(h, j):
        cols = slice(j * TILE, (j + 1) * TILE)
        u = folded(dot_nt(stacked(state_local[h, j]), c_rows[h, cols, :]))
        u_local[h, :, cols] = u
        fq = feat_q[h, :, cols]
        row_data[h, 3:4, cols] = jnp.sum(fq * norm_local[h, :, cols], 0, keepdims=True)
        row_data[h, 4:5, cols] = jnp.sum(fq * u, 0, keepdims=True)

    def local_states(h, _):
        span = slice(TILE, tiles * TILE)
        feat = feat_k[h, :, span]
        gone = feat * (1.0 - kept_lane[h, :, span])
        lines, norms = [], []
        for j in range(1, tiles):
            cut = (j - 1) * TILE
            pieces = [feat[:, :cut]] * (cut > 0) + [gone[:, cut : cut + TILE]]
            pieces += [jnp.zeros((8, (tiles - 1 - j) * TILE), F32)] * (j < tiles - 1)
            line = jnp.concatenate(pieces, 1)
            lines += halves(line)
            blocks = [line[:, i * TILE : (i + 1) * TILE] for i in range(j)]
            norms.append(jnp.sum(sum(blocks[1:], blocks[0]), 1, keepdims=True))
        result = dot_nn(jnp.concatenate(lines, 0).astype(BF16), v_rows[h, span, :])
        for j in range(1, tiles):
            keep_state(h, j, folded(result[(j - 1) * 16 : j * 16]), norms[j - 1])
        return 0

    scale2 = LOG2E / math.sqrt(width)
    key_at = lax.broadcasted_iota(jnp.int32, (TILE, TILE), 0)
    causal = key_at <= lax.broadcasted_iota(jnp.int32, (TILE, TILE), 1)

    def weigh(h, j):
        cols = slice(j * TILE, (j + 1) * TILE)
        scores = dot_nt(k_rows[h, j * TILE : (j + 2) * TILE, :], q_rows[h, cols, :])
        live = key_at < count_lane[j, h, 0:1, :]
        near = jnp.where(live, scores[:TILE], -1e30)
        here = jnp.where(causal, scores[TILE:], -1e30)
        top = jnp.maximum(jnp.max(near, 0, keepdims=True), jnp.max(here, 0, keepdims=True))
        shift = top * scale2
        weights = jnp.exp2(jnp.concatenate([near, here], 0) * scale2 - shift)
        rounded = weights.astype(BF16)
        weight_rows[h, j] = rounded
        row_data[h, 0:1, cols] = jnp.exp2(-shift)
        row_data[h, 1:2, cols] = jnp.sum(weights, 0, keepdims=True)
        return rounded

    def along(h, j, rounded):
        cols = slice(j * TILE, (j + 1) * TILE)
        product = dot_nt(v_rows[h, j * TILE : (j + 2) * TILE, :], c_rows[h, cols, :])
        row_data[h, 2:3, cols] = jnp.sum(rounded.astype(F32) * product, 0, keepdims=True)

    def sparse(h, j):
        along(h, j, weigh(h, j))

    def sparse_tile(j):
        def one(h, _):
            sparse(h, j)
            return 0

        lax.fori_loop(0, heads, one, 0, unroll=4)

    others(lambda s: arrival(p_send, p_land, p_sems[0], s).wait_recv())
    p_total[...] = sum(p_land[s] for s in range(1, group)) + p_land[0]
    for t in range(1, nz):
        @pl.when(t > z)
        def _():
            z_copy(p_total, p_far, p_sems[1], t).start()

    lax.fori_loop(0, heads, local_states, 0, unroll=8)
    each_head(lambda h: [local_products(h, j) for j in range(1, tiles)], 8)
    sparse_tile(1)
    sparse_tile(2)

    acc[...] = jnp.zeros_like(acc)
    for t in range(nz - 1):
        @pl.when(t < z)
        def _():
            z_arrival(p_total, p_far, p_sems[1], t).wait_recv()
            acc[...] += p_far[t]

    running = acc[...]
    for s in range(group):
        p_out[s] = running
        running = running + p_land[s]
    others(lambda s: scatter(p_out, p_back, p_sems[2], s).start())
    p_back[me] = p_out[me]

    sparse_tile(3)

    def halo_features(h):
        feat, slope = feature(dot_nt(wk_ref[h], k_rows[h, :TILE, :]) - SHIFT)
        slope_k[h, :, :TILE] = slope
        feat_k[h, :, :TILE] = feat * kept_lane[h, :, :TILE]

    def halo_state(h):
        held = feat_k[h, :, :TILE]
        state = folded(dot_nn(stacked(held), v_rows[h, :TILE, :]))
        keep_state(h, 0, -state, -jnp.sum(held, 1, keepdims=True))

    def halo_along(h):
        local_products(h, 0)
        along(h, 0, weight_rows[h, 0])

    for copy, (a, _, _) in zip(halo_copies, HALO_PIECES):
        if a == 0:
            copy.wait_recv()
    by_head(halo_raw.at[0], 0, 0, k_rows, TILE)
    each_head(halo_features, 8)
    each_head(lambda h: weigh(h, 0))
    for copy, (a, _, _) in zip(halo_copies, HALO_PIECES):
        if a == 1:
            copy.wait_recv()
    by_head(halo_raw.at[1], 0, 0, v_rows, TILE)
    each_head(halo_state, 16)
    each_head(halo_along, 8)

    def d_slice(o):
        pieces, norms = [], []
        back = p_back[o]
        for i in range(own):
            h = o * own + i
            far_norm = jnp.concatenate([norm_of(back[own * 8 :], i)] * tiles, 1)
            fq = feat_q[h]
            u_far = far_rows[h]
            decay = row_data[h, 0:1, :]
            kd = row_data[h, 3:4, :] + jnp.sum(fq * far_norm, 0, keepdims=True)
            cu = row_data[h, 4:5, :] + jnp.sum(fq * u_far, 0, keepdims=True)
            inverse = 1.0 / (row_data[h, 1:2, :] + decay * kd)
            share_of = decay * inverse
            g = fq * share_of
            g_den = -share_of * ((row_data[h, 2:3, :] + decay * cu) * inverse)
            g_rows[h] = g
            inverse_rows[h] = inverse
            gpre_q[h] = (
                share_of * (u_local[h] + u_far) + g_den * (norm_local[h] + far_norm)
            ) * slope_q[h]
            weighted = fq * g_den
            total, total_norm = None, None
            for j in range(tiles):
                cols = slice(j * TILE, (j + 1) * TILE)
                piece = folded(dot_nn(stacked(g[:, cols]), c_rows[h, cols, :]))
                norm = jnp.sum(weighted[:, cols], 1, keepdims=True)
                d_state[h, j] = piece
                d_norm[h, j] = jnp.broadcast_to(norm, (8, TILE))
                total = piece if j == 0 else total + piece
                total_norm = norm if j == 0 else total_norm + norm
            pieces.append(total)
            norms.append(total_norm)
        return owner_slice(pieces, norms)

    def far_products(o, i):
        far = p_back[o, i * 8 : (i + 1) * 8]
        far_rows[o * own + i] = folded(dot_nt(stacked(far), c_rows[o * own + i]))

    each_owner(far_products, lambda o: arrival(p_out, p_back, p_sems[2], o).wait_recv())
    by_owner(d_slice, s_send, s_land, s_sems[0], 2)

    def query_slice(o):
        pieces = []
        for i in range(own):
            h = o * own + i
            pieces.append(folded(dot_nn(stacked(gpre_q[h]), q_rows[h])))
        return jnp.concatenate(pieces, 0)

    by_owner(query_slice, rq_send, rq_land, rq_sems[0], 2)

    def key_local(h):
        parts = []
        for e in range(tiles):
            cols = slice(e * TILE, (e + 1) * TILE)
            v_tile = v_rows[h, cols, :]
            kept = kept_lane[h, :, cols]
            if e == 0:
                grad = -kept * (folded(dot_nt(stacked(d_state[h, 0]), v_tile)) + d_norm[h, 0])
            else:
                near, near_norm = d_state[h, e], d_norm[h, e]
                if e + 1 < tiles:
                    full = sum([d_state[h, j] for j in range(e + 2, tiles)], d_state[h, e + 1])
                    full_norm = sum([d_norm[h, j] for j in range(e + 2, tiles)], d_norm[h, e + 1])
                    both = jnp.concatenate([*halves(near), *halves(full)], 0).astype(BF16)
                    result = dot_nt(both, v_tile)
                    grad = (1.0 - kept) * (folded(result[:16]) + near_norm)
                    grad = grad + (folded(result[16:]) + full_norm)
                else:
                    grad = (1.0 - kept) * (folded(dot_nt(stacked(near), v_tile)) + near_norm)
            parts.append(grad * slope_k[h, :, cols])
        far_rows[h] = jnp.concatenate(parts, 1)

    def key_gradient(h):
        gk_local[h] = folded(dot_nn(stacked(far_rows[h]), k_rows[h, :tokens, :]))

    sub = lax.broadcasted_iota(jnp.int32, (8, TILE), 0)

    def outputs(h, o, i):
        back = p_back[o]
        far = back[i * 8 : (i + 1) * 8]
        for j in range(tiles):
            cols = slice(j * TILE, (j + 1) * TILE)
            high, low = halves(far + state_local[h, j])
            g_high, g_low = halves(g_rows[h, :, cols])
            first, rest = halves(inverse_rows[h, :, cols])
            second, third = halves(rest)
            inverse = jnp.where(sub == 0, first, jnp.where(sub == 1, second, third))
            inverse = jnp.where(sub < 3, inverse, 0.0)
            left = jnp.concatenate([g_high, g_low, g_high, inverse], 0).astype(BF16)
            zeros, ones = jnp.zeros((8, TILE), F32), jnp.ones((8, TILE), F32)
            right = jnp.concatenate(
                [
                    jnp.concatenate([high, high, low, zeros], 0),
                    jnp.concatenate([zeros, zeros, zeros, ones], 0),
                ],
                1,
            ).astype(BF16)
            both = dot_tn(left, right)
            window = slice(j * TILE, (j + 2) * TILE)
            numer = dot_tn(weight_rows[h, j], v_rows[h, window, :])
            result = numer * both[:, TILE:] + both[:, :TILE]
            o_rows[h, cols, :] = result.astype(BF16)

    def outputs_owner(o, _):
        for i in range(own):
            outputs(o * own + i, o, i)
        return 0

    each_head(key_local, 8)
    each_head(key_gradient, 8)

    others(lambda s: arrival(s_send, s_land, s_sems[0], s).wait_recv())
    s_total[...] = sum(s_land[s] for s in range(1, group)) + s_land[0]
    for t in range(nz - 1):
        @pl.when(t < z)
        def _():
            z_copy(s_total, s_far, s_sems[1], t).start()

    others(lambda s: arrival(rq_send, rq_land, rq_sems[0], s).wait_recv())
    rq_z[...] = sum(rq_land[s] for s in range(1, group)) + rq_land[0]
    others(lambda t: z_copy(rq_z, rq_zland, rq_sems[1], t).start(), nz, z)
    rq_zland[z] = rq_z[...]

    lax.fori_loop(0, 4, outputs_owner, 0)

    acc[...] = jnp.zeros_like(acc)
    for t in range(1, nz):
        @pl.when(t > z)
        def _():
            z_arrival(s_total, s_far, s_sems[1], t).wait_recv()
            acc[...] += s_far[t]

    running = acc[...]
    for s in reversed(range(group)):
        s_out[s] = running
        running = running + s_land[s]
    others(lambda s: scatter(s_out, s_back, s_sems[2], s).start())
    s_back[me] = s_out[me]

    others(lambda t: z_arrival(rq_z, rq_zland, rq_sems[1], t).wait_recv(), nz, z)
    rq_x[...] = sum(rq_zland[t] for t in range(1, nz)) + rq_zland[0]
    others(lambda t: x_copy(rq_x, rq_xland, rq_sems[2], t).start(), nx, x)
    rq_xland[x] = rq_x[...]

    lax.fori_loop(4, 6, outputs_owner, 0)

    def key_products(o, i):
        h = o * own + i
        back = s_back[o]
        far_norm = jnp.concatenate([norm_of(back[own * 8 :], i)] * tiles, 1)
        grad = folded(dot_nt(stacked(back[i * 8 : (i + 1) * 8]), v_rows[h, own_rows, :]))
        far_rows[h] = (grad + far_norm) * slope_k[h, :, TILE:]

    def key_slice(o):
        pieces = []
        for i in range(own):
            h = o * own + i
            pieces.append(gk_local[h] + folded(dot_nn(stacked(far_rows[h]), k_rows[h, own_rows, :])))
        return jnp.concatenate(pieces, 0)

    each_owner(key_products, lambda o: arrival(s_out, s_back, s_sems[2], o).wait_recv())
    by_owner(key_slice, rk_send, rk_land, rk_sems[0], 2)

    others(lambda t: x_arrival(rq_x, rq_xland, rq_sems[2], t).wait_recv(), nx, x)
    rq_sum[...] = sum(rq_xland[t] for t in range(1, nx)) + rq_xland[0]
    others(lambda s: share(rq_sum, gq_hbm, rq_sems[3], s).start())
    own_gq = pltpu.make_async_copy(rq_sum, gq_hbm.at[me], store_sem.at[tiles])
    own_gq.start()

    lax.fori_loop(6, group, outputs_owner, 0)

    def by_position(b, _):
        block = o_rows[:, pl.ds(b * BLOCK, BLOCK), :]
        o_raw[pl.ds(b * BLOCK, BLOCK)] = jnp.swapaxes(block, 0, 1)
        return 0

    stores = []

    def store(t):
        blocks = TILE // BLOCK
        lax.fori_loop(t * blocks, (t + 1) * blocks, by_position, 0, unroll=4)
        rows = pl.ds(t * TILE, TILE)
        stores.append(pltpu.make_async_copy(o_raw.at[rows], out_hbm.at[rows], store_sem.at[t]))
        stores[-1].start()

    store(0)

    others(lambda s: arrival(rk_send, rk_land, rk_sems[0], s).wait_recv())
    rk_z[...] = sum(rk_land[s] for s in range(1, group)) + rk_land[0]
    others(lambda t: z_copy(rk_z, rk_zland, rk_sems[1], t).start(), nz, z)
    rk_zland[z] = rk_z[...]
    for t in range(1, tiles):
        store(t)
    others(lambda t: z_arrival(rk_z, rk_zland, rk_sems[1], t).wait_recv(), nz, z)
    rk_x[...] = sum(rk_zland[t] for t in range(1, nz)) + rk_zland[0]
    others(lambda t: x_copy(rk_x, rk_xland, rk_sems[2], t).start(), nx, x)
    rk_xland[x] = rk_x[...]
    others(lambda t: x_arrival(rk_x, rk_xland, rk_sems[2], t).wait_recv(), nx, x)
    rk_sum[...] = sum(rk_xland[t] for t in range(1, nx)) + rk_xland[0]
    others(lambda s: share(rk_sum, gk_hbm, rk_sems[3], s).start())
    own_gk = pltpu.make_async_copy(rk_sum, gk_hbm.at[me], store_sem.at[tiles + 1])
    own_gk.start()

    for copy in halo_copies:
        copy.wait_send()
    others(lambda s: scatter(p_send, p_land, p_sems[0], s).wait_send())
    others(lambda s: scatter(p_out, p_back, p_sems[2], s).wait_send())
    others(lambda s: scatter(s_send, s_land, s_sems[0], s).wait_send())
    others(lambda s: scatter(s_out, s_back, s_sems[2], s).wait_send())
    for t in range(nz):
        @pl.when(t > z)
        def _():
            z_copy(p_total, p_far, p_sems[1], t).wait_send()

        @pl.when(t < z)
        def _():
            z_copy(s_total, s_far, s_sems[1], t).wait_send()
    for send, land, zs, zland, xs, xland, total, grad, sems in (
        (rq_send, rq_land, rq_z, rq_zland, rq_x, rq_xland, rq_sum, gq_hbm, rq_sems),
        (rk_send, rk_land, rk_z, rk_zland, rk_x, rk_xland, rk_sum, gk_hbm, rk_sems),
    ):
        others(lambda s: scatter(send, land, sems[0], s).wait_send())
        others(lambda t: z_copy(zs, zland, sems[1], t).wait_send(), nz, z)
        others(lambda t: x_copy(xs, xland, sems[2], t).wait_send(), nx, x)
        others(lambda s: share(total, grad, sems[3], s).wait_send())
        others(lambda s: share_arrival(total, grad, sems[3], s).wait_recv())
    for copy in (*stores, own_gq, own_gk):
        copy.wait()


def finish(rows_hbm, gq_hbm, gk_hbm, out_hbm, gq_out, gk_out, rows, gq, gk, sems):
    parts = rows.shape[0] // TILE
    moves = [(gq_hbm, gq, gq_out), (gk_hbm, gk, gk_out)]
    for t in range(parts):
        span = pl.ds(t * TILE, TILE)
        moves.append((rows_hbm.at[span], rows.at[span], out_hbm.at[span]))
    ins = [pltpu.make_async_copy(a, b, sems.at[0, n]) for n, (a, b, _) in enumerate(moves)]
    outs = [pltpu.make_async_copy(b, c, sems.at[1, n]) for n, (_, b, c) in enumerate(moves)]
    for copy in ins:
        copy.start()
    for arrived, copy in zip(ins, outs):
        arrived.wait()
        copy.start()
    for copy in outs:
        copy.wait()


def body(queries, keys, values, keep_count, query_map, key_map, cotangent):
    _, tokens, heads, width = queries.shape
    rank = query_map.shape[2]
    tiles = tokens // TILE
    sizes = tuple(lax.axis_size(a) for a in (Z_AXIS, Y_AXIS, C_AXIS, X_AXIS))
    nz, ny, nc, nx = sizes
    group = ny * nc
    own = heads // group
    ext = tokens + TILE
    part = (own * rank, width)
    slab = (own * rank + 8, width)
    dma = pltpu.SemaphoreType.DMA

    def vmem(shape, dtype=F32):
        return pltpu.VMEM(shape, dtype)

    def sums():
        return [
            vmem((group, *part)), vmem((group, *part)), vmem(part), vmem((nz, *part)),
            vmem(part), vmem((nx, *part)), vmem(part),
        ]

    def scans():
        return [
            vmem((group, *slab)), vmem((group, *slab)), vmem(slab), vmem((nz, *slab)),
            vmem((group, *slab)), vmem((group, *slab)),
        ]

    raw = (tokens, heads, width)
    lane_rows = (heads, rank, tokens)
    small = [vmem((heads, nz * group * tiles), jnp.int32), *[vmem((heads, rank, width), BF16)] * 2]
    scratch = [
        *small, vmem(raw, BF16),
        *[vmem(raw, BF16)] * 4, vmem((2, TILE, heads, width), BF16),
        vmem((heads, tokens, width), BF16), vmem((heads, ext, width), BF16),
        vmem((heads, ext, width), BF16), vmem((heads, tokens, width), BF16),
        vmem((heads, tokens, width), BF16), vmem((heads, tiles, 2 * TILE, TILE), BF16),
        vmem(lane_rows), vmem(lane_rows), vmem((heads, rank, ext)), vmem((heads, rank, ext)),
        vmem((heads, 8, ext)), vmem((tiles + 1, heads, 8, TILE), jnp.int32),
        vmem((heads, tiles, rank, width)), vmem(lane_rows), vmem(lane_rows),
        vmem((heads, 8, tokens)), vmem((heads, 1, tokens)), vmem(lane_rows), vmem(lane_rows),
        vmem((heads, tiles, rank, width)), vmem((heads, tiles, rank, width)),
        vmem((heads, rank, width)), vmem(lane_rows),
        *scans(), *scans(), *sums(), *sums(), vmem(slab),
        dma((4 * tiles + 3,)), dma((tiles + 2,)), dma((2, len(HALO_PIECES))),
        [dma((2 * group,)), dma((2 * nz,)), dma((2 * group,))],
        [dma((2 * group,)), dma((2 * nz,)), dma((2 * group,))],
        [dma((2 * group,)), dma((2 * nz,)), dma((2 * nx,)), dma((2 * group,))],
        [dma((2 * group,)), dma((2 * nz,)), dma((2 * nx,)), dma((2 * group,))],
    ]
    anywhere = pl.BlockSpec(memory_space=pl.ANY)
    grad = jax.ShapeDtypeStruct((group, *part), F32)
    rows, grad_q, grad_k = pl.pallas_call(
        functools.partial(kernel, sizes),
        out_shape=(jax.ShapeDtypeStruct(raw, BF16), grad, grad),
        in_specs=[anywhere] * 7,
        out_specs=(anywhere,) * 3,
        scratch_shapes=scratch,
        compiler_params=pltpu.CompilerParams(
            collective_id=0, has_side_effects=True, vmem_limit_bytes=60 * 2**20
        ),
        name="less_step",
    )(
        queries[0], keys[0], values[0], cotangent[0], keep_count[0],
        query_map.transpose(0, 2, 1), key_map.transpose(0, 2, 1),
    )

    out, grad_q, grad_k = pl.pallas_call(
        finish,
        out_shape=(jax.ShapeDtypeStruct(raw, BF16), grad, grad),
        in_specs=[anywhere] * 3,
        out_specs=(anywhere,) * 3,
        scratch_shapes=[
            vmem(raw, BF16), vmem((group, *part)), vmem((group, *part)), dma((2, tiles + 2)),
        ],
        name="finish",
    )(rows, grad_q, grad_k)

    def map_grad(g):
        return g.reshape(heads, rank, width).transpose(0, 2, 1)

    return (out[None], map_grad(grad_q), map_grad(grad_k))


def solution(mesh):
    chips, last = mesh.shape["seq"], mesh.shape["batch"]
    torus = Mesh(mesh.devices.reshape(chips // 8, 4, 2, last), (*SEQ, X_AXIS))
    rows = P(X_AXIS, SEQ, None, None)
    return jax.shard_map(
        body,
        mesh=torus,
        in_specs=(rows, rows, rows, P(X_AXIS, None, None), P(), P(), rows),
        out_specs=(rows, P(), P()),
        check_vma=False,
    )
```

```python
import functools
import math

import jax
import jax.numpy as jnp
from jax import lax
from jax.experimental import pallas as pl
from jax.experimental.pallas import tpu as pltpu
from jax.sharding import Mesh
from jax.sharding import PartitionSpec as P

TILE = 128
SHIFT = 1.5
LOG2E = math.log2(math.e)
Z_AXIS, Y_AXIS, C_AXIS, X_AXIS = "seq_0", "seq_1", "seq_2", "batch"
SEQ = (Z_AXIS, Y_AXIS, C_AXIS)
F32, BF16 = jnp.float32, jnp.bfloat16
BLOCK = 16
HALO_PIECES = ((0, 0, 64), (0, 64, 64), (1, 0, 128))


def dot_nn(a, b):
    return lax.dot_general(a, b, (((1,), (0,)), ((), ())), preferred_element_type=F32)


def dot_nt(a, b):
    return lax.dot_general(a, b, (((1,), (1,)), ((), ())), preferred_element_type=F32)


def dot_tn(a, b):
    return lax.dot_general(a, b, (((0,), (0,)), ((), ())), preferred_element_type=F32)


def halves(x):
    high = x.astype(BF16).astype(F32)
    return high, x - high


def stacked(x):
    return jnp.concatenate(halves(x), 0).astype(BF16)


def folded(x):
    half = x.shape[0] // 2
    return x[:half] + x[half:]


def feature(pre):
    small = jnp.exp(-jnp.abs(pre))
    inverse = 1.0 / (1.0 + small)
    return jnp.maximum(pre, 0.0) + jnp.log1p(small), jnp.where(pre >= 0.0, inverse, small * inverse)


def remote(source, target, send, receive, device):
    return pltpu.make_async_remote_copy(
        src_ref=source,
        dst_ref=target,
        send_sem=send,
        recv_sem=receive,
        device_id=device,
        device_id_type=pl.DeviceIdType.MESH,
    )


def kernel(
    sizes,
    q_hbm, k_hbm, v_hbm, c_hbm, count_hbm, wq_hbm, wk_hbm,
    out_hbm, gq_hbm, gk_hbm,
    count_ref, wq_ref, wk_ref, o_raw,
    q_raw, k_raw, v_raw, c_raw, halo_raw,
    q_rows, k_rows, v_rows, c_rows, o_rows, weight_rows,
    feat_q, slope_q, feat_k, slope_k, kept_lane, count_lane,
    state_local, norm_local, u_local, row_data, inverse_rows, g_rows, gpre_q, d_state, d_norm, gk_local, far_rows,
    p_send, p_land, p_total, p_far, p_out, p_back,
    s_send, s_land, s_total, s_far, s_out, s_back,
    rq_send, rq_land, rq_z, rq_zland, rq_x, rq_xland, rq_sum,
    rk_send, rk_land, rk_z, rk_zland, rk_x, rk_xland, rk_sum,
    acc,
    load_sem, store_sem, halo_sems, p_sems, s_sems, rq_sems, rk_sems,
):
    nz, ny, nc, nx = sizes
    group = ny * nc
    devices = nz * group
    tokens, heads, width = q_raw.shape
    tiles = tokens // TILE
    own = heads // group
    lanes = lax.broadcasted_iota(jnp.int32, (8, TILE), 1)
    z, y, c, x = (lax.axis_index(a) for a in (Z_AXIS, Y_AXIS, C_AXIS, X_AXIS))
    me = y * nc + c
    index = z * group + me

    def peer(s):
        return {Y_AXIS: s // nc, C_AXIS: s % nc}

    def place(i):
        return {Z_AXIS: i // group, Y_AXIS: (i // nc) % ny, C_AXIS: i % nc}

    after = place((index + 1) % devices)
    before = place((index + devices - 1) % devices)

    barrier = pltpu.get_barrier_semaphore()

    def greet(device):
        pl.semaphore_signal(barrier, inc=1, device_id=device, device_id_type=pl.DeviceIdType.MESH)

    greet(after)
    greet(before)
    for k in range(1, group):
        greet(peer((me + k) % group))
    for k in range(1, nz):
        greet({Z_AXIS: (z + k) % nz})
    for k in range(1, nx):
        greet({X_AXIS: (x + k) % nx})

    sources = (k_hbm, v_hbm, c_hbm, q_hbm)
    raws = (k_raw, v_raw, c_raw, q_raw)

    def load(a, t):
        rows = pl.ds(t * TILE, TILE)
        return pltpu.make_async_copy(sources[a].at[rows], raws[a].at[rows], load_sem.at[a * tiles + t])

    small = [
        pltpu.make_async_copy(source, target, load_sem.at[4 * tiles + n])
        for n, (source, target) in enumerate(
            ((wk_hbm, wk_ref), (count_hbm, count_ref), (wq_hbm, wq_ref))
        )
    ]
    for a in range(4):
        for t in range(tiles):
            load(a, t).start()
        if a == 0:
            for copy in small:
                copy.start()

    def by_head(raw, rows, first, target, count):
        def step(b, _):
            block = raw[pl.ds(rows + b * BLOCK, BLOCK)]
            target[:, pl.ds(first + b * BLOCK, BLOCK), :] = jnp.swapaxes(block, 0, 1)
            return 0

        lax.fori_loop(0, count // BLOCK, step, 0, unroll=4)

    for t in range(tiles):
        load(0, t).wait()
        by_head(k_raw, t * TILE, (t + 1) * TILE, k_rows, TILE)
    pl.semaphore_wait(barrier, 2 + group - 1 + nz - 1 + nx - 1)
    halo_copies = []
    for n, (a, first, count) in enumerate(HALO_PIECES):
        source = (k_raw, v_raw)[a].at[pl.ds(tokens - TILE + first, count)]
        target = halo_raw.at[a, pl.ds(first, count)]
        halo_copies.append(remote(source, target, halo_sems.at[0, n], halo_sems.at[1, n], after))
    halo_copies[0].start()
    small[0].wait()

    def key_features(h, _):
        feat, slope = feature(dot_nt(wk_ref[h], k_rows[h, pl.ds(TILE, tokens), :]) - SHIFT)
        feat_k[h, :, TILE:] = feat
        slope_k[h, :, TILE:] = slope
        return 0

    lax.fori_loop(0, heads, key_features, 0, unroll=8)
    for t in range(tiles):
        load(1, t).wait()
        by_head(v_raw, t * TILE, (t + 1) * TILE, v_rows, TILE)

    for copy in small[1:]:
        copy.wait()
    counts = count_ref[...]
    which = lax.broadcasted_iota(jnp.int32, counts.shape, 1)
    lane16 = lax.broadcasted_iota(jnp.int32, (heads, TILE), 1)
    for e in range(tiles + 1):
        picked = jnp.sum(jnp.where(which == index * tiles + (e - 1), counts, 0), 1, keepdims=True)
        spread = jnp.broadcast_to(picked, (heads, TILE))
        kept = (lane16 < spread).astype(F32)
        for h in range(heads):
            count_lane[e, h] = jnp.broadcast_to(spread[h : h + 1], (8, TILE))
            kept_lane[h, :, e * TILE : (e + 1) * TILE] = jnp.broadcast_to(kept[h : h + 1], (8, TILE))

    def scatter(buffer, land, sems, s):
        return remote(buffer.at[s], land.at[me], sems.at[s], sems.at[group + me], peer(s))

    def arrival(buffer, land, sems, s):
        return remote(buffer.at[s], land.at[s], sems.at[s], sems.at[group + s], peer(s))

    def share(buffer, land, sems, s):
        return remote(buffer, land.at[me], sems.at[s], sems.at[group + me], peer(s))

    def share_arrival(buffer, land, sems, s):
        return remote(buffer, land.at[s], sems.at[s], sems.at[group + s], peer(s))

    def z_copy(buffer, land, sems, t):
        return remote(buffer, land.at[z], sems.at[t], sems.at[nz + z], {Z_AXIS: t})

    def z_arrival(buffer, land, sems, t):
        return remote(buffer, land.at[t], sems.at[t], sems.at[nz + t], {Z_AXIS: t})

    def x_copy(buffer, land, sems, t):
        return remote(buffer, land.at[x], sems.at[t], sems.at[nx + x], {X_AXIS: t})

    def x_arrival(buffer, land, sems, t):
        return remote(buffer, land.at[t], sems.at[t], sems.at[nx + t], {X_AXIS: t})

    def others(step, count=group, here=None):
        here = me if here is None else here
        for k in sorted(range(1, count), key=lambda k: -min(k, count - k)):
            step((here + k) % count)

    def nearer(k, steps):
        found = []
        for n in range(steps):
            n = k * steps + n
            found += [(me + group // 2 - n) % group, (me + group // 2 + 1 + n) % group]
        return found

    def by_owner(compute, buffer, land, sems, steps=1):
        def one(k, _):
            pair = nearer(k, steps)
            slices = [compute(o) for o in pair]
            for o, piece in zip(pair, slices):
                buffer[o] = piece
            for o in pair:
                @pl.when(o != me)
                def _():
                    scatter(buffer, land, sems, o).start()
            return 0

        lax.fori_loop(0, group // 2 // steps, one, 0)
        land[me] = buffer[me]

    at_lane = [
        (lanes == lax.broadcasted_iota(jnp.int32, (8, TILE), 0) + 8 * i).astype(F32)
        for i in range(own)
    ]

    def owner_slice(pieces, norms):
        spread = sum(norms[i] * at_lane[i] for i in range(1, own)) + norms[0] * at_lane[0]
        return jnp.concatenate([*pieces, jnp.sum(spread, 0, keepdims=True)], 0)

    def norm_of(row, i):
        picked = jnp.sum(row * at_lane[i], 1, keepdims=True)
        return jnp.broadcast_to(picked, (8, TILE))

    own_rows = pl.ds(TILE, tokens)

    def each_head(step, unroll=4):
        def one(h, _):
            step(h)
            return 0

        lax.fori_loop(0, heads, one, 0, unroll=unroll)

    def each_owner(step, ready):
        def one(k, _):
            pair = nearer(k, 2)
            for o in pair:
                pl.when(o != me)(functools.partial(ready, o))
            for o in pair:
                for i in range(own):
                    step(o, i)
            return 0

        lax.fori_loop(0, group // 4, one, 0)

    def state_slice(o):
        pieces, norms = [], []
        for i in range(own):
            h = o * own + i
            feat = feat_k[h, :, TILE:]
            pieces.append(folded(dot_nn(stacked(feat), v_rows[h, own_rows, :])))
            norms.append(jnp.sum(feat, 1, keepdims=True))
        return owner_slice(pieces, norms)

    by_owner(state_slice, p_send, p_land, p_sems[0], 2)
    for copy in halo_copies[1:]:
        copy.start()

    def query_features(h, _):
        feat, slope = feature(dot_nt(wq_ref[h], q_rows[h]) - SHIFT)
        feat_q[h] = feat
        slope_q[h] = slope
        return 0

    for t in range(tiles):
        load(2, t).wait()
        by_head(c_raw, t * TILE, t * TILE, c_rows, TILE)
        load(3, t).wait()
        by_head(q_raw, t * TILE, t * TILE, q_rows, TILE)
    lax.fori_loop(0, heads, query_features, 0, unroll=8)

    def keep_state(h, j, state, norm):
        state_local[h, j] = state
        norm_local[h, :, j * TILE : (j + 1) * TILE] = jnp.broadcast_to(norm, (8, TILE))

    def local_products(h, j):
        cols = slice(j * TILE, (j + 1) * TILE)
        u = folded(dot_nt(stacked(state_local[h, j]), c_rows[h, cols, :]))
        u_local[h, :, cols] = u
        fq = feat_q[h, :, cols]
        row_data[h, 3:4, cols] = jnp.sum(fq * norm_local[h, :, cols], 0, keepdims=True)
        row_data[h, 4:5, cols] = jnp.sum(fq * u, 0, keepdims=True)

    def local_states(h, _):
        span = slice(TILE, tiles * TILE)
        feat = feat_k[h, :, span]
        gone = feat * (1.0 - kept_lane[h, :, span])
        lines, norms = [], []
        for j in range(1, tiles):
            cut = (j - 1) * TILE
            pieces = [feat[:, :cut]] * (cut > 0) + [gone[:, cut : cut + TILE]]
            pieces += [jnp.zeros((8, (tiles - 1 - j) * TILE), F32)] * (j < tiles - 1)
            line = jnp.concatenate(pieces, 1)
            lines += halves(line)
            blocks = [line[:, i * TILE : (i + 1) * TILE] for i in range(j)]
            norms.append(jnp.sum(sum(blocks[1:], blocks[0]), 1, keepdims=True))
        result = dot_nn(jnp.concatenate(lines, 0).astype(BF16), v_rows[h, span, :])
        for j in range(1, tiles):
            keep_state(h, j, folded(result[(j - 1) * 16 : j * 16]), norms[j - 1])
        return 0

    scale2 = LOG2E / math.sqrt(width)
    key_at = lax.broadcasted_iota(jnp.int32, (TILE, TILE), 0)
    causal = key_at <= lax.broadcasted_iota(jnp.int32, (TILE, TILE), 1)

    def weigh(h, j):
        cols = slice(j * TILE, (j + 1) * TILE)
        scores = dot_nt(k_rows[h, j * TILE : (j + 2) * TILE, :], q_rows[h, cols, :])
        live = key_at < count_lane[j, h, 0:1, :]
        near = jnp.where(live, scores[:TILE], -1e30)
        here = jnp.where(causal, scores[TILE:], -1e30)
        top = jnp.maximum(jnp.max(near, 0, keepdims=True), jnp.max(here, 0, keepdims=True))
        shift = top * scale2
        weights = jnp.exp2(jnp.concatenate([near, here], 0) * scale2 - shift)
        rounded = weights.astype(BF16)
        weight_rows[h, j] = rounded
        row_data[h, 0:1, cols] = jnp.exp2(-shift)
        row_data[h, 1:2, cols] = jnp.sum(weights, 0, keepdims=True)
        return rounded

    def along(h, j, rounded):
        cols = slice(j * TILE, (j + 1) * TILE)
        product = dot_nt(v_rows[h, j * TILE : (j + 2) * TILE, :], c_rows[h, cols, :])
        row_data[h, 2:3, cols] = jnp.sum(rounded.astype(F32) * product, 0, keepdims=True)

    def sparse(h, j):
        along(h, j, weigh(h, j))

    def sparse_tile(j):
        def one(h, _):
            sparse(h, j)
            return 0

        lax.fori_loop(0, heads, one, 0, unroll=4)

    others(lambda s: arrival(p_send, p_land, p_sems[0], s).wait_recv())
    p_total[...] = sum(p_land[s] for s in range(1, group)) + p_land[0]
    for t in range(1, nz):
        @pl.when(t > z)
        def _():
            z_copy(p_total, p_far, p_sems[1], t).start()

    lax.fori_loop(0, heads, local_states, 0, unroll=8)
    each_head(lambda h: [local_products(h, j) for j in range(1, tiles)], 8)
    sparse_tile(1)
    sparse_tile(2)

    acc[...] = jnp.zeros_like(acc)
    for t in range(nz - 1):
        @pl.when(t < z)
        def _():
            z_arrival(p_total, p_far, p_sems[1], t).wait_recv()
            acc[...] += p_far[t]

    running = acc[...]
    for s in range(group):
        p_out[s] = running
        running = running + p_land[s]
    others(lambda s: scatter(p_out, p_back, p_sems[2], s).start())
    p_back[me] = p_out[me]

    sparse_tile(3)

    def halo_features(h):
        feat, slope = feature(dot_nt(wk_ref[h], k_rows[h, :TILE, :]) - SHIFT)
        slope_k[h, :, :TILE] = slope
        feat_k[h, :, :TILE] = feat * kept_lane[h, :, :TILE]

    def halo_state(h):
        held = feat_k[h, :, :TILE]
        state = folded(dot_nn(stacked(held), v_rows[h, :TILE, :]))
        keep_state(h, 0, -state, -jnp.sum(held, 1, keepdims=True))

    def halo_along(h):
        local_products(h, 0)
        along(h, 0, weight_rows[h, 0])

    for copy, (a, _, _) in zip(halo_copies, HALO_PIECES):
        if a == 0:
            copy.wait_recv()
    by_head(halo_raw.at[0], 0, 0, k_rows, TILE)
    each_head(halo_features, 8)
    each_head(lambda h: weigh(h, 0))
    for copy, (a, _, _) in zip(halo_copies, HALO_PIECES):
        if a == 1:
            copy.wait_recv()
    by_head(halo_raw.at[1], 0, 0, v_rows, TILE)
    each_head(halo_state, 16)
    each_head(halo_along, 8)

    def d_slice(o):
        pieces, norms = [], []
        back = p_back[o]
        for i in range(own):
            h = o * own + i
            far_norm = jnp.concatenate([norm_of(back[own * 8 :], i)] * tiles, 1)
            fq = feat_q[h]
            u_far = far_rows[h]
            decay = row_data[h, 0:1, :]
            kd = row_data[h, 3:4, :] + jnp.sum(fq * far_norm, 0, keepdims=True)
            cu = row_data[h, 4:5, :] + jnp.sum(fq * u_far, 0, keepdims=True)
            inverse = 1.0 / (row_data[h, 1:2, :] + decay * kd)
            share_of = decay * inverse
            g = fq * share_of
            g_den = -share_of * ((row_data[h, 2:3, :] + decay * cu) * inverse)
            g_rows[h] = g
            inverse_rows[h] = inverse
            gpre_q[h] = (
                share_of * (u_local[h] + u_far) + g_den * (norm_local[h] + far_norm)
            ) * slope_q[h]
            weighted = fq * g_den
            total, total_norm = None, None
            for j in range(tiles):
                cols = slice(j * TILE, (j + 1) * TILE)
                piece = folded(dot_nn(stacked(g[:, cols]), c_rows[h, cols, :]))
                norm = jnp.sum(weighted[:, cols], 1, keepdims=True)
                d_state[h, j] = piece
                d_norm[h, j] = jnp.broadcast_to(norm, (8, TILE))
                total = piece if j == 0 else total + piece
                total_norm = norm if j == 0 else total_norm + norm
            pieces.append(total)
            norms.append(total_norm)
        return owner_slice(pieces, norms)

    def far_products(o, i):
        far = p_back[o, i * 8 : (i + 1) * 8]
        far_rows[o * own + i] = folded(dot_nt(stacked(far), c_rows[o * own + i]))

    each_owner(far_products, lambda o: arrival(p_out, p_back, p_sems[2], o).wait_recv())
    by_owner(d_slice, s_send, s_land, s_sems[0], 2)

    def query_slice(o):
        pieces = []
        for i in range(own):
            h = o * own + i
            pieces.append(folded(dot_nn(stacked(gpre_q[h]), q_rows[h])))
        return jnp.concatenate(pieces, 0)

    by_owner(query_slice, rq_send, rq_land, rq_sems[0], 2)

    def key_local(h):
        parts = []
        for e in range(tiles):
            cols = slice(e * TILE, (e + 1) * TILE)
            v_tile = v_rows[h, cols, :]
            kept = kept_lane[h, :, cols]
            if e == 0:
                grad = -kept * (folded(dot_nt(stacked(d_state[h, 0]), v_tile)) + d_norm[h, 0])
            else:
                near, near_norm = d_state[h, e], d_norm[h, e]
                if e + 1 < tiles:
                    full = sum([d_state[h, j] for j in range(e + 2, tiles)], d_state[h, e + 1])
                    full_norm = sum([d_norm[h, j] for j in range(e + 2, tiles)], d_norm[h, e + 1])
                    both = jnp.concatenate([*halves(near), *halves(full)], 0).astype(BF16)
                    result = dot_nt(both, v_tile)
                    grad = (1.0 - kept) * (folded(result[:16]) + near_norm)
                    grad = grad + (folded(result[16:]) + full_norm)
                else:
                    grad = (1.0 - kept) * (folded(dot_nt(stacked(near), v_tile)) + near_norm)
            parts.append(grad * slope_k[h, :, cols])
        far_rows[h] = jnp.concatenate(parts, 1)

    def key_gradient(h):
        gk_local[h] = folded(dot_nn(stacked(far_rows[h]), k_rows[h, :tokens, :]))

    sub = lax.broadcasted_iota(jnp.int32, (8, TILE), 0)

    def outputs(h, o, i):
        back = p_back[o]
        far = back[i * 8 : (i + 1) * 8]
        for j in range(tiles):
            cols = slice(j * TILE, (j + 1) * TILE)
            high, low = halves(far + state_local[h, j])
            g_high, g_low = halves(g_rows[h, :, cols])
            first, rest = halves(inverse_rows[h, :, cols])
            second, third = halves(rest)
            inverse = jnp.where(sub == 0, first, jnp.where(sub == 1, second, third))
            inverse = jnp.where(sub < 3, inverse, 0.0)
            left = jnp.concatenate([g_high, g_low, g_high, inverse], 0).astype(BF16)
            zeros, ones = jnp.zeros((8, TILE), F32), jnp.ones((8, TILE), F32)
            right = jnp.concatenate(
                [
                    jnp.concatenate([high, high, low, zeros], 0),
                    jnp.concatenate([zeros, zeros, zeros, ones], 0),
                ],
                1,
            ).astype(BF16)
            both = dot_tn(left, right)
            window = slice(j * TILE, (j + 2) * TILE)
            numer = dot_tn(weight_rows[h, j], v_rows[h, window, :])
            result = numer * both[:, TILE:] + both[:, :TILE]
            o_rows[h, cols, :] = result.astype(BF16)

    def outputs_owner(o, _):
        for i in range(own):
            outputs(o * own + i, o, i)
        return 0

    each_head(key_local, 8)
    each_head(key_gradient, 8)

    others(lambda s: arrival(s_send, s_land, s_sems[0], s).wait_recv())
    s_total[...] = sum(s_land[s] for s in range(1, group)) + s_land[0]
    for t in range(nz - 1):
        @pl.when(t < z)
        def _():
            z_copy(s_total, s_far, s_sems[1], t).start()

    others(lambda s: arrival(rq_send, rq_land, rq_sems[0], s).wait_recv())
    rq_z[...] = sum(rq_land[s] for s in range(1, group)) + rq_land[0]
    others(lambda t: z_copy(rq_z, rq_zland, rq_sems[1], t).start(), nz, z)
    rq_zland[z] = rq_z[...]

    lax.fori_loop(0, 4, outputs_owner, 0)

    acc[...] = jnp.zeros_like(acc)
    for t in range(1, nz):
        @pl.when(t > z)
        def _():
            z_arrival(s_total, s_far, s_sems[1], t).wait_recv()
            acc[...] += s_far[t]

    running = acc[...]
    for s in reversed(range(group)):
        s_out[s] = running
        running = running + s_land[s]
    others(lambda s: scatter(s_out, s_back, s_sems[2], s).start())
    s_back[me] = s_out[me]

    others(lambda t: z_arrival(rq_z, rq_zland, rq_sems[1], t).wait_recv(), nz, z)
    rq_x[...] = sum(rq_zland[t] for t in range(1, nz)) + rq_zland[0]
    others(lambda t: x_copy(rq_x, rq_xland, rq_sems[2], t).start(), nx, x)
    rq_xland[x] = rq_x[...]

    lax.fori_loop(4, 6, outputs_owner, 0)

    def key_products(o, i):
        h = o * own + i
        back = s_back[o]
        far_norm = jnp.concatenate([norm_of(back[own * 8 :], i)] * tiles, 1)
        grad = folded(dot_nt(stacked(back[i * 8 : (i + 1) * 8]), v_rows[h, own_rows, :]))
        far_rows[h] = (grad + far_norm) * slope_k[h, :, TILE:]

    def key_slice(o):
        pieces = []
        for i in range(own):
            h = o * own + i
            pieces.append(gk_local[h] + folded(dot_nn(stacked(far_rows[h]), k_rows[h, own_rows, :])))
        return jnp.concatenate(pieces, 0)

    each_owner(key_products, lambda o: arrival(s_out, s_back, s_sems[2], o).wait_recv())
    by_owner(key_slice, rk_send, rk_land, rk_sems[0], 2)

    others(lambda t: x_arrival(rq_x, rq_xland, rq_sems[2], t).wait_recv(), nx, x)
    rq_sum[...] = sum(rq_xland[t] for t in range(1, nx)) + rq_xland[0]
    others(lambda s: share(rq_sum, gq_hbm, rq_sems[3], s).start())
    own_gq = pltpu.make_async_copy(rq_sum, gq_hbm.at[me], store_sem.at[tiles])
    own_gq.start()

    lax.fori_loop(6, group, outputs_owner, 0)

    def by_position(b, _):
        block = o_rows[:, pl.ds(b * BLOCK, BLOCK), :]
        o_raw[pl.ds(b * BLOCK, BLOCK)] = jnp.swapaxes(block, 0, 1)
        return 0

    stores = []

    def store(t):
        blocks = TILE // BLOCK
        lax.fori_loop(t * blocks, (t + 1) * blocks, by_position, 0, unroll=4)
        rows = pl.ds(t * TILE, TILE)
        stores.append(pltpu.make_async_copy(o_raw.at[rows], out_hbm.at[rows], store_sem.at[t]))
        stores[-1].start()

    store(0)

    others(lambda s: arrival(rk_send, rk_land, rk_sems[0], s).wait_recv())
    rk_z[...] = sum(rk_land[s] for s in range(1, group)) + rk_land[0]
    others(lambda t: z_copy(rk_z, rk_zland, rk_sems[1], t).start(), nz, z)
    rk_zland[z] = rk_z[...]
    for t in range(1, tiles):
        store(t)
    others(lambda t: z_arrival(rk_z, rk_zland, rk_sems[1], t).wait_recv(), nz, z)
    rk_x[...] = sum(rk_zland[t] for t in range(1, nz)) + rk_zland[0]
    others(lambda t: x_copy(rk_x, rk_xland, rk_sems[2], t).start(), nx, x)
    rk_xland[x] = rk_x[...]
    others(lambda t: x_arrival(rk_x, rk_xland, rk_sems[2], t).wait_recv(), nx, x)
    rk_sum[...] = sum(rk_xland[t] for t in range(1, nx)) + rk_xland[0]
    others(lambda s: share(rk_sum, gk_hbm, rk_sems[3], s).start())
    own_gk = pltpu.make_async_copy(rk_sum, gk_hbm.at[me], store_sem.at[tiles + 1])
    own_gk.start()

    for copy in halo_copies:
        copy.wait_send()
    others(lambda s: scatter(p_send, p_land, p_sems[0], s).wait_send())
    others(lambda s: scatter(p_out, p_back, p_sems[2], s).wait_send())
    others(lambda s: scatter(s_send, s_land, s_sems[0], s).wait_send())
    others(lambda s: scatter(s_out, s_back, s_sems[2], s).wait_send())
    for t in range(nz):
        @pl.when(t > z)
        def _():
            z_copy(p_total, p_far, p_sems[1], t).wait_send()

        @pl.when(t < z)
        def _():
            z_copy(s_total, s_far, s_sems[1], t).wait_send()
    for send, land, zs, zland, xs, xland, total, grad, sems in (
        (rq_send, rq_land, rq_z, rq_zland, rq_x, rq_xland, rq_sum, gq_hbm, rq_sems),
        (rk_send, rk_land, rk_z, rk_zland, rk_x, rk_xland, rk_sum, gk_hbm, rk_sems),
    ):
        others(lambda s: scatter(send, land, sems[0], s).wait_send())
        others(lambda t: z_copy(zs, zland, sems[1], t).wait_send(), nz, z)
        others(lambda t: x_copy(xs, xland, sems[2], t).wait_send(), nx, x)
        others(lambda s: share(total, grad, sems[3], s).wait_send())
        others(lambda s: share_arrival(total, grad, sems[3], s).wait_recv())
    for copy in (*stores, own_gq, own_gk):
        copy.wait()


def finish(rows_hbm, gq_hbm, gk_hbm, out_hbm, gq_out, gk_out, rows, gq, gk, sems):
    parts = rows.shape[0] // TILE
    moves = [(gq_hbm, gq, gq_out), (gk_hbm, gk, gk_out)]
    for t in range(parts):
        span = pl.ds(t * TILE, TILE)
        moves.append((rows_hbm.at[span], rows.at[span], out_hbm.at[span]))
    ins = [pltpu.make_async_copy(a, b, sems.at[0, n]) for n, (a, b, _) in enumerate(moves)]
    outs = [pltpu.make_async_copy(b, c, sems.at[1, n]) for n, (_, b, c) in enumerate(moves)]
    for copy in ins:
        copy.start()
    for arrived, copy in zip(ins, outs):
        arrived.wait()
        copy.start()
    for copy in outs:
        copy.wait()


def body(queries, keys, values, keep_count, query_map, key_map, cotangent):
    _, tokens, heads, width = queries.shape
    rank = query_map.shape[2]
    tiles = tokens // TILE
    sizes = tuple(lax.axis_size(a) for a in (Z_AXIS, Y_AXIS, C_AXIS, X_AXIS))
    nz, ny, nc, nx = sizes
    group = ny * nc
    own = heads // group
    ext = tokens + TILE
    part = (own * rank, width)
    slab = (own * rank + 1, width)
    dma = pltpu.SemaphoreType.DMA

    def vmem(shape, dtype=F32):
        return pltpu.VMEM(shape, dtype)

    def sums():
        return [
            vmem((group, *part)), vmem((group, *part)), vmem(part), vmem((nz, *part)),
            vmem(part), vmem((nx, *part)), vmem(part),
        ]

    def scans():
        return [
            vmem((group, *slab)), vmem((group, *slab)), vmem(slab), vmem((nz, *slab)),
            vmem((group, *slab)), vmem((group, *slab)),
        ]

    raw = (tokens, heads, width)
    lane_rows = (heads, rank, tokens)
    small = [vmem((heads, nz * group * tiles), jnp.int32), *[vmem((heads, rank, width), BF16)] * 2]
    scratch = [
        *small, vmem(raw, BF16),
        *[vmem(raw, BF16)] * 4, vmem((2, TILE, heads, width), BF16),
        vmem((heads, tokens, width), BF16), vmem((heads, ext, width), BF16),
        vmem((heads, ext, width), BF16), vmem((heads, tokens, width), BF16),
        vmem((heads, tokens, width), BF16), vmem((heads, tiles, 2 * TILE, TILE), BF16),
        vmem(lane_rows), vmem(lane_rows), vmem((heads, rank, ext)), vmem((heads, rank, ext)),
        vmem((heads, 8, ext)), vmem((tiles + 1, heads, 8, TILE), jnp.int32),
        vmem((heads, tiles, rank, width)), vmem(lane_rows), vmem(lane_rows),
        vmem((heads, 8, tokens)), vmem((heads, 1, tokens)), vmem(lane_rows), vmem(lane_rows),
        vmem((heads, tiles, rank, width)), vmem((heads, tiles, rank, width)),
        vmem((heads, rank, width)), vmem(lane_rows),
        *scans(), *scans(), *sums(), *sums(), vmem(slab),
        dma((4 * tiles + 3,)), dma((tiles + 2,)), dma((2, len(HALO_PIECES))),
        [dma((2 * group,)), dma((2 * nz,)), dma((2 * group,))],
        [dma((2 * group,)), dma((2 * nz,)), dma((2 * group,))],
        [dma((2 * group,)), dma((2 * nz,)), dma((2 * nx,)), dma((2 * group,))],
        [dma((2 * group,)), dma((2 * nz,)), dma((2 * nx,)), dma((2 * group,))],
    ]
    anywhere = pl.BlockSpec(memory_space=pl.ANY)
    grad = jax.ShapeDtypeStruct((group, *part), F32)
    rows, grad_q, grad_k = pl.pallas_call(
        functools.partial(kernel, sizes),
        out_shape=(jax.ShapeDtypeStruct(raw, BF16), grad, grad),
        in_specs=[anywhere] * 7,
        out_specs=(anywhere,) * 3,
        scratch_shapes=scratch,
        compiler_params=pltpu.CompilerParams(
            collective_id=0, has_side_effects=True, vmem_limit_bytes=60 * 2**20
        ),
        name="less_step",
    )(
        queries[0], keys[0], values[0], cotangent[0], keep_count[0],
        query_map.transpose(0, 2, 1), key_map.transpose(0, 2, 1),
    )

    out, grad_q, grad_k = pl.pallas_call(
        finish,
        out_shape=(jax.ShapeDtypeStruct(raw, BF16), grad, grad),
        in_specs=[anywhere] * 3,
        out_specs=(anywhere,) * 3,
        scratch_shapes=[
            vmem(raw, BF16), vmem((group, *part)), vmem((group, *part)), dma((2, tiles + 2)),
        ],
        name="finish",
    )(rows, grad_q, grad_k)

    def map_grad(g):
        return g.reshape(heads, rank, width).transpose(0, 2, 1)

    return (out[None], map_grad(grad_q), map_grad(grad_k))


def solution(mesh):
    chips, last = mesh.shape["seq"], mesh.shape["batch"]
    torus = Mesh(mesh.devices.reshape(chips // 8, 4, 2, last), (*SEQ, X_AXIS))
    rows = P(X_AXIS, SEQ, None, None)
    return jax.shard_map(
        body,
        mesh=torus,
        in_specs=(rows, rows, rows, P(X_AXIS, None, None), P(), P(), rows),
        out_specs=(rows, P(), P()),
        check_vma=False,
    )
```

```python
import functools
import math

import jax
import jax.numpy as jnp
from jax import lax
from jax.experimental import pallas as pl
from jax.experimental.pallas import tpu as pltpu
from jax.sharding import Mesh
from jax.sharding import PartitionSpec as P

TILE = 128
SHIFT = 1.5
LOG2E = math.log2(math.e)
Z_AXIS, Y_AXIS, C_AXIS, X_AXIS = "seq_0", "seq_1", "seq_2", "batch"
SEQ = (Z_AXIS, Y_AXIS, C_AXIS)
F32, BF16 = jnp.float32, jnp.bfloat16
BLOCK = 16
HALO_PIECES = ((0, 0, 64), (0, 64, 64), (1, 0, 128))


def dot_nn(a, b):
    return lax.dot_general(a, b, (((1,), (0,)), ((), ())), preferred_element_type=F32)


def dot_nt(a, b):
    return lax.dot_general(a, b, (((1,), (1,)), ((), ())), preferred_element_type=F32)


def dot_tn(a, b):
    return lax.dot_general(a, b, (((0,), (0,)), ((), ())), preferred_element_type=F32)


def halves(x):
    high = x.astype(BF16).astype(F32)
    return high, x - high


def stacked(x):
    return jnp.concatenate(halves(x), 0).astype(BF16)


def folded(x):
    half = x.shape[0] // 2
    return x[:half] + x[half:]


def feature(pre):
    small = jnp.exp(-jnp.abs(pre))
    inverse = 1.0 / (1.0 + small)
    return jnp.maximum(pre, 0.0) + jnp.log1p(small), jnp.where(pre >= 0.0, inverse, small * inverse)


def remote(source, target, send, receive, device):
    return pltpu.make_async_remote_copy(
        src_ref=source,
        dst_ref=target,
        send_sem=send,
        recv_sem=receive,
        device_id=device,
        device_id_type=pl.DeviceIdType.MESH,
    )


def kernel(
    sizes,
    q_hbm, k_hbm, v_hbm, c_hbm, count_hbm, wq_hbm, wk_hbm,
    out_hbm, gq_hbm, gk_hbm,
    count_ref, wq_ref, wk_ref, o_raw,
    q_raw, k_raw, v_raw, c_raw, halo_raw,
    q_rows, k_rows, v_rows, c_rows, o_rows, weight_rows,
    feat_q, slope_q, feat_k, slope_k, kept_lane, count_lane,
    state_local, norm_local, u_local, row_data, inverse_rows, g_rows, gpre_q, d_state, d_norm, gk_local, far_rows,
    p_send, p_land, p_total, p_far, p_out, p_back,
    s_send, s_land, s_total, s_far, s_out, s_back,
    rq_send, rq_land, rq_z, rq_zland, rq_x, rq_xland, rq_sum,
    rk_send, rk_land, rk_z, rk_zland, rk_x, rk_xland, rk_sum,
    acc,
    load_sem, store_sem, halo_sems, p_sems, s_sems, rq_sems, rk_sems,
):
    nz, ny, nc, nx = sizes
    group = ny * nc
    devices = nz * group
    tokens, heads, width = q_raw.shape
    tiles = tokens // TILE
    own = heads // group
    lanes = lax.broadcasted_iota(jnp.int32, (8, TILE), 1)
    z, y, c, x = (lax.axis_index(a) for a in (Z_AXIS, Y_AXIS, C_AXIS, X_AXIS))
    me = y * nc + c
    index = z * group + me

    def peer(s):
        return {Y_AXIS: s // nc, C_AXIS: s % nc}

    def place(i):
        return {Z_AXIS: i // group, Y_AXIS: (i // nc) % ny, C_AXIS: i % nc}

    after = place((index + 1) % devices)
    before = place((index + devices - 1) % devices)

    barrier = pltpu.get_barrier_semaphore()

    def greet(device):
        pl.semaphore_signal(barrier, inc=1, device_id=device, device_id_type=pl.DeviceIdType.MESH)

    greet(after)
    greet(before)
    for k in range(1, group):
        greet(peer((me + k) % group))
    for k in range(1, nz):
        greet({Z_AXIS: (z + k) % nz})
    for k in range(1, nx):
        greet({X_AXIS: (x + k) % nx})

    sources = (k_hbm, v_hbm, c_hbm, q_hbm)
    raws = (k_raw, v_raw, c_raw, q_raw)

    def load(a, t):
        rows = pl.ds(t * TILE, TILE)
        return pltpu.make_async_copy(sources[a].at[rows], raws[a].at[rows], load_sem.at[a * tiles + t])

    small = [
        pltpu.make_async_copy(source, target, load_sem.at[4 * tiles + n])
        for n, (source, target) in enumerate(
            ((wk_hbm, wk_ref), (count_hbm, count_ref), (wq_hbm, wq_ref))
        )
    ]
    for a in range(4):
        for t in range(tiles):
            load(a, t).start()
        if a == 0:
            for copy in small:
                copy.start()

    def by_head(raw, rows, first, target, count):
        def step(b, _):
            block = raw[pl.ds(rows + b * BLOCK, BLOCK)]
            target[:, pl.ds(first + b * BLOCK, BLOCK), :] = jnp.swapaxes(block, 0, 1)
            return 0

        lax.fori_loop(0, count // BLOCK, step, 0, unroll=4)

    for t in range(tiles):
        load(0, t).wait()
        by_head(k_raw, t * TILE, (t + 1) * TILE, k_rows, TILE)
    pl.semaphore_wait(barrier, 2 + group - 1 + nz - 1 + nx - 1)
    halo_copies = []
    for n, (a, first, count) in enumerate(HALO_PIECES):
        source = (k_raw, v_raw)[a].at[pl.ds(tokens - TILE + first, count)]
        target = halo_raw.at[a, pl.ds(first, count)]
        halo_copies.append(remote(source, target, halo_sems.at[0, n], halo_sems.at[1, n], after))
    halo_copies[0].start()
    small[0].wait()

    def key_features(h, _):
        feat, slope = feature(dot_nt(wk_ref[h], k_rows[h, pl.ds(TILE, tokens), :]) - SHIFT)
        feat_k[h, :, TILE:] = feat
        slope_k[h, :, TILE:] = slope
        return 0

    lax.fori_loop(0, heads, key_features, 0, unroll=8)
    for t in range(tiles):
        load(1, t).wait()
        by_head(v_raw, t * TILE, (t + 1) * TILE, v_rows, TILE)

    for copy in small[1:]:
        copy.wait()
    counts = count_ref[...]
    which = lax.broadcasted_iota(jnp.int32, counts.shape, 1)
    lane16 = lax.broadcasted_iota(jnp.int32, (heads, TILE), 1)
    for e in range(tiles + 1):
        picked = jnp.sum(jnp.where(which == index * tiles + (e - 1), counts, 0), 1, keepdims=True)
        spread = jnp.broadcast_to(picked, (heads, TILE))
        kept = (lane16 < spread).astype(F32)
        for h in range(heads):
            count_lane[e, h] = jnp.broadcast_to(spread[h : h + 1], (8, TILE))
            kept_lane[h, :, e * TILE : (e + 1) * TILE] = jnp.broadcast_to(kept[h : h + 1], (8, TILE))

    def scatter(buffer, land, sems, s):
        return remote(buffer.at[s], land.at[me], sems.at[s], sems.at[group + me], peer(s))

    def arrival(buffer, land, sems, s):
        return remote(buffer.at[s], land.at[s], sems.at[s], sems.at[group + s], peer(s))

    def share(buffer, land, sems, s):
        return remote(buffer, land.at[me], sems.at[s], sems.at[group + me], peer(s))

    def share_arrival(buffer, land, sems, s):
        return remote(buffer, land.at[s], sems.at[s], sems.at[group + s], peer(s))

    def z_copy(buffer, land, sems, t):
        return remote(buffer, land.at[z], sems.at[t], sems.at[nz + z], {Z_AXIS: t})

    def z_arrival(buffer, land, sems, t):
        return remote(buffer, land.at[t], sems.at[t], sems.at[nz + t], {Z_AXIS: t})

    def x_copy(buffer, land, sems, t):
        return remote(buffer, land.at[x], sems.at[t], sems.at[nx + x], {X_AXIS: t})

    def x_arrival(buffer, land, sems, t):
        return remote(buffer, land.at[t], sems.at[t], sems.at[nx + t], {X_AXIS: t})

    def others(step, count=group, here=None):
        here = me if here is None else here
        for k in sorted(range(1, count), key=lambda k: -min(k, count - k)):
            step((here + k) % count)

    def nearer(k, steps):
        found = []
        for n in range(steps):
            n = k * steps + n
            found += [(me + group // 2 - n) % group, (me + group // 2 + 1 + n) % group]
        return found

    def by_owner(compute, buffer, land, sems, steps=1):
        def one(k, _):
            pair = nearer(k, steps)
            slices = [compute(o) for o in pair]
            for o, piece in zip(pair, slices):
                buffer[o] = piece
            for o in pair:
                @pl.when(o != me)
                def _():
                    scatter(buffer, land, sems, o).start()
            return 0

        lax.fori_loop(0, group // 2 // steps, one, 0)
        land[me] = buffer[me]

    at_lane = [
        (lanes == lax.broadcasted_iota(jnp.int32, (8, TILE), 0) + 8 * i).astype(F32)
        for i in range(own)
    ]

    def owner_slice(pieces, norms):
        spread = sum(norms[i] * at_lane[i] for i in range(1, own)) + norms[0] * at_lane[0]
        return jnp.concatenate([*pieces, jnp.sum(spread, 0, keepdims=True)], 0)

    def norm_of(row, i):
        picked = jnp.sum(row * at_lane[i], 1, keepdims=True)
        return jnp.broadcast_to(picked, (8, TILE))

    own_rows = pl.ds(TILE, tokens)

    def each_head(step, unroll=4):
        def one(h, _):
            step(h)
            return 0

        lax.fori_loop(0, heads, one, 0, unroll=unroll)

    def each_owner(step, ready):
        def one(k, _):
            pair = nearer(k, 2)
            for o in pair:
                pl.when(o != me)(functools.partial(ready, o))
            for o in pair:
                for i in range(own):
                    step(o, i)
            return 0

        lax.fori_loop(0, group // 4, one, 0)

    def state_slice(o):
        pieces, norms = [], []
        for i in range(own):
            h = o * own + i
            feat = feat_k[h, :, TILE:]
            pieces.append(folded(dot_nn(stacked(feat), v_rows[h, own_rows, :])))
            norms.append(jnp.sum(feat, 1, keepdims=True))
        return owner_slice(pieces, norms)

    by_owner(state_slice, p_send, p_land, p_sems[0], 2)
    for copy in halo_copies[1:]:
        copy.start()

    def query_features(h, _):
        feat, slope = feature(dot_nt(wq_ref[h], q_rows[h]) - SHIFT)
        feat_q[h] = feat
        slope_q[h] = slope
        return 0

    for t in range(tiles):
        load(2, t).wait()
        by_head(c_raw, t * TILE, t * TILE, c_rows, TILE)
        load(3, t).wait()
        by_head(q_raw, t * TILE, t * TILE, q_rows, TILE)
    lax.fori_loop(0, heads, query_features, 0, unroll=8)

    def keep_state(h, j, state, norm):
        state_local[h, j] = state
        norm_local[h, :, j * TILE : (j + 1) * TILE] = jnp.broadcast_to(norm, (8, TILE))

    def local_products(h, j):
        cols = slice(j * TILE, (j + 1) * TILE)
        u = folded(dot_nt(stacked(state_local[h, j]), c_rows[h, cols, :]))
        u_local[h, :, cols] = u
        fq = feat_q[h, :, cols]
        row_data[h, 3:4, cols] = jnp.sum(fq * norm_local[h, :, cols], 0, keepdims=True)
        row_data[h, 4:5, cols] = jnp.sum(fq * u, 0, keepdims=True)

    def local_states(h, _):
        span = slice(TILE, tiles * TILE)
        feat = feat_k[h, :, span]
        gone = feat * (1.0 - kept_lane[h, :, span])
        lines, norms = [], []
        for j in range(1, tiles):
            cut = (j - 1) * TILE
            pieces = [feat[:, :cut]] * (cut > 0) + [gone[:, cut : cut + TILE]]
            pieces += [jnp.zeros((8, (tiles - 1 - j) * TILE), F32)] * (j < tiles - 1)
            line = jnp.concatenate(pieces, 1)
            lines += halves(line)
            blocks = [line[:, i * TILE : (i + 1) * TILE] for i in range(j)]
            norms.append(jnp.sum(sum(blocks[1:], blocks[0]), 1, keepdims=True))
        result = dot_nn(jnp.concatenate(lines, 0).astype(BF16), v_rows[h, span, :])
        for j in range(1, tiles):
            keep_state(h, j, folded(result[(j - 1) * 16 : j * 16]), norms[j - 1])
        return 0

    scale2 = LOG2E / math.sqrt(width)
    key_at = lax.broadcasted_iota(jnp.int32, (TILE, TILE), 0)
    causal = key_at <= lax.broadcasted_iota(jnp.int32, (TILE, TILE), 1)

    def weigh(h, j):
        cols = slice(j * TILE, (j + 1) * TILE)
        scores = dot_nt(k_rows[h, j * TILE : (j + 2) * TILE, :], q_rows[h, cols, :])
        live = key_at < count_lane[j, h, 0:1, :]
        near = jnp.where(live, scores[:TILE], -1e30)
        here = jnp.where(causal, scores[TILE:], -1e30)
        top = jnp.maximum(jnp.max(near, 0, keepdims=True), jnp.max(here, 0, keepdims=True))
        shift = top * scale2
        weights = jnp.exp2(jnp.concatenate([near, here], 0) * scale2 - shift)
        rounded = weights.astype(BF16)
        weight_rows[h, j] = rounded
        row_data[h, 0:1, cols] = jnp.exp2(-shift)
        row_data[h, 1:2, cols] = jnp.sum(weights, 0, keepdims=True)
        return rounded

    def along(h, j, rounded):
        cols = slice(j * TILE, (j + 1) * TILE)
        product = dot_nt(v_rows[h, j * TILE : (j + 2) * TILE, :], c_rows[h, cols, :])
        row_data[h, 2:3, cols] = jnp.sum(rounded.astype(F32) * product, 0, keepdims=True)

    def sparse(h, j):
        along(h, j, weigh(h, j))

    def sparse_tile(j):
        def one(h, _):
            sparse(h, j)
            return 0

        lax.fori_loop(0, heads, one, 0, unroll=4)

    others(lambda s: arrival(p_send, p_land, p_sems[0], s).wait_recv())
    p_total[...] = sum(p_land[s] for s in range(1, group)) + p_land[0]
    for t in range(1, nz):
        @pl.when(t > z)
        def _():
            z_copy(p_total, p_far, p_sems[1], t).start()

    lax.fori_loop(0, heads, local_states, 0, unroll=8)
    each_head(lambda h: [local_products(h, j) for j in range(1, tiles)], 8)
    sparse_tile(1)
    sparse_tile(2)

    acc[...] = jnp.zeros_like(acc)
    for t in range(nz - 1):
        @pl.when(t < z)
        def _():
            z_arrival(p_total, p_far, p_sems[1], t).wait_recv()
            acc[...] += p_far[t]

    running = acc[...]
    for s in range(group):
        p_out[s] = running
        running = running + p_land[s]
    others(lambda s: scatter(p_out, p_back, p_sems[2], s).start())
    p_back[me] = p_out[me]

    sparse_tile(3)

    def halo_features(h):
        feat, slope = feature(dot_nt(wk_ref[h], k_rows[h, :TILE, :]) - SHIFT)
        slope_k[h, :, :TILE] = slope
        feat_k[h, :, :TILE] = feat * kept_lane[h, :, :TILE]

    def halo_state(h):
        held = feat_k[h, :, :TILE]
        state = folded(dot_nn(stacked(held), v_rows[h, :TILE, :]))
        keep_state(h, 0, -state, -jnp.sum(held, 1, keepdims=True))

    def halo_along(h):
        local_products(h, 0)
        along(h, 0, weight_rows[h, 0])

    for copy, (a, _, _) in zip(halo_copies, HALO_PIECES):
        if a == 0:
            copy.wait_recv()
    by_head(halo_raw.at[0], 0, 0, k_rows, TILE)
    each_head(halo_features, 8)
    each_head(lambda h: weigh(h, 0))
    for copy, (a, _, _) in zip(halo_copies, HALO_PIECES):
        if a == 1:
            copy.wait_recv()
    by_head(halo_raw.at[1], 0, 0, v_rows, TILE)
    each_head(halo_state, 16)
    each_head(halo_along, 8)

    def d_slice(o):
        pieces, norms = [], []
        back = p_back[o]
        for i in range(own):
            h = o * own + i
            far_norm = jnp.concatenate([norm_of(back[own * 8 :], i)] * tiles, 1)
            fq = feat_q[h]
            u_far = far_rows[h]
            decay = row_data[h, 0:1, :]
            kd = row_data[h, 3:4, :] + jnp.sum(fq * far_norm, 0, keepdims=True)
            cu = row_data[h, 4:5, :] + jnp.sum(fq * u_far, 0, keepdims=True)
            inverse = 1.0 / (row_data[h, 1:2, :] + decay * kd)
            share_of = decay * inverse
            g = fq * share_of
            g_den = -share_of * ((row_data[h, 2:3, :] + decay * cu) * inverse)
            g_rows[h] = g
            inverse_rows[h] = inverse
            gpre_q[h] = (
                share_of * (u_local[h] + u_far) + g_den * (norm_local[h] + far_norm)
            ) * slope_q[h]
            weighted = fq * g_den
            total, total_norm = None, None
            for j in range(tiles):
                cols = slice(j * TILE, (j + 1) * TILE)
                piece = folded(dot_nn(stacked(g[:, cols]), c_rows[h, cols, :]))
                norm = jnp.sum(weighted[:, cols], 1, keepdims=True)
                d_state[h, j] = piece
                d_norm[h, j] = jnp.broadcast_to(norm, (8, TILE))
                total = piece if j == 0 else total + piece
                total_norm = norm if j == 0 else total_norm + norm
            pieces.append(total)
            norms.append(total_norm)
        return owner_slice(pieces, norms)

    def far_products(o, i):
        far = p_back[o, i * 8 : (i + 1) * 8]
        far_rows[o * own + i] = folded(dot_nt(stacked(far), c_rows[o * own + i]))

    each_owner(far_products, lambda o: arrival(p_out, p_back, p_sems[2], o).wait_recv())
    by_owner(d_slice, s_send, s_land, s_sems[0], 2)

    def query_slice(o):
        pieces = []
        for i in range(own):
            h = o * own + i
            pieces.append(folded(dot_nn(stacked(gpre_q[h]), q_rows[h])))
        return jnp.concatenate(pieces, 0)

    by_owner(query_slice, rq_send, rq_land, rq_sems[0], 2)

    def key_local(h):
        parts = []
        for e in range(tiles):
            cols = slice(e * TILE, (e + 1) * TILE)
            v_tile = v_rows[h, cols, :]
            kept = kept_lane[h, :, cols]
            if e == 0:
                grad = -kept * (folded(dot_nt(stacked(d_state[h, 0]), v_tile)) + d_norm[h, 0])
            else:
                near, near_norm = d_state[h, e], d_norm[h, e]
                if e + 1 < tiles:
                    full = sum([d_state[h, j] for j in range(e + 2, tiles)], d_state[h, e + 1])
                    full_norm = sum([d_norm[h, j] for j in range(e + 2, tiles)], d_norm[h, e + 1])
                    both = jnp.concatenate([*halves(near), *halves(full)], 0).astype(BF16)
                    result = dot_nt(both, v_tile)
                    grad = (1.0 - kept) * (folded(result[:16]) + near_norm)
                    grad = grad + (folded(result[16:]) + full_norm)
                else:
                    grad = (1.0 - kept) * (folded(dot_nt(stacked(near), v_tile)) + near_norm)
            parts.append(grad * slope_k[h, :, cols])
        far_rows[h] = jnp.concatenate(parts, 1)

    def key_gradient(h):
        gk_local[h] = folded(dot_nn(stacked(far_rows[h]), k_rows[h, :tokens, :]))

    sub = lax.broadcasted_iota(jnp.int32, (8, TILE), 0)

    def outputs(h, o, i):
        back = p_back[o]
        far = back[i * 8 : (i + 1) * 8]
        for j in range(tiles):
            cols = slice(j * TILE, (j + 1) * TILE)
            high, low = halves(far + state_local[h, j])
            g_high, g_low = halves(g_rows[h, :, cols])
            first, rest = halves(inverse_rows[h, :, cols])
            second, third = halves(rest)
            inverse = jnp.where(sub == 0, first, jnp.where(sub == 1, second, third))
            inverse = jnp.where(sub < 3, inverse, 0.0)
            left = jnp.concatenate([g_high, g_low, g_high, inverse], 0).astype(BF16)
            zeros, ones = jnp.zeros((8, TILE), F32), jnp.ones((8, TILE), F32)
            right = jnp.concatenate(
                [
                    jnp.concatenate([high, high, low, zeros], 0),
                    jnp.concatenate([zeros, zeros, zeros, ones], 0),
                ],
                1,
            ).astype(BF16)
            both = dot_tn(left, right)
            window = slice(j * TILE, (j + 2) * TILE)
            numer = dot_tn(weight_rows[h, j], v_rows[h, window, :])
            result = numer * both[:, TILE:] + both[:, :TILE]
            o_rows[h, cols, :] = result.astype(BF16)

    def outputs_owner(o, _):
        for i in range(own):
            outputs(o * own + i, o, i)
        return 0

    each_head(key_local, 8)
    each_head(key_gradient, 8)

    others(lambda s: arrival(s_send, s_land, s_sems[0], s).wait_recv())
    s_total[...] = sum(s_land[s] for s in range(1, group)) + s_land[0]
    for t in range(nz - 1):
        @pl.when(t < z)
        def _():
            z_copy(s_total, s_far, s_sems[1], t).start()

    others(lambda s: arrival(rq_send, rq_land, rq_sems[0], s).wait_recv())
    rq_z[...] = sum(rq_land[s] for s in range(1, group)) + rq_land[0]

    lax.fori_loop(0, 4, outputs_owner, 0)

    acc[...] = jnp.zeros_like(acc)
    for t in range(1, nz):
        @pl.when(t > z)
        def _():
            z_arrival(s_total, s_far, s_sems[1], t).wait_recv()
            acc[...] += s_far[t]

    running = acc[...]
    for s in reversed(range(group)):
        s_out[s] = running
        running = running + s_land[s]
    others(lambda s: scatter(s_out, s_back, s_sems[2], s).start())
    s_back[me] = s_out[me]
    others(lambda t: z_copy(rq_z, rq_zland, rq_sems[1], t).start(), nz, z)
    rq_zland[z] = rq_z[...]


    lax.fori_loop(4, 6, outputs_owner, 0)

    def key_products(o, i):
        h = o * own + i
        back = s_back[o]
        far_norm = jnp.concatenate([norm_of(back[own * 8 :], i)] * tiles, 1)
        grad = folded(dot_nt(stacked(back[i * 8 : (i + 1) * 8]), v_rows[h, own_rows, :]))
        far_rows[h] = (grad + far_norm) * slope_k[h, :, TILE:]

    def key_slice(o):
        pieces = []
        for i in range(own):
            h = o * own + i
            pieces.append(gk_local[h] + folded(dot_nn(stacked(far_rows[h]), k_rows[h, own_rows, :])))
        return jnp.concatenate(pieces, 0)

    each_owner(key_products, lambda o: arrival(s_out, s_back, s_sems[2], o).wait_recv())
    by_owner(key_slice, rk_send, rk_land, rk_sems[0], 2)
    others(lambda t: z_arrival(rq_z, rq_zland, rq_sems[1], t).wait_recv(), nz, z)
    rq_x[...] = sum(rq_zland[t] for t in range(1, nz)) + rq_zland[0]
    others(lambda t: x_copy(rq_x, rq_xland, rq_sems[2], t).start(), nx, x)
    rq_xland[x] = rq_x[...]


    lax.fori_loop(6, group, outputs_owner, 0)

    def by_position(b, _):
        block = o_rows[:, pl.ds(b * BLOCK, BLOCK), :]
        o_raw[pl.ds(b * BLOCK, BLOCK)] = jnp.swapaxes(block, 0, 1)
        return 0

    stores = []

    def store(t):
        blocks = TILE // BLOCK
        lax.fori_loop(t * blocks, (t + 1) * blocks, by_position, 0, unroll=4)
        rows = pl.ds(t * TILE, TILE)
        stores.append(pltpu.make_async_copy(o_raw.at[rows], out_hbm.at[rows], store_sem.at[t]))
        stores[-1].start()

    store(0)

    others(lambda s: arrival(rk_send, rk_land, rk_sems[0], s).wait_recv())
    rk_z[...] = sum(rk_land[s] for s in range(1, group)) + rk_land[0]
    others(lambda t: z_copy(rk_z, rk_zland, rk_sems[1], t).start(), nz, z)
    rk_zland[z] = rk_z[...]
    others(lambda t: x_arrival(rq_x, rq_xland, rq_sems[2], t).wait_recv(), nx, x)
    rq_sum[...] = sum(rq_xland[t] for t in range(1, nx)) + rq_xland[0]
    others(lambda s: share(rq_sum, gq_hbm, rq_sems[3], s).start())
    own_gq = pltpu.make_async_copy(rq_sum, gq_hbm.at[me], store_sem.at[tiles])
    own_gq.start()
    for t in range(1, tiles):
        store(t)
    others(lambda t: z_arrival(rk_z, rk_zland, rk_sems[1], t).wait_recv(), nz, z)
    rk_x[...] = sum(rk_zland[t] for t in range(1, nz)) + rk_zland[0]
    others(lambda t: x_copy(rk_x, rk_xland, rk_sems[2], t).start(), nx, x)
    rk_xland[x] = rk_x[...]
    others(lambda t: x_arrival(rk_x, rk_xland, rk_sems[2], t).wait_recv(), nx, x)
    rk_sum[...] = sum(rk_xland[t] for t in range(1, nx)) + rk_xland[0]
    others(lambda s: share(rk_sum, gk_hbm, rk_sems[3], s).start())
    own_gk = pltpu.make_async_copy(rk_sum, gk_hbm.at[me], store_sem.at[tiles + 1])
    own_gk.start()

    for copy in halo_copies:
        copy.wait_send()
    others(lambda s: scatter(p_send, p_land, p_sems[0], s).wait_send())
    others(lambda s: scatter(p_out, p_back, p_sems[2], s).wait_send())
    others(lambda s: scatter(s_send, s_land, s_sems[0], s).wait_send())
    others(lambda s: scatter(s_out, s_back, s_sems[2], s).wait_send())
    for t in range(nz):
        @pl.when(t > z)
        def _():
            z_copy(p_total, p_far, p_sems[1], t).wait_send()

        @pl.when(t < z)
        def _():
            z_copy(s_total, s_far, s_sems[1], t).wait_send()
    for send, land, zs, zland, xs, xland, total, grad, sems in (
        (rq_send, rq_land, rq_z, rq_zland, rq_x, rq_xland, rq_sum, gq_hbm, rq_sems),
        (rk_send, rk_land, rk_z, rk_zland, rk_x, rk_xland, rk_sum, gk_hbm, rk_sems),
    ):
        others(lambda s: scatter(send, land, sems[0], s).wait_send())
        others(lambda t: z_copy(zs, zland, sems[1], t).wait_send(), nz, z)
        others(lambda t: x_copy(xs, xland, sems[2], t).wait_send(), nx, x)
        others(lambda s: share(total, grad, sems[3], s).wait_send())
        others(lambda s: share_arrival(total, grad, sems[3], s).wait_recv())
    for copy in (*stores, own_gq, own_gk):
        copy.wait()


def finish(rows_hbm, gq_hbm, gk_hbm, out_hbm, gq_out, gk_out, rows, gq, gk, sems):
    parts = rows.shape[0] // TILE
    moves = [(gq_hbm, gq, gq_out), (gk_hbm, gk, gk_out)]
    for t in range(parts):
        span = pl.ds(t * TILE, TILE)
        moves.append((rows_hbm.at[span], rows.at[span], out_hbm.at[span]))
    ins = [pltpu.make_async_copy(a, b, sems.at[0, n]) for n, (a, b, _) in enumerate(moves)]
    outs = [pltpu.make_async_copy(b, c, sems.at[1, n]) for n, (_, b, c) in enumerate(moves)]
    for copy in ins:
        copy.start()
    for arrived, copy in zip(ins, outs):
        arrived.wait()
        copy.start()
    for copy in outs:
        copy.wait()


def body(queries, keys, values, keep_count, query_map, key_map, cotangent):
    _, tokens, heads, width = queries.shape
    rank = query_map.shape[2]
    tiles = tokens // TILE
    sizes = tuple(lax.axis_size(a) for a in (Z_AXIS, Y_AXIS, C_AXIS, X_AXIS))
    nz, ny, nc, nx = sizes
    group = ny * nc
    own = heads // group
    ext = tokens + TILE
    part = (own * rank, width)
    slab = (own * rank + 1, width)
    dma = pltpu.SemaphoreType.DMA

    def vmem(shape, dtype=F32):
        return pltpu.VMEM(shape, dtype)

    def sums():
        return [
            vmem((group, *part)), vmem((group, *part)), vmem(part), vmem((nz, *part)),
            vmem(part), vmem((nx, *part)), vmem(part),
        ]

    def scans():
        return [
            vmem((group, *slab)), vmem((group, *slab)), vmem(slab), vmem((nz, *slab)),
            vmem((group, *slab)), vmem((group, *slab)),
        ]

    raw = (tokens, heads, width)
    lane_rows = (heads, rank, tokens)
    small = [vmem((heads, nz * group * tiles), jnp.int32), *[vmem((heads, rank, width), BF16)] * 2]
    scratch = [
        *small, vmem(raw, BF16),
        *[vmem(raw, BF16)] * 4, vmem((2, TILE, heads, width), BF16),
        vmem((heads, tokens, width), BF16), vmem((heads, ext, width), BF16),
        vmem((heads, ext, width), BF16), vmem((heads, tokens, width), BF16),
        vmem((heads, tokens, width), BF16), vmem((heads, tiles, 2 * TILE, TILE), BF16),
        vmem(lane_rows), vmem(lane_rows), vmem((heads, rank, ext)), vmem((heads, rank, ext)),
        vmem((heads, 8, ext)), vmem((tiles + 1, heads, 8, TILE), jnp.int32),
        vmem((heads, tiles, rank, width)), vmem(lane_rows), vmem(lane_rows),
        vmem((heads, 8, tokens)), vmem((heads, 1, tokens)), vmem(lane_rows), vmem(lane_rows),
        vmem((heads, tiles, rank, width)), vmem((heads, tiles, rank, width)),
        vmem((heads, rank, width)), vmem(lane_rows),
        *scans(), *scans(), *sums(), *sums(), vmem(slab),
        dma((4 * tiles + 3,)), dma((tiles + 2,)), dma((2, len(HALO_PIECES))),
        [dma((2 * group,)), dma((2 * nz,)), dma((2 * group,))],
        [dma((2 * group,)), dma((2 * nz,)), dma((2 * group,))],
        [dma((2 * group,)), dma((2 * nz,)), dma((2 * nx,)), dma((2 * group,))],
        [dma((2 * group,)), dma((2 * nz,)), dma((2 * nx,)), dma((2 * group,))],
    ]
    anywhere = pl.BlockSpec(memory_space=pl.ANY)
    grad = jax.ShapeDtypeStruct((group, *part), F32)
    rows, grad_q, grad_k = pl.pallas_call(
        functools.partial(kernel, sizes),
        out_shape=(jax.ShapeDtypeStruct(raw, BF16), grad, grad),
        in_specs=[anywhere] * 7,
        out_specs=(anywhere,) * 3,
        scratch_shapes=scratch,
        compiler_params=pltpu.CompilerParams(
            collective_id=0, has_side_effects=True, vmem_limit_bytes=60 * 2**20
        ),
        name="less_step",
    )(
        queries[0], keys[0], values[0], cotangent[0], keep_count[0],
        query_map.transpose(0, 2, 1), key_map.transpose(0, 2, 1),
    )

    out, grad_q, grad_k = pl.pallas_call(
        finish,
        out_shape=(jax.ShapeDtypeStruct(raw, BF16), grad, grad),
        in_specs=[anywhere] * 3,
        out_specs=(anywhere,) * 3,
        scratch_shapes=[
            vmem(raw, BF16), vmem((group, *part)), vmem((group, *part)), dma((2, tiles + 2)),
        ],
        name="finish",
    )(rows, grad_q, grad_k)

    def map_grad(g):
        return g.reshape(heads, rank, width).transpose(0, 2, 1)

    return (out[None], map_grad(grad_q), map_grad(grad_k))


def solution(mesh):
    chips, last = mesh.shape["seq"], mesh.shape["batch"]
    torus = Mesh(mesh.devices.reshape(chips // 8, 4, 2, last), (*SEQ, X_AXIS))
    rows = P(X_AXIS, SEQ, None, None)
    return jax.shard_map(
        body,
        mesh=torus,
        in_specs=(rows, rows, rows, P(X_AXIS, None, None), P(), P(), rows),
        out_specs=(rows, P(), P()),
        check_vma=False,
    )
```
